32 devices in a mesh: dp: 4 (over x, core), seq: 8 (over z, y).
Axes of the slice: x: 2, y: 2, z: 4, core: 2. Of those that a mesh axis runs over, the one named last changes fastest.
Arguments:
- tokens: bfloat16 [4, 1024, 768], P('dp', 'seq'), may hold values from -6 to 6
- lengths: int32 [4], P('dp'), may hold values from 256 to 1024, as said below
- qkv_weight: bfloat16 [2, 442368], P(None, ('dp', 'seq')), may hold values from -0.4375 to 0.4375
- out_weight: bfloat16 [2, 589824], P(None, ('dp', 'seq')), may hold values from -2.5 to 2.5
- up_weight: bfloat16 [2, 589824], P(None, ('dp', 'seq')), may hold values from -0.4375 to 0.4375
- down_weight: bfloat16 [2, 589824], P(None, ('dp', 'seq')), may hold values from -0.21875 to 0.21875
- norm_gain: bfloat16 [2, 1536], P(None, ('dp', 'seq')), may hold values from 0.5 to 1.5
- norm_shift: bfloat16 [2, 1536], P(None, ('dp', 'seq')), may hold values from -1.5 to 1.5
- cotangent: bfloat16 [4, 1024, 768], P('dp', 'seq'), may hold values from -6 to 6
Outputs:
- mixed: bfloat16 [4, 1024, 768], P('dp', 'seq')
- tokens_grad: bfloat16 [4, 1024, 768], P('dp', 'seq')
- qkv_grad: float32 [2, 442368], P(None, ('dp', 'seq'))
- out_grad: float32 [2, 589824], P(None, ('dp', 'seq'))
- up_grad: float32 [2, 589824], P(None, ('dp', 'seq'))
- down_grad: float32 [2, 589824], P(None, ('dp', 'seq'))
- gain_grad: float32 [2, 1536], P(None, ('dp', 'seq'))
- shift_grad: float32 [2, 1536], P(None, ('dp', 'seq'))
The draws below stay inside these ranges and needn't reach their ends.
Inputs may be any that keep to these rules, and one draw needn't show every extreme that they name: `lengths`: valid slots of each sequence, counted from its first slot; in every draw some sequence fills all 1024 slots and some has exactly a quarter of them.
All inputs are finite; a program needn't handle non-finite values.
Results may differ from the reference program's by a relative error of at most 0.025.
Values may be sent and summed in bfloat16 or wider, within the bound.
A program may use at most 128 MiB of HBM per device.

```python
import jax
import jax.numpy as jnp
from jax import lax

D = 768
HEADS = 12
HEAD = 64
FF = 3072
GROUPS = 4
LAYERS = 2
SLOTS = 1024
BATCH = 4


def draw_lengths(key, part):
    key_values = jax.random.fold_in(key, 11)
    key_order = jax.random.fold_in(key, 12)
    values = jax.random.randint(key_values, (BATCH,), SLOTS // 4, SLOTS + 1)
    order = jax.random.permutation(key_order, BATCH)
    values = values.at[order[0]].set(SLOTS)
    values = values.at[order[1]].set(SLOTS // 4)
    return values.astype(jnp.int32)


def level_of(rng, shape, cuts, low, top_value):
    def one(dim, blocks):
        heights = jax.random.uniform(jax.random.fold_in(jax.random.fold_in(rng, 6), dim), (blocks,), jnp.float32, low / len(cuts), top_value / len(cuts))
        return jnp.repeat(jnp.exp(heights), shape[dim] // blocks).reshape((-1,) + (1,) * (len(shape) - dim - 1))

    loudness = one(*cuts[0])
    for cut in cuts[1:]:
        loudness = loudness * one(*cut)
    return loudness


def normal_values(stream_key, shape, deviation, limit, cuts=(), kind=jnp.bfloat16):
    values = deviation * jax.random.normal(stream_key, shape, jnp.float32)
    if cuts:
        values = values * level_of(stream_key, shape, cuts, -0.22, 0.18)
    return jnp.clip(values, -limit, limit).astype(kind)


def setup_inputs(seed: int = 0) -> dict:
    arg_keys = jax.random.split(jax.random.key(seed), 10)
    return {
        "tokens": normal_values(arg_keys[0], (BATCH, SLOTS, D), 1.0, 6.0, ((0, 4), (1, 8))),
        "lengths": draw_lengths(jax.random.fold_in(arg_keys[9], 71), 0),
        "qkv_weight": normal_values(arg_keys[2], (LAYERS, 3 * D * D // GROUPS), (D // GROUPS) ** -0.5, 0.4375, ((1, 32),)),
        "out_weight": normal_values(arg_keys[3], (LAYERS, D * D), (max(1, D * 8 // SLOTS)) ** -0.5, 2.5, ((1, 32),)),
        "up_weight": normal_values(arg_keys[4], (LAYERS, D * FF // GROUPS), (D // GROUPS) ** -0.5, 0.4375, ((1, 32),)),
        "down_weight": normal_values(arg_keys[5], (LAYERS, FF * D // GROUPS), (FF // GROUPS) ** -0.5, 0.21875, ((1, 32),)),
        "norm_gain": jnp.clip(1.0 + 0.1 * jax.random.normal(arg_keys[6], (LAYERS, 2 * D), jnp.float32), 0.5, 1.5).astype(jnp.bfloat16),
        "norm_shift": normal_values(arg_keys[7], (LAYERS, 2 * D), 0.3, 1.5, ((1, 32),)),
        "cotangent": normal_values(arg_keys[8], (BATCH, SLOTS, D), 1.0, 6.0, ((0, 4), (1, 8))),
    }


EPSILON = 1e-06

@jax.custom_vjp
def low(v):
    return lax.optimization_barrier(v.astype(jnp.bfloat16)).astype(jnp.float32)

@jax.custom_vjp
def low_back(v):
    return v

def low_keep(v):
    return (low(v), None)

def low_pass(kept, grad):
    return (grad,)

def back_keep(v):
    return (v, None)

def back_low(kept, grad):
    return (low(grad),)
low.defvjp(low_keep, low_pass)
low_back.defvjp(back_keep, back_low)

def rounded_both(value):
    return low(low_back(value))

def grouped(inputs, weight):
    count = inputs.shape[0]
    shaped = inputs.reshape(count, weight.shape[0], -1)
    result = jnp.einsum('tgi,gio->tgo', shaped, weight, precision=lax.Precision.HIGHEST)
    return result.reshape(count, -1)

def normalize(values, gain, shift):
    center = values - lax.optimization_barrier(jnp.mean(values, axis=-1, keepdims=True))
    spread = lax.optimization_barrier(jnp.mean(center * center, axis=-1, keepdims=True))
    return center * lax.rsqrt(spread + EPSILON) * gain + shift

def attention(queries, keys, values, length):
    slots = keys.shape[0]
    block = min(512, slots)
    scaling = HEAD ** (-0.5)
    heads_key = keys.reshape(slots, HEADS, HEAD).transpose(1, 0, 2)
    heads_value = values.reshape(slots, HEADS, HEAD).transpose(1, 0, 2)
    key_ok = jnp.arange(slots, dtype=jnp.int32) < length

    def one_block(query_block):
        heads_query = query_block.reshape(block, HEADS, HEAD).transpose(1, 0, 2)
        scores = jnp.einsum('hqd,hkd->hqk', heads_query, heads_key, precision=lax.Precision.HIGHEST) * scaling
        scores = low_back(jnp.where(key_ok[None, None, :], scores, -1e+30))
        probs = low(jax.nn.softmax(scores, axis=-1))
        result = jnp.einsum('hqk,hkd->hqd', probs, heads_value, precision=lax.Precision.HIGHEST)
        return result.transpose(1, 0, 2).reshape(block, HEADS * HEAD)
    blocks = queries.reshape(slots // block, block, -1)
    return lax.map(jax.checkpoint(one_block), blocks).reshape(slots, -1)

def layer_forward(hidden, length, qkv_flat, out_flat, up_flat, down_flat, gain_flat, shift_flat):
    part = D // GROUPS
    part_ff = FF // GROUPS
    inputs_low = low(hidden)
    project = qkv_flat.reshape(3, GROUPS, part, part)
    queries = rounded_both(grouped(inputs_low, project[0]))
    keys = rounded_both(grouped(inputs_low, project[1]))
    values = rounded_both(grouped(inputs_low, project[2]))
    attended = rounded_both(attention(queries, keys, values, length))
    branch = low_back(jnp.dot(attended, out_flat.reshape(D, D), precision=lax.Precision.HIGHEST))
    gains = gain_flat.reshape(2, D)
    shifts = shift_flat.reshape(2, D)
    middle = low(normalize(inputs_low + branch, gains[0], shifts[0]))
    expanded = low_back(grouped(middle, up_flat.reshape(GROUPS, part, part_ff)))
    activated = low(jax.nn.gelu(expanded, approximate=False))
    shrunk = low_back(grouped(activated, down_flat.reshape(GROUPS, part_ff, part)))
    return normalize(middle + shrunk, gains[1], shifts[1])

def reference(tokens, lengths, qkv_weight, out_weight, up_weight, down_weight, norm_gain, norm_shift, cotangent):
    weights = tuple((array.astype(jnp.float32) for array in (qkv_weight, out_weight, up_weight, down_weight, norm_gain, norm_shift)))

    def network(sequence_in, length, params):
        hidden = sequence_in
        for layer_index in range(LAYERS):
            hidden = layer_forward(hidden, length, *(array[layer_index] for array in params))
        return hidden

    def one_sequence(totals, inputs_now):
        sequence, length, grad_out = inputs_now
        row_mask = (jnp.arange(SLOTS, dtype=jnp.int32) < length).astype(jnp.float32)
        output, pullback = jax.vjp(lambda sequence_in, params: network(sequence_in, length, params), sequence, weights)
        sequence_grad, param_grads = pullback(grad_out * row_mask[:, None])
        totals = tuple((summed + extra for summed, extra in zip(totals, param_grads)))
        return (totals, (output.astype(jnp.bfloat16), sequence_grad.astype(jnp.bfloat16)))
    zeros = tuple((jnp.zeros_like(array) for array in weights))
    totals, outputs = lax.scan(one_sequence, zeros, (tokens.astype(jnp.float32), lengths, cotangent.astype(jnp.float32)))
    mixed, tokens_grad = outputs
    return (mixed, tokens_grad, totals[0], totals[1], totals[2], totals[3], totals[4], totals[5])
```

```python
import types
from functools import partial

import jax
import jax.numpy as jnp
from jax import lax
from jax.experimental import pallas as pl
from jax.experimental.pallas import tpu as pltpu
from jax.sharding import PartitionSpec as P

D = 768
HEADS = 12
HEAD = 64
FF = 3072
GROUPS = 4


EPSILON = 1e-06


def grouped(inputs, weight):
    count = inputs.shape[0]
    shaped = inputs.reshape(count, weight.shape[0], -1)
    result = jnp.einsum("tgi,gio->tgo", shaped, weight, preferred_element_type=jnp.float32)
    return result.reshape(count, -1)


def normalize(values, gain, shift):
    center = values - jnp.mean(values, axis=-1, keepdims=True)
    factor = lax.rsqrt(jnp.mean(center * center, axis=-1, keepdims=True) + EPSILON)
    scaled = center * factor
    return (scaled * gain + shift, scaled, factor)


def normalize_back(grad_out, scaled, factor, gain):
    weighted = grad_out * gain
    grad_in = factor * (
        weighted
        - jnp.mean(weighted, axis=-1, keepdims=True)
        - scaled * jnp.mean(weighted * scaled, axis=-1, keepdims=True)
    )
    return (grad_in, jnp.sum(grad_out * scaled, axis=0), jnp.sum(grad_out, axis=0))


def unpack(pieces):
    qkv_flat, out_flat, up_flat, down_flat, gain_flat, shift_flat = pieces
    part = D // GROUPS
    part_ff = FF // GROUPS
    return (
        qkv_flat.reshape(3, GROUPS, part, part),
        out_flat.reshape(D, D),
        up_flat.reshape(GROUPS, part, part_ff),
        down_flat.reshape(GROUPS, part_ff, part),
        gain_flat.reshape(2, D).astype(jnp.float32),
        shift_flat.reshape(2, D).astype(jnp.float32),
    )


def project_heads(rows, matrices):
    total_rows = rows.shape[0]
    part = D // GROUPS
    result = jnp.einsum(
        "tgi,cgio->ctgo",
        rows.reshape(total_rows, GROUPS, part),
        matrices,
        preferred_element_type=jnp.float32,
    ).astype(jnp.bfloat16)
    return result.reshape(matrices.shape[0], total_rows, HEADS, HEAD).transpose(0, 2, 1, 3)


def head_forward(key_ok, scaling, pieces):
    query_head, key_head, value_head = pieces
    scores = (
        jnp.einsum("td,sd->ts", query_head, key_head, preferred_element_type=jnp.float32) * scaling
    )
    scores = jnp.where(key_ok[None, :], scores, -1e30)
    largest = jnp.max(scores, axis=-1, keepdims=True)
    powers = jnp.exp(scores - largest)
    total = jnp.sum(powers, axis=-1, keepdims=True)
    probs = (powers / total).astype(jnp.bfloat16)
    result = jnp.dot(probs, value_head, preferred_element_type=jnp.float32)
    return (result, (largest + jnp.log(total))[:, 0])


def head_backward(key_ok, scaling, pieces):
    query_head, key_head, value_head, grad_head, log_total = pieces
    scores = (
        jnp.einsum("td,sd->ts", query_head, key_head, preferred_element_type=jnp.float32) * scaling
    )
    scores = jnp.where(key_ok[None, :], scores, -1e30)
    probs = jnp.exp(scores - log_total[:, None])
    grad_probs = jnp.einsum("td,sd->ts", grad_head, value_head, preferred_element_type=jnp.float32)
    delta_row = jnp.sum(probs * grad_probs, axis=-1, keepdims=True)
    grad_scores = (probs * (grad_probs - delta_row)).astype(jnp.bfloat16)
    grad_query = jnp.dot(grad_scores, key_head, preferred_element_type=jnp.float32) * scaling
    grad_key = (
        jnp.einsum("ts,td->sd", grad_scores, query_head, preferred_element_type=jnp.float32)
        * scaling
    )
    grad_value = jnp.einsum(
        "ts,td->sd", probs.astype(jnp.bfloat16), grad_head, preferred_element_type=jnp.float32
    )
    return (grad_query, grad_key, grad_value)


def per_device(
    tokens,
    lengths,
    qkv_weight,
    out_weight,
    up_weight,
    down_weight,
    norm_gain,
    norm_shift,
    cotangent,
):
    layers = qkv_weight.shape[0]
    count = tokens.shape[1]
    slots = count * lax.axis_size("seq")
    first_slot = lax.axis_index("seq") * count
    length = lengths[0]
    key_ok = jnp.arange(slots, dtype=jnp.int32) < length
    row_ok = first_slot + jnp.arange(count, dtype=jnp.int32) < length
    scaling = HEAD ** (-0.5)
    part = D // GROUPS
    part_ff = FF // GROUPS
    hidden_low = tokens[0]
    saved = []
    for layer_index in range(layers):
        gathered = (
            lax.all_gather(qkv_weight[layer_index], ("dp", "seq"), axis=0, tiled=True),
            lax.all_gather(out_weight[layer_index], ("dp", "seq"), axis=0, tiled=True),
            lax.all_gather(up_weight[layer_index], ("dp", "seq"), axis=0, tiled=True),
            lax.all_gather(down_weight[layer_index], ("dp", "seq"), axis=0, tiled=True),
            lax.all_gather(norm_gain[layer_index], ("dp", "seq"), axis=0, tiled=True),
            lax.all_gather(norm_shift[layer_index], ("dp", "seq"), axis=0, tiled=True),
        )
        project, out_matrix, up_matrix, down_matrix, gains, shifts = unpack(gathered)
        heads = project_heads(hidden_low, project)
        key_all, value_all = (
            lax.all_gather(heads[1], "seq", axis=1, tiled=True),
            lax.all_gather(heads[2], "seq", axis=1, tiled=True),
        )
        attended, log_total = lax.map(
            partial(head_forward, key_ok, scaling), (heads[0], key_all, value_all)
        )
        attended_low = attended.transpose(1, 0, 2).reshape(count, D).astype(jnp.bfloat16)
        branch = jnp.dot(attended_low, out_matrix, preferred_element_type=jnp.float32)
        middle, scaled_one, factor_one = normalize(
            hidden_low.astype(jnp.float32) + branch, gains[0], shifts[0]
        )
        middle_low = middle.astype(jnp.bfloat16)
        expanded = grouped(middle_low, up_matrix)
        activated = jax.nn.gelu(expanded, approximate=False).astype(jnp.bfloat16)
        shrunk = grouped(activated, down_matrix)
        output, scaled_two, factor_two = normalize(
            middle_low.astype(jnp.float32) + shrunk, gains[1], shifts[1]
        )
        kept = None
        saved.append(
            (
                hidden_low,
                heads,
                log_total,
                attended_low,
                middle_low,
                expanded,
                activated,
                scaled_one,
                factor_one,
                scaled_two,
                factor_two,
                kept,
            )
        )
        hidden_low = output.astype(jnp.bfloat16)
    mixed = hidden_low[None]
    grad_hidden = cotangent[0].astype(jnp.float32) * row_ok[:, None].astype(jnp.float32)
    owned_list = []
    for layer_index in reversed(range(layers)):
        (
            inputs_low,
            heads,
            log_total,
            attended_low,
            middle_low,
            expanded,
            activated,
            scaled_one,
            factor_one,
            scaled_two,
            factor_two,
            kept,
        ) = saved[layer_index]
        gathered = (
            lax.all_gather(qkv_weight[layer_index], ("dp", "seq"), axis=0, tiled=True),
            lax.all_gather(out_weight[layer_index], ("dp", "seq"), axis=0, tiled=True),
            lax.all_gather(up_weight[layer_index], ("dp", "seq"), axis=0, tiled=True),
            lax.all_gather(down_weight[layer_index], ("dp", "seq"), axis=0, tiled=True),
            lax.all_gather(norm_gain[layer_index], ("dp", "seq"), axis=0, tiled=True),
            lax.all_gather(norm_shift[layer_index], ("dp", "seq"), axis=0, tiled=True),
        )
        project, out_matrix, up_matrix, down_matrix, gains, shifts = unpack(gathered)
        key_all, value_all = (
            lax.all_gather(heads[1], "seq", axis=1, tiled=True),
            lax.all_gather(heads[2], "seq", axis=1, tiled=True),
        )
        grad_two, gain_two, shift_two = normalize_back(
            grad_hidden, scaled_two, factor_two, gains[1]
        )
        shrunk_grad = grad_two.astype(jnp.bfloat16).reshape(count, GROUPS, part)
        down_terms = jnp.einsum(
            "tgf,tgo->gfo",
            activated.reshape(count, GROUPS, part_ff),
            shrunk_grad,
            preferred_element_type=jnp.float32,
        )
        active_grad = jnp.einsum(
            "tgo,gfo->tgf", shrunk_grad, down_matrix, preferred_element_type=jnp.float32
        ).reshape(count, FF)
        unused_value, gelu_pull = jax.vjp(partial(jax.nn.gelu, approximate=False), expanded)
        expanded_grad = (
            gelu_pull(active_grad)[0].astype(jnp.bfloat16).reshape(count, GROUPS, part_ff)
        )
        up_terms = jnp.einsum(
            "tgi,tgf->gif",
            middle_low.reshape(count, GROUPS, part),
            expanded_grad,
            preferred_element_type=jnp.float32,
        )
        middle_grad = grad_two + jnp.einsum(
            "tgf,gif->tgi", expanded_grad, up_matrix, preferred_element_type=jnp.float32
        ).reshape(count, D)
        grad_one, gain_one, shift_one = normalize_back(
            middle_grad, scaled_one, factor_one, gains[0]
        )
        branch_grad = grad_one.astype(jnp.bfloat16)
        out_terms = jnp.einsum(
            "ti,to->io", attended_low, branch_grad, preferred_element_type=jnp.float32
        )
        attended_grad = jnp.einsum(
            "to,io->ti", branch_grad, out_matrix, preferred_element_type=jnp.float32
        ).astype(jnp.bfloat16)
        grad_heads = attended_grad.reshape(count, HEADS, HEAD).transpose(1, 0, 2)
        grad_query, key_terms, value_terms = lax.map(
            partial(head_backward, key_ok, scaling),
            (heads[0], key_all, value_all, grad_heads, log_total),
        )
        grad_key, grad_value = (
            lax.psum_scatter(
                key_terms.astype(jnp.bfloat16), "seq", scatter_dimension=1, tiled=True
            ).astype(jnp.float32),
            lax.psum_scatter(
                value_terms.astype(jnp.bfloat16), "seq", scatter_dimension=1, tiled=True
            ).astype(jnp.float32),
        )
        grad_projected = jnp.stack((grad_query, grad_key, grad_value)).astype(jnp.bfloat16)
        grad_projected = grad_projected.transpose(0, 2, 1, 3).reshape(3, count, GROUPS, part)
        qkv_terms = jnp.einsum(
            "tgi,ctgo->cgio",
            inputs_low.reshape(count, GROUPS, part),
            grad_projected,
            preferred_element_type=jnp.float32,
        )
        grad_hidden = grad_one + jnp.einsum(
            "ctgo,cgio->tgi", grad_projected, project, preferred_element_type=jnp.float32
        ).reshape(count, D)
        owned = (
            lax.psum_scatter(qkv_terms.reshape(-1), ("dp", "seq"), scatter_dimension=0, tiled=True),
            lax.psum_scatter(out_terms.reshape(-1), ("dp", "seq"), scatter_dimension=0, tiled=True),
            lax.psum_scatter(up_terms.reshape(-1), ("dp", "seq"), scatter_dimension=0, tiled=True),
            lax.psum_scatter(
                down_terms.reshape(-1), ("dp", "seq"), scatter_dimension=0, tiled=True
            ),
            lax.psum_scatter(
                jnp.stack((gain_one, gain_two)).reshape(-1),
                ("dp", "seq"),
                scatter_dimension=0,
                tiled=True,
            ),
            lax.psum_scatter(
                jnp.stack((shift_one, shift_two)).reshape(-1),
                ("dp", "seq"),
                scatter_dimension=0,
                tiled=True,
            ),
        )
        owned_list.insert(0, owned)
    tokens_grad = grad_hidden.astype(jnp.bfloat16)[None]
    stacked = tuple((jnp.stack([entry[member] for entry in owned_list]) for member in range(6)))
    return (
        mixed,
        tokens_grad,
        stacked[0],
        stacked[1],
        stacked[2],
        stacked[3],
        stacked[4],
        stacked[5],
    )


F32 = jnp.float32
BF16 = jnp.bfloat16
PART = D // GROUPS
PART_FF = FF // GROUPS
LAYERS = 2
ROWS = 128
HALF = 4 * ROWS
FULL = 2 * HALF
NDEV = 32
UNIT = PART // 8
HEADS_HERE = HEADS // GROUPS
KEY_BLOCK = 256
FF_BLOCK = 128
SEMS = 512
MESH = pl.DeviceIdType.MESH

SCRATCH = dict(
    x_all=((LAYERS, PART, FULL), BF16),
    cot_t=((PART, HALF), BF16),
    tok_t=((D, ROWS), BF16),
    cotown_t=((D, ROWS), BF16),
    ln_in=((8, 128), F32),
    gn_in=((2, PART, 128), BF16),
    wq_in=((LAYERS, 8, 3, UNIT, PART), BF16),
    wr_in=((LAYERS, 8, GROUPS, UNIT, PART), BF16),
    wc_in=((LAYERS, 8, GROUPS, UNIT, PART), BF16),
    wu_in=((LAYERS, 8, UNIT, PART_FF), BF16),
    wd_in=((LAYERS, 8, PART_FF // 8, PART), BF16),
    wn_q=((LAYERS, 3, PART, PART), BF16),
    wn_r=((LAYERS, GROUPS, PART, PART), BF16),
    wn_u=((LAYERS, PART, PART_FF), BF16),
    wn_d=((LAYERS, PART_FF, PART), BF16),
    wt_u=((PART_FF, PART), BF16),
    bias=((FULL, 128), F32),
    q_t=((LAYERS, PART, HALF), BF16),
    k_t=((LAYERS, PART, FULL), BF16),
    v_t=((LAYERS, PART, FULL), BF16),
    k_n=((LAYERS, HEADS_HERE, FULL, HEAD), BF16),
    v_n=((LAYERS, HEADS_HERE, FULL, HEAD), BF16),
    p_t=((LAYERS, HEADS_HERE, FULL, HALF), BF16),
    rinv=((LAYERS, HEADS_HERE, 8, HALF), F32),
    s_scr=((FULL, HALF), F32),
    ds_scr=((FULL, HALF), BF16),
    o_t=((LAYERS, PART, HALF), F32),
    att_all=((LAYERS, D, HALF), BF16),
    bg_all=((LAYERS, D, HALF), BF16),
    xh1=((LAYERS, PART, HALF), F32),
    xh2=((LAYERS, PART, HALF), F32),
    r1=((LAYERS, 8, HALF), F32),
    r2=((LAYERS, 8, HALF), F32),
    mid=((LAYERS, PART, HALF), BF16),
    act=((LAYERS, PART_FF, HALF), BF16),
    dgl=((LAYERS, PART_FF, HALF), F32),
    eg=((LAYERS, PART_FF, HALF), BF16),
    sgb=((LAYERS, PART, HALF), BF16),
    fg=((PART, HALF), F32),
    do_t=((PART, HALF), BF16),
    dq_t=((PART, HALF), BF16),
    dk_t=((PART, FULL), BF16),
    dv_t=((PART, FULL), BF16),
    dx_out=((LAYERS, PART, HALF), F32),
    dx_in=((LAYERS, PART, HALF), F32),
    stats=((4 * LAYERS, 4, 8, HALF), F32),
    mix_out=((PART, HALF), BF16),
    mix_in=((D, ROWS), BF16),
    tg_out=((PART, HALF), BF16),
    tg_in=((D, ROWS), BF16),
    gs_acc=((2, PART, 128), F32),
    gs_in=((8, PART // 4, 128), F32),
    gb_d=((LAYERS, 8, PART_FF // 8, PART), BF16),
    gb_u=((LAYERS, 8, UNIT, PART_FF), BF16),
    gb_o=((LAYERS, 8, GROUPS, UNIT, PART), BF16),
    gb_q=((LAYERS, 8, 3, UNIT, PART), BF16),
    sb_d=((LAYERS, 4, PART_FF // 8, PART), BF16),
    sb_u=((LAYERS, 4, UNIT, PART_FF), BF16),
    sb_o=((LAYERS, 4, GROUPS, UNIT, PART), BF16),
    sb_q=((LAYERS, 4, 3, UNIT, PART), BF16),
    gm_d=((LAYERS, 4, PART_FF // 8, PART), BF16),
    gm_u=((LAYERS, 4, UNIT, PART_FF), BF16),
    gm_o=((LAYERS, 4, GROUPS, UNIT, PART), BF16),
    gm_q=((LAYERS, 4, 3, UNIT, PART), BF16),
    rg_d=((LAYERS, 4, PART_FF // 8, PART), BF16),
    rg_u=((LAYERS, 4, UNIT, PART_FF), BF16),
    rg_o=((LAYERS, 4, GROUPS, UNIT, PART), BF16),
    rg_q=((LAYERS, 4, 3, UNIT, PART), BF16),
)


def mm(a, b):
    return jnp.dot(a, b, preferred_element_type=F32)


def mm_nt(a, b):
    return lax.dot_general(a, b, (((1,), (1,)), ((), ())), preferred_element_type=F32)


def rows_of(units):
    count, rows, columns = units.shape
    return units.astype(F32).reshape(count * rows, columns).astype(BF16)


def units_of(matrix):
    rows, columns = matrix.shape
    return matrix.reshape(rows // UNIT, UNIT, columns).astype(BF16)


def erf_pair(v):
    cdf = 0.5 * (1.0 + lax.erf(v * (0.5**0.5)))
    slope = cdf + v * (jnp.exp(-0.5 * v * v) * 0.3989422804014327)
    return cdf, slope


def fast_kernel(
    tokens, cotangent, length, misc, w_qkv, w_out, w_up, w_down,
    mixed, tokens_grad, g_qkv, g_out, g_up, g_down, g_norm,
    sems, *scratch,
):
    b = types.SimpleNamespace(**dict(zip(SCRATCH, scratch)))
    p, s = lax.axis_index("dp"), lax.axis_index("seq")
    x, c, z, y = p // 2, p % 2, s // 2, s % 2
    g = 2 * x + y
    own = pl.multiple_of(HALF * c, HALF)
    other = pl.multiple_of(HALF * (1 - c), HALF)
    g_rows = pl.multiple_of(PART * g, PART)
    used = [0]
    pending = []

    def new_sems(count=1):
        first = used[0]
        used[0] += count
        assert used[0] <= SEMS
        return first

    def dev(dx, dc, dz, dy):
        return (2 * dx + dc, 2 * dz + dy)

    sibling = dev(x, 1 - c, z, y)
    square = (dev(x, c, z, 1 - y), dev(1 - x, c, z, y), dev(1 - x, c, z, 1 - y))

    def send(src, dst, to, arrive, maybe_here=False):
        copy = pltpu.make_async_remote_copy(
            src, dst, sems.at[new_sems()], sems.at[arrive], device_id=to, device_id_type=MESH
        )
        if not maybe_here:
            copy.start()
            pending.append((copy, None))
            return
        away = jnp.logical_or(to[0] != p, to[1] != s)

        @pl.when(away)
        def _():
            copy.start()

        @pl.when(jnp.logical_not(away))
        def _():
            pltpu.make_async_copy(src, dst, sems.at[arrive]).start()

        pending.append((copy, away))

    def arrived(ref, arrive):
        pltpu.make_async_copy(ref, ref, sems.at[arrive]).wait()

    me = 8 * p + s
    barrier = pltpu.get_barrier_semaphore()

    def greet(i, carry):
        d = (me + i) % NDEV
        pl.semaphore_signal(barrier, inc=1, device_id=(d // 8, d % 8), device_id_type=MESH)
        return carry

    lax.fori_loop(1, NDEV, greet, 0)
    b.tok_t[...] = tokens[...].T
    b.cotown_t[...] = cotangent[...].T
    b.gs_acc[...] = jnp.zeros((2, PART, 128), F32)
    pl.semaphore_wait(barrier, NDEV - 1)

    tok_sem, len_sem, cot_sem, gn_sem = (new_sems() for _ in range(4))
    half_of = s // 4
    for gg in range(4):
        to = dev(gg // 2, half_of, p, gg % 2)
        lane = pl.multiple_of(ROWS * s, ROWS)
        send(
            b.tok_t.at[pl.ds(PART * gg, PART), :],
            b.x_all.at[0, :, pl.ds(lane, ROWS)],
            to, tok_sem, True,
        )
    len_copies = []
    first_chunk = s % 4 == 0
    for gg in range(4):
        to = dev(gg // 2, half_of, p, gg % 2)
        away = jnp.logical_or(to[0] != p, to[1] != s)
        copy = pltpu.make_async_remote_copy(
            length, b.ln_in, sems.at[new_sems()], sems.at[len_sem], device_id=to, device_id_type=MESH
        )

        @pl.when(jnp.logical_and(first_chunk, away))
        def _():
            copy.start()

        @pl.when(jnp.logical_and(first_chunk, jnp.logical_not(away)))
        def _():
            pltpu.make_async_copy(length, b.ln_in, sems.at[len_sem]).start()

        pending.append((copy, jnp.logical_and(first_chunk, away)))

    weights_in = dict(q=b.wq_in, r=b.wr_in, c=b.wc_in, u=b.wu_in, d=b.wd_in)
    arrive_w = {(name, l): new_sems() for l in range(LAYERS) for name in "qrcud"}
    relay_w = {(name, l): new_sems() for l in range(LAYERS) for name in "qrcud"}

    def send_qkv(l):
        for k in range(3):
            u = 3 * me + k
            cc, gg, t = u // 32, (u % 32) // 8, u % 8
            for zz in range(4):
                send(
                    w_qkv.at[l, k], b.wq_in.at[l, t, cc],
                    dev(gg // 2, t // 4, zz, gg % 2), arrive_w["q", l], True,
                )

    def send_out(l):
        for zz in range(4):
            send(w_out.at[l], b.wr_in.at[l, s], dev(p // 2, s // 4, zz, p % 2), arrive_w["r", l], True)
        for cg in range(4):
            for zz in range(4):
                send(
                    w_out.at[l, cg], b.wc_in.at[l, s, p],
                    dev(cg // 2, s // 4, zz, cg % 2), arrive_w["c", l], True,
                )

    def send_updown(l):
        for zz in range(4):
            send(w_up.at[l], b.wu_in.at[l, s], dev(p // 2, s // 4, zz, p % 2), arrive_w["u", l], True)
        for zz in range(4):
            send(w_down.at[l], b.wd_in.at[l, s], dev(p // 2, s // 4, zz, p % 2), arrive_w["d", l], True)

    def relay(name, l):
        buffer = weights_in[name]
        mine = buffer.at[l, pl.ds(4 * c, 4)]
        arrived(mine, arrive_w[name, l])
        send(mine, mine, sibling, relay_w[name, l])

    def relayed(name, l):
        arrived(weights_in[name].at[l, pl.ds(4 * (1 - c), 4)], relay_w[name, l])

    send_qkv(0)
    for zz in range(4):
        for cc in range(2):
            gg = 2 * (p % 2) + s // 4
            row = pl.multiple_of(48 * (s % 4), 16)
            send(
                misc, b.gn_in.at[p // 2, pl.ds(row, 48), :],
                dev(gg // 2, cc, zz, gg % 2), gn_sem, True,
            )
    send_out(0)
    send_updown(0)
    for gg in range(4):
        lane = pl.multiple_of(ROWS * (s % 4), ROWS)
        send(
            b.cotown_t.at[pl.ds(PART * gg, PART), :], b.cot_t.at[:, pl.ds(lane, ROWS)],
            dev(gg // 2, half_of, p, gg % 2), cot_sem, True,
        )
    send_qkv(1)
    send_out(1)
    send_updown(1)

    x_sem = [new_sems() for _ in range(LAYERS)]
    x_half = b.x_all.at[0, :, pl.ds(own, HALF)]
    arrived(x_half, tok_sem)
    send(x_half, x_half, sibling, x_sem[0])
    relay("q", 0)
    arrived(b.ln_in, len_sem)
    valid = b.ln_in[0:1, 0:1]
    key_at = lax.broadcasted_iota(jnp.int32, (FULL, 128), 0).astype(F32)
    b.bias[...] = jnp.where(key_at < valid, 0.0, -1e30)
    arrived(b.gn_in, gn_sem)

    def gain_shift(l, k):
        columns = b.gn_in[k].astype(F32)
        return columns[:, 2 * l : 2 * l + 1], columns[:, 2 * l + 1 : 2 * l + 2]

    stat_used = [0]

    def exchange(first, second):
        i = stat_used[0]
        stat_used[0] += 1
        buffer = b.stats.at[i]
        buffer[0] = jnp.concatenate([first, second, jnp.zeros((6, HALF), F32)], axis=0)
        base = new_sems(3)
        for d in range(3):
            send(buffer.at[0], buffer.at[d + 1], square[d], base + d)

        def finish():
            for d in range(3):
                arrived(buffer.at[d + 1], base + d)
            return [(buffer[d, 0:1], buffer[d, 1:2]) for d in range(4)]

        return finish

    def normalize_here(v, name, l, gain, shift):
        mean_here = jnp.sum(v, axis=0, keepdims=True) * (1.0 / PART)
        d = v - mean_here
        finish = exchange(mean_here, jnp.sum(d * d, axis=0, keepdims=True))
        pairs = finish()
        mean = (pairs[0][0] + pairs[1][0] + pairs[2][0] + pairs[3][0]) * 0.25
        total = sum(m2 + PART * (m1 - mean) * (m1 - mean) for m1, m2 in pairs)
        factor = lax.rsqrt(total * (1.0 / D) + EPSILON)
        scaled = (v - mean) * factor
        getattr(b, "xh" + name)[l] = scaled
        getattr(b, "r" + name)[l, 0:1] = factor
        return scaled * gain + shift

    att_sem = [[new_sems(3) for _ in range(3)] for _ in range(LAYERS)]
    att_send = [[new_sems(3) for _ in range(3)] for _ in range(LAYERS)]

    def forward(l):
        x_own = b.x_all[l, :, pl.ds(own, HALF)]
        if l > 0:
            relay("q", l)
        relayed("q", l)
        turned = []
        for cc in range(3):
            nat = rows_of(b.wq_in[l, :, cc])
            b.wn_q[l, cc] = nat
            turned.append(nat.T)
        b.q_t[l] = mm(turned[0], x_own).astype(BF16) * jnp.asarray(0.125, BF16)

        def keys_values(start, part):
            for matrix, name in ((turned[1], "k"), (turned[2], "v")):
                value = mm(matrix, part).astype(BF16)
                getattr(b, name + "_t")[l, :, pl.ds(start, HALF)] = value
                for h in range(HEADS_HERE):
                    getattr(b, name + "_n")[l, h, pl.ds(start, HALF), :] = value[HEAD * h : HEAD * (h + 1)].T

        keys_values(own, x_own)
        arrived(b.x_all.at[l, :, pl.ds(other, HALF)], x_sem[l])
        keys_values(other, b.x_all[l, :, pl.ds(other, HALF)])

        def one_head(h, carry):
            head = pl.multiple_of(HEAD * h, HEAD)
            q = b.q_t[l, pl.ds(head, HEAD), :]
            largest = jnp.full((1, HALF), -jnp.inf, F32)
            for kb in range(0, FULL, KEY_BLOCK):
                scores = mm(b.k_n[l, h, kb : kb + KEY_BLOCK, :], q) + b.bias[kb : kb + KEY_BLOCK, 0:1]
                b.s_scr[kb : kb + KEY_BLOCK] = scores
                largest = jnp.maximum(largest, jnp.max(scores, axis=0, keepdims=True))
            total = jnp.zeros((1, HALF), F32)
            for kb in range(0, FULL, KEY_BLOCK):
                powers = jnp.exp(b.s_scr[kb : kb + KEY_BLOCK] - largest)
                total += jnp.sum(powers, axis=0, keepdims=True)
                b.p_t[l, h, kb : kb + KEY_BLOCK] = powers.astype(BF16)
            inverse = 1.0 / total
            b.rinv[l, h, 0:1] = inverse
            out = mm(b.v_t[l, pl.ds(head, HEAD), :], b.p_t[l, h]) * inverse
            b.o_t[l, pl.ds(head, HEAD), :] = out
            rows = pl.ds(pl.multiple_of(g_rows + head, HEAD), HEAD)
            b.att_all[l, rows, :] = out.astype(BF16)
            piece = b.att_all.at[l, rows, :]
            for d in range(3):
                pltpu.make_async_remote_copy(
                    piece, piece, sems.at[att_send[l][d] + h], sems.at[att_sem[l][d] + h],
                    device_id=square[d], device_id_type=MESH,
                ).start()
            return carry

        lax.fori_loop(0, HEADS_HERE, one_head, 0)
        for name in "cudr":
            relay(name, l)
        relayed("c", l)
        turned = [rows_of(b.wc_in[l, :, r]).T for r in range(4)]
        relayed("u", l)
        nat = rows_of(b.wu_in[l])
        b.wn_u[l] = nat
        b.wt_u[...] = nat.T
        relayed("d", l)
        nat = b.wd_in[l].reshape(PART_FF, PART)
        b.wn_d[l] = nat
        down_t = nat.T
        flips = ((0, 1), (1, 0), (1, 1))
        for h in range(HEADS_HERE):
            for d, (fx, fy) in enumerate(flips):
                px = 1 - x if fx else x
                py = 1 - y if fy else y
                start = pl.multiple_of(PART * (2 * px + py) + HEAD * h, HEAD)
                arrived(b.att_all.at[l, pl.ds(start, HEAD), :], att_sem[l][d] + h)
        branch = sum(mm(turned[r], b.att_all[l, PART * r : PART * (r + 1), :]) for r in range(4))
        gain, shift = gain_shift(l, 0)
        middle = normalize_here(x_own.astype(F32) + branch, "1", l, gain, shift).astype(BF16)
        b.mid[l] = middle

        def one_block(i, carry):
            rows = pl.ds(pl.multiple_of(FF_BLOCK * i, FF_BLOCK), FF_BLOCK)
            expanded = mm(b.wt_u[rows, :], b.mid[l])
            cdf, slope = erf_pair(expanded)
            b.act[l, rows, :] = (expanded * cdf).astype(BF16)
            b.dgl[l, rows, :] = slope
            return carry

        lax.fori_loop(0, PART_FF // FF_BLOCK, one_block, 0)
        second = middle.astype(F32) + mm(down_t, b.act[l])
        gain, shift = gain_shift(l, 1)
        return normalize_here(second, "2", l, gain, shift)

    hidden = forward(0)
    b.x_all[1, :, pl.ds(own, HALF)] = hidden.astype(BF16)
    x_half = b.x_all.at[1, :, pl.ds(own, HALF)]
    send(x_half, x_half, sibling, x_sem[1])
    hidden = forward(1)

    mix_sem, tg_sem = new_sems(), new_sems()

    def send_back(value, out_ref, in_ref, arrive):
        out_ref[...] = value.astype(BF16)
        for k in range(4):
            send(
                out_ref.at[:, ROWS * k : ROWS * (k + 1)], in_ref.at[pl.ds(g_rows, PART), :],
                (z, 4 * c + k), arrive, True,
            )

    send_back(hidden, b.mix_out, b.mix_in, mix_sem)

    half_sem = {(name, l): new_sems() for l in range(LAYERS) for name in "duoq"}
    owner_sem = {(name, l): new_sems() for l in range(LAYERS) for name in "duoq"}

    def to_sibling(name, l):
        send(
            getattr(b, "gb_" + name).at[l, pl.ds(4 * (1 - c), 4)], getattr(b, "sb_" + name).at[l], sibling, half_sem[name, l]
        )

    def to_owners(name, l):
        arrived(getattr(b, "sb_" + name).at[l], half_sem[name, l])
        mine = getattr(b, "gb_" + name)[l, pl.ds(4 * c, 4)].astype(F32) + getattr(b, "sb_" + name)[l].astype(F32)
        getattr(b, "gm_" + name)[l] = mine.astype(BF16)
        for k in range(4):
            t = 4 * c + k
            if name != "q":
                send(getattr(b, "gm_" + name).at[l, k], getattr(b, "rg_" + name).at[l, z], (g, t), owner_sem[name, l], True)
                continue
            for cc in range(3):
                u = 32 * cc + 8 * g + t
                j = u // 3
                send(
                    b.gm_q.at[l, k, cc], b.rg_q.at[l, z, u % 3], (j // 8, j % 8), owner_sem["q", l], True
                )

    lane_at = lax.broadcasted_iota(jnp.int32, (PART, 128), 1)

    def normalize_back_here(grad, name, l, k):
        gain, _ = gain_shift(l, k)
        scaled = getattr(b, "xh" + name)[l]
        weighted = grad * gain
        finish = exchange(
            jnp.sum(weighted, axis=0, keepdims=True), jnp.sum(weighted * scaled, axis=0, keepdims=True)
        )
        gain_grad = jnp.sum(grad * scaled, axis=1, keepdims=True)
        shift_grad = jnp.sum(grad, axis=1, keepdims=True)
        b.gs_acc[k] += jnp.where(lane_at == 2 * l, gain_grad, 0.0) + jnp.where(
            lane_at == 2 * l + 1, shift_grad, 0.0
        )
        pairs = finish()
        one = (pairs[0][0] + pairs[1][0] + pairs[2][0] + pairs[3][0]) * (1.0 / D)
        two = (pairs[0][1] + pairs[1][1] + pairs[2][1] + pairs[3][1]) * (1.0 / D)
        return getattr(b, "r" + name)[l, 0:1] * (weighted - one - scaled * two)

    bg_sem = [new_sems(3) for _ in range(LAYERS)]
    dx_sem = [new_sems() for _ in range(LAYERS)]

    def backward(l, grad):
        second_grad = normalize_back_here(grad, "2", l, 1)
        b.sgb[l] = second_grad.astype(BF16)
        if l + 1 < LAYERS:
            to_owners("q", l + 1)

        def one_block(i, carry):
            rows = pl.ds(pl.multiple_of(FF_BLOCK * i, FF_BLOCK), FF_BLOCK)
            active_grad = mm(b.wn_d[l, rows, :], b.sgb[l])
            b.eg[l, rows, :] = (active_grad * b.dgl[l, rows, :]).astype(BF16)
            return carry

        lax.fori_loop(0, PART_FF // FF_BLOCK, one_block, 0)
        middle_grad = second_grad + mm(b.wn_u[l], b.eg[l])
        first_grad = normalize_back_here(middle_grad, "1", l, 0)
        b.fg[...] = first_grad
        b.bg_all[l, pl.ds(g_rows, PART), :] = first_grad.astype(BF16)
        piece = b.bg_all.at[l, pl.ds(g_rows, PART), :]
        for d in range(3):
            send(piece, piece, square[d], bg_sem[l] + d)
        grads = mm_nt(b.act[l], b.sgb[l])
        b.gb_d[l] = grads.astype(BF16).reshape(8, PART_FF // 8, PART)
        to_sibling("d", l)
        b.gb_u[l] = units_of(mm_nt(b.mid[l], b.eg[l]))
        to_sibling("u", l)
        relayed("r", l)
        for cg in range(4):
            b.wn_r[l, cg] = rows_of(b.wr_in[l, :, cg])
        for d, (fx, fy) in enumerate(((0, 1), (1, 0), (1, 1))):
            px = 1 - x if fx else x
            py = 1 - y if fy else y
            start = pl.multiple_of(PART * (2 * px + py), PART)
            arrived(b.bg_all.at[l, pl.ds(start, PART), :], bg_sem[l] + d)
        attended_grad = sum(mm(b.wn_r[l, r], b.bg_all[l, PART * r : PART * (r + 1), :]) for r in range(4))
        b.do_t[...] = attended_grad.astype(BF16)
        att = b.att_all[l, pl.ds(g_rows, PART), :]
        for cg in range(4):
            b.gb_o[l, :, cg] = units_of(mm_nt(att, b.bg_all[l, PART * cg : PART * (cg + 1), :]))
        to_sibling("o", l)

        def one_head(h, carry):
            head = pl.multiple_of(HEAD * h, HEAD)
            rows = pl.ds(head, HEAD)
            inverse = b.rinv[l, h, 0:1]
            grad_out = b.do_t[rows, :].astype(F32)
            delta = jnp.sum(grad_out * b.o_t[l, rows, :], axis=0, keepdims=True) * inverse
            grad_scaled = (grad_out * inverse).astype(BF16)
            for kb in range(0, FULL, KEY_BLOCK):
                block = slice(kb, kb + KEY_BLOCK)
                grad_probs = mm(b.v_n[l, h, block, :], grad_scaled)
                b.ds_scr[block] = (b.p_t[l, h, block].astype(F32) * (grad_probs - delta)).astype(BF16)
            b.dq_t[rows, :] = (mm(b.k_t[l, rows, :], b.ds_scr[...]) * 0.125).astype(BF16)
            b.dk_t[rows, :] = mm_nt(b.q_t[l, rows, :], b.ds_scr[...]).astype(BF16)
            b.dv_t[rows, :] = mm_nt(grad_scaled, b.p_t[l, h]).astype(BF16)
            return carry

        lax.fori_loop(0, HEADS_HERE, one_head, 0)
        w_q, w_k, w_v = (b.wn_q[l, cc] for cc in range(3))
        b.dx_out[l] = mm(w_k, b.dk_t[:, pl.ds(other, HALF)]) + mm(w_v, b.dv_t[:, pl.ds(other, HALF)])
        send(b.dx_out.at[l], b.dx_in.at[l], sibling, dx_sem[l])
        x_own = b.x_all[l, :, pl.ds(own, HALF)]
        b.gb_q[l, :, 0] = units_of(mm_nt(x_own, b.dq_t[...]))
        b.gb_q[l, :, 1] = units_of(mm_nt(b.x_all[l], b.dk_t[...]))
        b.gb_q[l, :, 2] = units_of(mm_nt(b.x_all[l], b.dv_t[...]))
        to_sibling("q", l)
        for name in "duo":
            to_owners(name, l)
        here = mm(w_q, b.dq_t[...])
        here += mm(w_k, b.dk_t[:, pl.ds(own, HALF)]) + mm(w_v, b.dv_t[:, pl.ds(own, HALF)])
        arrived(b.dx_in.at[l], dx_sem[l])
        return b.fg[...] + here + b.dx_in[l]

    arrived(b.cot_t, cot_sem)
    position = lax.broadcasted_iota(jnp.int32, (PART, HALF), 1) + HALF * c
    grad = jnp.where(position.astype(F32) < valid, b.cot_t[...].astype(F32), 0.0)
    grad = backward(1, grad)
    grad = backward(0, grad)
    send_back(grad, b.tg_out, b.tg_in, tg_sem)
    to_owners("q", 0)

    gs_sem = new_sems()
    for k in range(2):
        for q in range(4):
            send(
                b.gs_acc.at[k, 48 * q : 48 * (q + 1), :], b.gs_in.at[2 * z + c],
                (2 * k + g // 2, 4 * (g % 2) + q), gs_sem, True,
            )

    arrived(b.mix_in, mix_sem)
    mixed[...] = b.mix_in[...].T
    for l in reversed(range(LAYERS)):
        for name, out in (("d", g_down), ("u", g_up), ("o", g_out), ("q", g_qkv)):
            arrived(getattr(b, "rg_" + name).at[l], owner_sem[name, l])
            out[l] = sum(getattr(b, "rg_" + name)[l, i].astype(F32) for i in range(4))
    arrived(b.tg_in, tg_sem)
    tokens_grad[...] = b.tg_in[...].T
    arrived(b.gs_in, gs_sem)
    g_norm[...] = sum(b.gs_in[i] for i in range(8))

    for copy, when in pending:
        if when is None:
            copy.wait_send()
        else:
            pl.when(when)(copy.wait_send)
    for l in range(LAYERS):
        for h in range(HEADS_HERE):
            for d in range(3):
                piece = b.att_all.at[l, pl.ds(pl.multiple_of(g_rows + HEAD * h, HEAD), HEAD), :]
                pltpu.make_async_remote_copy(
                    piece, piece, sems.at[att_send[l][d] + h], sems.at[att_sem[l][d] + h],
                    device_id=square[d], device_id_type=MESH,
                ).wait_send()


def fast_device(
    tokens, lengths, qkv_weight, out_weight, up_weight, down_weight, norm_gain, norm_shift, cotangent
):
    length = jnp.full((8, 128), lengths[0], F32)
    misc = jnp.stack([norm_gain[0], norm_shift[0], norm_gain[1], norm_shift[1]], axis=1)
    misc = jnp.pad(misc, ((0, 0), (0, 124)))
    operands = (
        tokens[0],
        cotangent[0],
        length,
        misc,
        qkv_weight.reshape(LAYERS, 3, UNIT, PART),
        out_weight.reshape(LAYERS, UNIT, GROUPS, PART).transpose(0, 2, 1, 3),
        up_weight.reshape(LAYERS, UNIT, PART_FF),
        down_weight.reshape(LAYERS, PART_FF // 8, PART),
    )
    vmem = pl.BlockSpec(memory_space=pltpu.VMEM)
    shapes = (
        ((ROWS, D), BF16),
        ((ROWS, D), BF16),
        ((LAYERS, 3, UNIT, PART), F32),
        ((LAYERS, GROUPS, UNIT, PART), F32),
        ((LAYERS, UNIT, PART_FF), F32),
        ((LAYERS, PART_FF // 8, PART), F32),
        ((PART // 4, 128), F32),
    )
    mixed, tokens_grad, g_qkv, g_out, g_up, g_down, g_norm = pl.pallas_call(
        fast_kernel,
        out_shape=tuple(jax.ShapeDtypeStruct(*shape) for shape in shapes),
        in_specs=[vmem] * len(operands),
        out_specs=tuple([vmem] * len(shapes)),
        scratch_shapes=[pltpu.SemaphoreType.DMA((SEMS,))] + [pltpu.VMEM(*entry) for entry in SCRATCH.values()],
        compiler_params=pltpu.CompilerParams(
            collective_id=0, has_side_effects=True, vmem_limit_bytes=60 * 2**20
        ),
        name="encoder",
    )(*operands)
    g_norm = g_norm[:, :4].T
    return (
        mixed[None],
        tokens_grad[None],
        g_qkv.reshape(LAYERS, -1),
        g_out.transpose(0, 2, 1, 3).reshape(LAYERS, -1),
        g_up.reshape(LAYERS, -1),
        g_down.reshape(LAYERS, -1),
        g_norm[0::2],
        g_norm[1::2],
    )


def solution(mesh):
    small = (mesh.shape["dp"], mesh.shape["seq"]) == (4, 8)
    return jax.shard_map(
        fast_device if small else per_device,
        mesh=mesh,
        in_specs=(
            P("dp", "seq", None),
            P("dp"),
            P(None, ("dp", "seq")),
            P(None, ("dp", "seq")),
            P(None, ("dp", "seq")),
            P(None, ("dp", "seq")),
            P(None, ("dp", "seq")),
            P(None, ("dp", "seq")),
            P("dp", "seq", None),
        ),
        out_specs=(
            P("dp", "seq", None),
            P("dp", "seq", None),
            P(None, ("dp", "seq")),
            P(None, ("dp", "seq")),
            P(None, ("dp", "seq")),
            P(None, ("dp", "seq")),
            P(None, ("dp", "seq")),
            P(None, ("dp", "seq")),
        ),
        check_vma=False,
    )
```

```python
import types
from functools import partial

import jax
import jax.numpy as jnp
from jax import lax
from jax.experimental import pallas as pl
from jax.experimental.pallas import tpu as pltpu
from jax.sharding import PartitionSpec as P

D = 768
HEADS = 12
HEAD = 64
FF = 3072
GROUPS = 4


EPSILON = 1e-06


def grouped(inputs, weight):
    count = inputs.shape[0]
    shaped = inputs.reshape(count, weight.shape[0], -1)
    result = jnp.einsum("tgi,gio->tgo", shaped, weight, preferred_element_type=jnp.float32)
    return result.reshape(count, -1)


def normalize(values, gain, shift):
    center = values - jnp.mean(values, axis=-1, keepdims=True)
    factor = lax.rsqrt(jnp.mean(center * center, axis=-1, keepdims=True) + EPSILON)
    scaled = center * factor
    return (scaled * gain + shift, scaled, factor)


def normalize_back(grad_out, scaled, factor, gain):
    weighted = grad_out * gain
    grad_in = factor * (
        weighted
        - jnp.mean(weighted, axis=-1, keepdims=True)
        - scaled * jnp.mean(weighted * scaled, axis=-1, keepdims=True)
    )
    return (grad_in, jnp.sum(grad_out * scaled, axis=0), jnp.sum(grad_out, axis=0))


def unpack(pieces):
    qkv_flat, out_flat, up_flat, down_flat, gain_flat, shift_flat = pieces
    part = D // GROUPS
    part_ff = FF // GROUPS
    return (
        qkv_flat.reshape(3, GROUPS, part, part),
        out_flat.reshape(D, D),
        up_flat.reshape(GROUPS, part, part_ff),
        down_flat.reshape(GROUPS, part_ff, part),
        gain_flat.reshape(2, D).astype(jnp.float32),
        shift_flat.reshape(2, D).astype(jnp.float32),
    )


def project_heads(rows, matrices):
    total_rows = rows.shape[0]
    part = D // GROUPS
    result = jnp.einsum(
        "tgi,cgio->ctgo",
        rows.reshape(total_rows, GROUPS, part),
        matrices,
        preferred_element_type=jnp.float32,
    ).astype(jnp.bfloat16)
    return result.reshape(matrices.shape[0], total_rows, HEADS, HEAD).transpose(0, 2, 1, 3)


def head_forward(key_ok, scaling, pieces):
    query_head, key_head, value_head = pieces
    scores = (
        jnp.einsum("td,sd->ts", query_head, key_head, preferred_element_type=jnp.float32) * scaling
    )
    scores = jnp.where(key_ok[None, :], scores, -1e30)
    largest = jnp.max(scores, axis=-1, keepdims=True)
    powers = jnp.exp(scores - largest)
    total = jnp.sum(powers, axis=-1, keepdims=True)
    probs = (powers / total).astype(jnp.bfloat16)
    result = jnp.dot(probs, value_head, preferred_element_type=jnp.float32)
    return (result, (largest + jnp.log(total))[:, 0])


def head_backward(key_ok, scaling, pieces):
    query_head, key_head, value_head, grad_head, log_total = pieces
    scores = (
        jnp.einsum("td,sd->ts", query_head, key_head, preferred_element_type=jnp.float32) * scaling
    )
    scores = jnp.where(key_ok[None, :], scores, -1e30)
    probs = jnp.exp(scores - log_total[:, None])
    grad_probs = jnp.einsum("td,sd->ts", grad_head, value_head, preferred_element_type=jnp.float32)
    delta_row = jnp.sum(probs * grad_probs, axis=-1, keepdims=True)
    grad_scores = (probs * (grad_probs - delta_row)).astype(jnp.bfloat16)
    grad_query = jnp.dot(grad_scores, key_head, preferred_element_type=jnp.float32) * scaling
    grad_key = (
        jnp.einsum("ts,td->sd", grad_scores, query_head, preferred_element_type=jnp.float32)
        * scaling
    )
    grad_value = jnp.einsum(
        "ts,td->sd", probs.astype(jnp.bfloat16), grad_head, preferred_element_type=jnp.float32
    )
    return (grad_query, grad_key, grad_value)


def per_device(
    tokens,
    lengths,
    qkv_weight,
    out_weight,
    up_weight,
    down_weight,
    norm_gain,
    norm_shift,
    cotangent,
):
    layers = qkv_weight.shape[0]
    count = tokens.shape[1]
    slots = count * lax.axis_size("seq")
    first_slot = lax.axis_index("seq") * count
    length = lengths[0]
    key_ok = jnp.arange(slots, dtype=jnp.int32) < length
    row_ok = first_slot + jnp.arange(count, dtype=jnp.int32) < length
    scaling = HEAD ** (-0.5)
    part = D // GROUPS
    part_ff = FF // GROUPS
    hidden_low = tokens[0]
    saved = []
    for layer_index in range(layers):
        gathered = (
            lax.all_gather(qkv_weight[layer_index], ("dp", "seq"), axis=0, tiled=True),
            lax.all_gather(out_weight[layer_index], ("dp", "seq"), axis=0, tiled=True),
            lax.all_gather(up_weight[layer_index], ("dp", "seq"), axis=0, tiled=True),
            lax.all_gather(down_weight[layer_index], ("dp", "seq"), axis=0, tiled=True),
            lax.all_gather(norm_gain[layer_index], ("dp", "seq"), axis=0, tiled=True),
            lax.all_gather(norm_shift[layer_index], ("dp", "seq"), axis=0, tiled=True),
        )
        project, out_matrix, up_matrix, down_matrix, gains, shifts = unpack(gathered)
        heads = project_heads(hidden_low, project)
        key_all, value_all = (
            lax.all_gather(heads[1], "seq", axis=1, tiled=True),
            lax.all_gather(heads[2], "seq", axis=1, tiled=True),
        )
        attended, log_total = lax.map(
            partial(head_forward, key_ok, scaling), (heads[0], key_all, value_all)
        )
        attended_low = attended.transpose(1, 0, 2).reshape(count, D).astype(jnp.bfloat16)
        branch = jnp.dot(attended_low, out_matrix, preferred_element_type=jnp.float32)
        middle, scaled_one, factor_one = normalize(
            hidden_low.astype(jnp.float32) + branch, gains[0], shifts[0]
        )
        middle_low = middle.astype(jnp.bfloat16)
        expanded = grouped(middle_low, up_matrix)
        activated = jax.nn.gelu(expanded, approximate=False).astype(jnp.bfloat16)
        shrunk = grouped(activated, down_matrix)
        output, scaled_two, factor_two = normalize(
            middle_low.astype(jnp.float32) + shrunk, gains[1], shifts[1]
        )
        kept = None
        saved.append(
            (
                hidden_low,
                heads,
                log_total,
                attended_low,
                middle_low,
                expanded,
                activated,
                scaled_one,
                factor_one,
                scaled_two,
                factor_two,
                kept,
            )
        )
        hidden_low = output.astype(jnp.bfloat16)
    mixed = hidden_low[None]
    grad_hidden = cotangent[0].astype(jnp.float32) * row_ok[:, None].astype(jnp.float32)
    owned_list = []
    for layer_index in reversed(range(layers)):
        (
            inputs_low,
            heads,
            log_total,
            attended_low,
            middle_low,
            expanded,
            activated,
            scaled_one,
            factor_one,
            scaled_two,
            factor_two,
            kept,
        ) = saved[layer_index]
        gathered = (
            lax.all_gather(qkv_weight[layer_index], ("dp", "seq"), axis=0, tiled=True),
            lax.all_gather(out_weight[layer_index], ("dp", "seq"), axis=0, tiled=True),
            lax.all_gather(up_weight[layer_index], ("dp", "seq"), axis=0, tiled=True),
            lax.all_gather(down_weight[layer_index], ("dp", "seq"), axis=0, tiled=True),
            lax.all_gather(norm_gain[layer_index], ("dp", "seq"), axis=0, tiled=True),
            lax.all_gather(norm_shift[layer_index], ("dp", "seq"), axis=0, tiled=True),
        )
        project, out_matrix, up_matrix, down_matrix, gains, shifts = unpack(gathered)
        key_all, value_all = (
            lax.all_gather(heads[1], "seq", axis=1, tiled=True),
            lax.all_gather(heads[2], "seq", axis=1, tiled=True),
        )
        grad_two, gain_two, shift_two = normalize_back(
            grad_hidden, scaled_two, factor_two, gains[1]
        )
        shrunk_grad = grad_two.astype(jnp.bfloat16).reshape(count, GROUPS, part)
        down_terms = jnp.einsum(
            "tgf,tgo->gfo",
            activated.reshape(count, GROUPS, part_ff),
            shrunk_grad,
            preferred_element_type=jnp.float32,
        )
        active_grad = jnp.einsum(
            "tgo,gfo->tgf", shrunk_grad, down_matrix, preferred_element_type=jnp.float32
        ).reshape(count, FF)
        unused_value, gelu_pull = jax.vjp(partial(jax.nn.gelu, approximate=False), expanded)
        expanded_grad = (
            gelu_pull(active_grad)[0].astype(jnp.bfloat16).reshape(count, GROUPS, part_ff)
        )
        up_terms = jnp.einsum(
            "tgi,tgf->gif",
            middle_low.reshape(count, GROUPS, part),
            expanded_grad,
            preferred_element_type=jnp.float32,
        )
        middle_grad = grad_two + jnp.einsum(
            "tgf,gif->tgi", expanded_grad, up_matrix, preferred_element_type=jnp.float32
        ).reshape(count, D)
        grad_one, gain_one, shift_one = normalize_back(
            middle_grad, scaled_one, factor_one, gains[0]
        )
        branch_grad = grad_one.astype(jnp.bfloat16)
        out_terms = jnp.einsum(
            "ti,to->io", attended_low, branch_grad, preferred_element_type=jnp.float32
        )
        attended_grad = jnp.einsum(
            "to,io->ti", branch_grad, out_matrix, preferred_element_type=jnp.float32
        ).astype(jnp.bfloat16)
        grad_heads = attended_grad.reshape(count, HEADS, HEAD).transpose(1, 0, 2)
        grad_query, key_terms, value_terms = lax.map(
            partial(head_backward, key_ok, scaling),
            (heads[0], key_all, value_all, grad_heads, log_total),
        )
        grad_key, grad_value = (
            lax.psum_scatter(
                key_terms.astype(jnp.bfloat16), "seq", scatter_dimension=1, tiled=True
            ).astype(jnp.float32),
            lax.psum_scatter(
                value_terms.astype(jnp.bfloat16), "seq", scatter_dimension=1, tiled=True
            ).astype(jnp.float32),
        )
        grad_projected = jnp.stack((grad_query, grad_key, grad_value)).astype(jnp.bfloat16)
        grad_projected = grad_projected.transpose(0, 2, 1, 3).reshape(3, count, GROUPS, part)
        qkv_terms = jnp.einsum(
            "tgi,ctgo->cgio",
            inputs_low.reshape(count, GROUPS, part),
            grad_projected,
            preferred_element_type=jnp.float32,
        )
        grad_hidden = grad_one + jnp.einsum(
            "ctgo,cgio->tgi", grad_projected, project, preferred_element_type=jnp.float32
        ).reshape(count, D)
        owned = (
            lax.psum_scatter(qkv_terms.reshape(-1), ("dp", "seq"), scatter_dimension=0, tiled=True),
            lax.psum_scatter(out_terms.reshape(-1), ("dp", "seq"), scatter_dimension=0, tiled=True),
            lax.psum_scatter(up_terms.reshape(-1), ("dp", "seq"), scatter_dimension=0, tiled=True),
            lax.psum_scatter(
                down_terms.reshape(-1), ("dp", "seq"), scatter_dimension=0, tiled=True
            ),
            lax.psum_scatter(
                jnp.stack((gain_one, gain_two)).reshape(-1),
                ("dp", "seq"),
                scatter_dimension=0,
                tiled=True,
            ),
            lax.psum_scatter(
                jnp.stack((shift_one, shift_two)).reshape(-1),
                ("dp", "seq"),
                scatter_dimension=0,
                tiled=True,
            ),
        )
        owned_list.insert(0, owned)
    tokens_grad = grad_hidden.astype(jnp.bfloat16)[None]
    stacked = tuple((jnp.stack([entry[member] for entry in owned_list]) for member in range(6)))
    return (
        mixed,
        tokens_grad,
        stacked[0],
        stacked[1],
        stacked[2],
        stacked[3],
        stacked[4],
        stacked[5],
    )


F32 = jnp.float32
BF16 = jnp.bfloat16
PART = D // GROUPS
PART_FF = FF // GROUPS
LAYERS = 2
ROWS = 128
HALF = 4 * ROWS
FULL = 2 * HALF
NDEV = 32
UNIT = PART // 8
FLAT = UNIT * PART_FF // 128
HEADS_HERE = HEADS // GROUPS
KEY_BLOCK = 256
FF_BLOCK = 128
SEMS = 512
MESH = pl.DeviceIdType.MESH

SCRATCH = dict(
    x_all=((LAYERS, PART, FULL), BF16),
    cot_t=((PART, HALF), BF16),
    tok_t=((D, ROWS), BF16),
    cotown_t=((D, ROWS), BF16),
    ln_in=((8, 128), F32),
    gn_in=((2, PART, 128), BF16),
    misc=((128, 128), BF16),
    ln_out=((8, 128), F32),
    wq_out=((LAYERS, 3, 2 * UNIT, 128), BF16),
    wc_out=((LAYERS, GROUPS, 2 * UNIT, 128), BF16),
    wr_out=((LAYERS, FLAT, 128), BF16),
    wm_out=((LAYERS, 2, FLAT, 128), BF16),
    wq_in=((LAYERS, 3, 8, 2 * UNIT, 128), BF16),
    wc_in=((LAYERS, GROUPS, 8, 2 * UNIT, 128), BF16),
    wr_in=((LAYERS, 8, FLAT, 128), BF16),
    wm_in=((LAYERS, 8, 2, FLAT, 128), BF16),
    raw=((8 * FLAT, 128), F32),
    left=((PART_FF, 128), F32),
    right=((PART_FF, 128), F32),
    wn_q=((LAYERS, 3, PART, PART), BF16),
    wn_r=((LAYERS, PART, D), BF16),
    wn_u=((LAYERS, PART, PART_FF), BF16),
    wn_d=((LAYERS, PART_FF, PART), BF16),
    wt_u=((PART_FF, PART), BF16),
    bias=((FULL, 128), F32),
    q_t=((LAYERS, PART, HALF), BF16),
    k_t=((LAYERS, PART, FULL), BF16),
    v_t=((LAYERS, PART, FULL), BF16),
    k_n=((LAYERS, HEADS_HERE, FULL, HEAD), BF16),
    v_n=((LAYERS, HEADS_HERE, FULL, HEAD), BF16),
    p_t=((LAYERS, HEADS_HERE, FULL, HALF), BF16),
    rinv=((LAYERS, HEADS_HERE, 8, HALF), F32),
    s_scr=((FULL, HALF), F32),
    ds_scr=((FULL, HALF), BF16),
    o_t=((LAYERS, PART, HALF), F32),
    att_all=((LAYERS, D, HALF), BF16),
    bg_all=((LAYERS, D, HALF), BF16),
    xh1=((LAYERS, PART, HALF), F32),
    xh2=((LAYERS, PART, HALF), F32),
    r1=((LAYERS, 8, HALF), F32),
    r2=((LAYERS, 8, HALF), F32),
    mid=((LAYERS, PART, HALF), BF16),
    act=((LAYERS, PART_FF, HALF), BF16),
    dgl=((LAYERS, PART_FF, HALF), F32),
    eg=((LAYERS, PART_FF, HALF), BF16),
    sgb=((LAYERS, PART, HALF), BF16),
    fg=((PART, HALF), F32),
    do_t=((PART, HALF), BF16),
    dq_t=((PART, HALF), BF16),
    dk_t=((PART, FULL), BF16),
    dv_t=((PART, FULL), BF16),
    dx_out=((LAYERS, PART, HALF), F32),
    dx_in=((LAYERS, PART, HALF), F32),
    stats=((4 * LAYERS, 4, 8, HALF), F32),
    mix_out=((PART, HALF), BF16),
    mix_in=((D, ROWS), BF16),
    tg_out=((PART, HALF), BF16),
    tg_in=((D, ROWS), BF16),
    gs_acc=((2, PART, 128), F32),
    gs_out=((2, 4, 8, 128), F32),
    gs_in=((8, 8, 128), F32),
    gb_d=((LAYERS, 8, FLAT, 128), BF16),
    gb_u=((LAYERS, 8, FLAT, 128), BF16),
    gb_o=((LAYERS, 8, FLAT, 128), BF16),
    gb_q=((LAYERS, 8, 3, 2 * UNIT, 128), BF16),
    sb_d=((LAYERS, 4, FLAT, 128), BF16),
    sb_u=((LAYERS, 4, FLAT, 128), BF16),
    sb_o=((LAYERS, 4, FLAT, 128), BF16),
    sb_q=((LAYERS, 4, 3, 2 * UNIT, 128), BF16),
    gm_d=((LAYERS, 4, FLAT, 128), BF16),
    gm_u=((LAYERS, 4, FLAT, 128), BF16),
    gm_o=((LAYERS, 4, FLAT, 128), BF16),
    gm_q=((LAYERS, 4, 3, 2 * UNIT, 128), BF16),
    rg_d=((LAYERS, 4, FLAT, 128), BF16),
    rg_u=((LAYERS, 4, FLAT, 128), BF16),
    rg_o=((LAYERS, 4, FLAT, 128), BF16),
    rg_q=((LAYERS, 4, 3, 2 * UNIT, 128), BF16),
)


def mm(a, b):
    return jnp.dot(a, b, preferred_element_type=F32)


def mm_nt(a, b):
    return lax.dot_general(a, b, (((1,), (1,)), ((), ())), preferred_element_type=F32)


def turn(v):
    return pltpu.roll(v, 64, axis=1)


def low_lanes(a, b):
    return jnp.where(lax.broadcasted_iota(jnp.int32, a.shape, 1) < 64, a, b)


def every(start, count, step):
    return pl.ds(start, count, stride=step)


def rows_from_triples(first, second, third, left, right):
    count = first.shape[0]
    second_turned, third_turned = turn(second), turn(third)
    left[every(0, count, 2), :] = first
    left[every(1, count, 2), :] = low_lanes(second_turned, third_turned)
    right[every(0, count, 2), :] = second
    right[every(1, count, 2), :] = third_turned


def triples_from_rows(count, left, right):
    turned = turn(left[every(1, count, 2), :])
    first = left[every(0, count, 2), :]
    second = low_lanes(right[every(0, count, 2), :], turned)
    third = low_lanes(turned, turn(right[every(1, count, 2), :]))
    return first, second, third


def matrix_of(units):
    count = units.shape[0]
    wide = units.astype(F32)
    left = wide[:, :UNIT].reshape(UNIT * count, 128)
    right = wide[:, UNIT:].reshape(UNIT * count, 128)
    return jnp.concatenate([left, right[:, :64]], axis=1).astype(BF16)


def units_of(matrix):
    count = matrix.shape[0] // UNIT
    left = matrix[:, :128].reshape(count, UNIT, 128)
    right = jnp.concatenate([matrix[:, 128:], matrix[:, :64]], axis=1).reshape(count, UNIT, 128)
    return jnp.concatenate([left, right], axis=1).astype(BF16)


def erf_pair(v):
    cdf = 0.5 * (1.0 + lax.erf(v * (0.5**0.5)))
    slope = cdf + v * (jnp.exp(-0.5 * v * v) * 0.3989422804014327)
    return cdf, slope


def fast_kernel(
    tokens, cotangent, length, gains, shifts, w_qkv, w_out, w_up, w_down,
    mixed, tokens_grad, g_qkv, g_out, g_up, g_down, g_norm,
    sems, *scratch,
):
    b = types.SimpleNamespace(**dict(zip(SCRATCH, scratch)))
    p, s = lax.axis_index("dp"), lax.axis_index("seq")
    x, c, z, y = p // 2, p % 2, s // 2, s % 2
    g = 2 * x + y
    seq_here = jnp.where(z == 3, 3, (z + 2) % 3)
    z_mine = jnp.where(p == 3, 3, (p + 1) % 3)
    own = pl.multiple_of(HALF * c, HALF)
    other = pl.multiple_of(HALF * (1 - c), HALF)
    g_rows = pl.multiple_of(PART * g, PART)
    used = [0]
    pending = []

    def new_sems(count=1):
        first = used[0]
        used[0] += count
        assert used[0] <= SEMS
        return first

    def dev(dx, dc, dz, dy):
        return (2 * dx + dc, 2 * dz + dy)

    sibling = dev(x, 1 - c, z, y)
    square = (dev(x, c, z, 1 - y), dev(1 - x, c, z, y), dev(1 - x, c, z, 1 - y))

    def send(src, dst, to, arrive, maybe_here=False):
        copy = pltpu.make_async_remote_copy(
            src, dst, sems.at[new_sems()], sems.at[arrive], device_id=to, device_id_type=MESH
        )
        if not maybe_here:
            copy.start()
            pending.append((copy, None))
            return
        away = jnp.logical_or(to[0] != p, to[1] != s)

        @pl.when(away)
        def _():
            copy.start()

        @pl.when(jnp.logical_not(away))
        def _():
            pltpu.make_async_copy(src, dst, sems.at[arrive]).start()

        pending.append((copy, away))

    def arrived(ref, arrive):
        pltpu.make_async_copy(ref, ref, sems.at[arrive]).wait()

    me = 8 * p + s
    barrier = pltpu.get_barrier_semaphore()

    def greet(i, carry):
        d = (me + i) % NDEV
        pl.semaphore_signal(barrier, inc=1, device_id=(d // 8, d % 8), device_id_type=MESH)
        return carry

    lax.fori_loop(1, NDEV, greet, 0)
    b.tok_t[...] = tokens[...].T
    b.cotown_t[...] = cotangent[...].T
    b.gs_acc[...] = jnp.zeros((2, PART, 128), F32)
    b.ln_out[...] = jnp.full((8, 128), length[0].astype(F32), F32)
    norm_rows = [ref[...].astype(F32)[l : l + 1] for l in range(LAYERS) for ref in (gains, shifts)]
    norm_rows = jnp.concatenate(norm_rows + [jnp.zeros((4, 48), F32)], axis=0)
    norm_rows = jnp.concatenate([norm_rows, jnp.zeros((8, 80), F32)], axis=1)
    norm_rows = jnp.concatenate([norm_rows, jnp.zeros((120, 128), F32)], axis=0)
    b.misc[...] = norm_rows.T.astype(BF16)
    b.raw[0:216] = w_qkv[...].astype(F32)
    for l in range(LAYERS):
        rows_from_triples(*(b.raw[every(l + 2 * i, 36, 6), :] for i in range(3)), b.left, b.right)
        for k in range(3):
            rows = slice(UNIT * k, UNIT * (k + 1))
            b.wq_out[l, k] = jnp.concatenate([b.left[rows], b.right[rows]], axis=0).astype(BF16)
    pl.semaphore_wait(barrier, NDEV - 1)

    tok_sem, len_sem, cot_sem, gn_sem = (new_sems() for _ in range(4))
    half_of = s // 4
    for gg in range(4):
        to = dev(gg // 2, half_of, z_mine, gg % 2)
        lane = pl.multiple_of(ROWS * s, ROWS)
        send(
            b.tok_t.at[pl.ds(PART * gg, PART), :],
            b.x_all.at[0, :, pl.ds(lane, ROWS)],
            to, tok_sem, True,
        )
    len_copies = []
    first_chunk = s % 4 == 0
    for gg in range(4):
        to = dev(gg // 2, half_of, z_mine, gg % 2)
        away = jnp.logical_or(to[0] != p, to[1] != s)
        copy = pltpu.make_async_remote_copy(
            b.ln_out, b.ln_in, sems.at[new_sems()], sems.at[len_sem], device_id=to, device_id_type=MESH
        )

        @pl.when(jnp.logical_and(first_chunk, away))
        def _():
            copy.start()

        @pl.when(jnp.logical_and(first_chunk, jnp.logical_not(away)))
        def _():
            pltpu.make_async_copy(b.ln_out, b.ln_in, sems.at[len_sem]).start()

        pending.append((copy, jnp.logical_and(first_chunk, away)))

    weights_in = dict(q=b.wq_in, r=b.wr_in, c=b.wc_in, m=b.wm_in)
    arrive_w = {(name, l): new_sems() for l in range(LAYERS) for name in "qrcm"}
    relay_w = {(name, l): new_sems() for l in range(LAYERS) for name in "qrcm"}

    def send_qkv(l):
        for k in range(3):
            u = 3 * me + k
            cc, gg, t = u // 32, (u % 32) // 8, u % 8
            for zz in range(4):
                send(
                    b.wq_out.at[l, k], b.wq_in.at[l, cc, t],
                    dev(gg // 2, t // 4, zz, gg % 2), arrive_w["q", l], True,
                )

    def send_columns(l):
        for cg in range(4):
            for zz in range(4):
                send(
                    b.wc_out.at[l, cg], b.wc_in.at[l, p, s],
                    dev(cg // 2, s // 4, zz, cg % 2), arrive_w["c", l], True,
                )

    def send_rows(l):
        for zz in range(4):
            send(b.wr_out.at[l], b.wr_in.at[l, s], dev(p // 2, s // 4, zz, p % 2), arrive_w["r", l], True)

    def send_updown(l):
        for zz in range(4):
            send(b.wm_out.at[l], b.wm_in.at[l, s], dev(p // 2, s // 4, zz, p % 2), arrive_w["m", l], True)

    def half(name, l, which):
        ref = weights_in[name]
        units = pl.ds(4 * which, 4)
        return ref.at[l, :, units] if name in "qc" else ref.at[l, units]

    def relay(name, l):
        mine = half(name, l, c)
        arrived(mine, arrive_w[name, l])
        send(mine, mine, sibling, relay_w[name, l])

    def relayed(name, l):
        arrived(half(name, l, 1 - c), relay_w[name, l])

    send_qkv(0)
    for zz in range(4):
        for cc in range(2):
            gg = 2 * (p % 2) + s // 4
            row = pl.multiple_of(48 * (s % 4), 16)
            send(
                b.misc.at[0:48, :], b.gn_in.at[p // 2, pl.ds(row, 48), :],
                dev(gg // 2, cc, zz, gg % 2), gn_sem, True,
            )
    b.raw[0:288] = w_out[...].astype(F32)
    for l in range(LAYERS):
        b.wr_out[l] = b.raw[every(l, FLAT, 2), :].astype(BF16)
        parts = [b.raw[every(2 * i + l, UNIT, 12), :] for i in range(6)]
        turned = [turn(part) for part in parts]
        pieces = (
            (parts[0], parts[1]),
            (low_lanes(turned[1], turned[2]), turned[2]),
            (parts[3], parts[4]),
            (low_lanes(turned[4], turned[5]), turned[5]),
        )
        for cg in range(4):
            b.wc_out[l, cg] = jnp.concatenate(pieces[cg], axis=0).astype(BF16)
    for i, ref in enumerate((w_up, w_down)):
        b.raw[0:288] = ref[...].astype(F32)
        for l in range(LAYERS):
            b.wm_out[l, i] = b.raw[every(l, FLAT, 2), :].astype(BF16)

    x_sem = [new_sems() for _ in range(LAYERS)]
    x_half = b.x_all.at[0, :, pl.ds(own, HALF)]
    arrived(x_half, tok_sem)
    send(x_half, x_half, sibling, x_sem[0])
    relay("q", 0)
    send_columns(0)
    send_updown(0)
    arrived(b.ln_in, len_sem)
    valid = b.ln_in[0:1, 0:1]
    key_at = lax.broadcasted_iota(jnp.int32, (FULL, 128), 0).astype(F32)
    b.bias[...] = jnp.where(key_at < valid, 0.0, -1e30)
    arrived(b.gn_in, gn_sem)

    def gain_shift(l, k):
        columns = b.gn_in[k].astype(F32)
        return columns[:, 2 * l : 2 * l + 1], columns[:, 2 * l + 1 : 2 * l + 2]

    stat_used = [0]

    def exchange(*rows):
        i = stat_used[0]
        stat_used[0] += 1
        buffer = b.stats.at[i]
        buffer[0] = jnp.concatenate([*rows, jnp.zeros((8 - len(rows), HALF), F32)], axis=0)
        base = new_sems(3)
        for d in range(3):
            send(buffer.at[0], buffer.at[d + 1], square[d], base + d)

        def finish():
            for d in range(3):
                arrived(buffer.at[d + 1], base + d)
            return [[buffer[d, i : i + 1] for i in range(len(rows))] for d in range(4)]

        return finish

    def normalize_here(v, name, l, gain, shift, weighted=None):
        mean_here = jnp.sum(v, axis=0, keepdims=True) * (1.0 / PART)
        d = v - mean_here
        rows = [mean_here, jnp.sum(d * d, axis=0, keepdims=True)]
        if weighted is not None:
            rows += [jnp.sum(weighted, axis=0, keepdims=True), jnp.sum(weighted * d, axis=0, keepdims=True)]
        exchanged = exchange(*rows)
        return lambda: normalize_there(exchanged(), v, name, l, gain, shift, weighted)

    def normalize_there(four, v, name, l, gain, shift, weighted):
        mean = (four[0][0] + four[1][0] + four[2][0] + four[3][0]) * 0.25
        total = sum(f[1] + PART * (f[0] - mean) * (f[0] - mean) for f in four)
        factor = lax.rsqrt(total * (1.0 / D) + EPSILON)
        scaled = (v - mean) * factor
        getattr(b, "xh" + name)[l] = scaled
        getattr(b, "r" + name)[l, 0:1] = factor
        result = scaled * gain + shift
        if weighted is None:
            return result
        one = sum(f[2] for f in four) * (1.0 / D)
        two = sum(f[3] + (f[0] - mean) * f[2] for f in four) * factor * (1.0 / D)
        return result, one, two

    def wide_rows(units, into):
        b.raw[...] = units.astype(F32).reshape(8 * FLAT, 128)
        for i in range(6):
            into[:, 128 * i : 128 * (i + 1)] = b.raw[every(i, PART, 6), :].astype(BF16)

    def flat_units(matrix):
        for i in range(6):
            b.raw[every(i, PART, 6), :] = matrix[:, 128 * i : 128 * (i + 1)]
        return b.raw[...].astype(BF16).reshape(8, FLAT, 128)

    att_sem = [[new_sems(3) for _ in range(3)] for _ in range(LAYERS)]
    att_send = [[new_sems(3) for _ in range(3)] for _ in range(LAYERS)]

    def send_cotangent():
        for gg in range(4):
            lane = pl.multiple_of(ROWS * (s % 4), ROWS)
            send(
                b.cotown_t.at[pl.ds(PART * gg, PART), :], b.cot_t.at[:, pl.ds(lane, ROWS)],
                dev(gg // 2, half_of, z_mine, gg % 2), cot_sem, True,
            )

    def forward(l):
        x_own = b.x_all[l, :, pl.ds(own, HALF)]
        relayed("q", l)
        turned = []
        for cc in range(3):
            nat = matrix_of(b.wq_in[l, cc])
            b.wn_q[l, cc] = nat
            turned.append(nat.T)
        b.q_t[l] = mm(turned[0], x_own).astype(BF16) * jnp.asarray(0.125, BF16)

        def keys_values(start, part):
            for matrix, name in ((turned[1], "k"), (turned[2], "v")):
                value = mm(matrix, part).astype(BF16)
                getattr(b, name + "_t")[l, :, pl.ds(start, HALF)] = value
                for h in range(HEADS_HERE):
                    getattr(b, name + "_n")[l, h, pl.ds(start, HALF), :] = value[HEAD * h : HEAD * (h + 1)].T

        keys_values(own, x_own)
        arrived(b.x_all.at[l, :, pl.ds(other, HALF)], x_sem[l])
        keys_values(other, b.x_all[l, :, pl.ds(other, HALF)])

        def one_head(h, carry):
            head = pl.multiple_of(HEAD * h, HEAD)
            q = b.q_t[l, pl.ds(head, HEAD), :]
            largest = jnp.full((1, HALF), -jnp.inf, F32)
            for kb in range(0, FULL, KEY_BLOCK):
                scores = mm(b.k_n[l, h, kb : kb + KEY_BLOCK, :], q) + b.bias[kb : kb + KEY_BLOCK, 0:1]
                b.s_scr[kb : kb + KEY_BLOCK] = scores
                largest = jnp.maximum(largest, jnp.max(scores, axis=0, keepdims=True))
            total = jnp.zeros((1, HALF), F32)
            for kb in range(0, FULL, KEY_BLOCK):
                powers = jnp.exp(b.s_scr[kb : kb + KEY_BLOCK] - largest)
                total += jnp.sum(powers, axis=0, keepdims=True)
                b.p_t[l, h, kb : kb + KEY_BLOCK] = powers.astype(BF16)
            inverse = 1.0 / total
            b.rinv[l, h, 0:1] = inverse
            out = mm(b.v_t[l, pl.ds(head, HEAD), :], b.p_t[l, h]) * inverse
            b.o_t[l, pl.ds(head, HEAD), :] = out
            rows = pl.ds(pl.multiple_of(g_rows + head, HEAD), HEAD)
            b.att_all[l, rows, :] = out.astype(BF16)
            piece = b.att_all.at[l, rows, :]
            for d in range(3):
                pltpu.make_async_remote_copy(
                    piece, piece, sems.at[att_send[l][d] + h], sems.at[att_sem[l][d] + h],
                    device_id=square[d], device_id_type=MESH,
                ).start()
            return carry

        lax.fori_loop(0, HEADS_HERE, one_head, 0)
        relay("c", l)
        relayed("c", l)
        columns_t = matrix_of(b.wc_in[l].reshape(32, 2 * UNIT, 128)).T
        flips = ((0, 1), (1, 0), (1, 1))
        for h in range(HEADS_HERE):
            for d, (fx, fy) in enumerate(flips):
                px = 1 - x if fx else x
                py = 1 - y if fy else y
                start = pl.multiple_of(PART * (2 * px + py) + HEAD * h, HEAD)
                arrived(b.att_all.at[l, pl.ds(start, HEAD), :], att_sem[l][d] + h)
        relay("m", l)
        branch = mm(columns_t, b.att_all[l])
        gain, shift = gain_shift(l, 0)
        finish = normalize_here(x_own.astype(F32) + branch, "1", l, gain, shift)
        relayed("m", l)
        wide_rows(b.wm_in[l, :, 0], b.wn_u.at[l])
        b.wt_u[...] = b.wn_u[l].T
        b.raw[...] = b.wm_in[l, :, 1].astype(F32).reshape(8 * FLAT, 128)
        rows_from_triples(*(b.raw[every(i, PART_FF // 2, 3), :] for i in range(3)), b.left, b.right)
        nat = jnp.concatenate([b.left[...], b.right[:, 0:64]], axis=1).astype(BF16)
        b.wn_d[l] = nat
        down_t = nat.T
        middle = finish().astype(BF16)
        if l == 0:
            send_qkv(1)
            send_cotangent()
        b.mid[l] = middle

        def one_block(i, carry):
            rows = pl.ds(pl.multiple_of(FF_BLOCK * i, FF_BLOCK), FF_BLOCK)
            expanded = mm(b.wt_u[rows, :], b.mid[l])
            cdf, slope = erf_pair(expanded)
            b.act[l, rows, :] = (expanded * cdf).astype(BF16)
            b.dgl[l, rows, :] = slope
            return carry

        lax.fori_loop(0, PART_FF // FF_BLOCK, one_block, 0)
        second = middle.astype(F32) + mm(down_t, b.act[l])
        gain, shift = gain_shift(l, 1)
        if l + 1 < LAYERS:
            return normalize_here(second, "2", l, gain, shift)()
        arrived(b.cot_t, cot_sem)
        position = lax.broadcasted_iota(jnp.int32, (PART, HALF), 1) + HALF * c
        grad = jnp.where(position.astype(F32) < valid, b.cot_t[...].astype(F32), 0.0)
        return normalize_here(second, "2", l, gain, shift, grad * gain)(), grad

    hidden = forward(0)
    b.x_all[1, :, pl.ds(own, HALF)] = hidden.astype(BF16)
    x_half = b.x_all.at[1, :, pl.ds(own, HALF)]
    send(x_half, x_half, sibling, x_sem[1])
    relay("q", 1)
    send_columns(1)
    send_updown(1)
    send_rows(1)
    send_rows(0)
    (hidden, one, two), grad = forward(1)

    mix_sem, tg_sem = new_sems(), new_sems()

    def send_back(value, out_ref, in_ref, arrive):
        out_ref[...] = value.astype(BF16)
        for k in range(4):
            send(
                out_ref.at[:, ROWS * k : ROWS * (k + 1)], in_ref.at[pl.ds(g_rows, PART), :],
                (seq_here, 4 * c + k), arrive, True,
            )

    send_back(hidden, b.mix_out, b.mix_in, mix_sem)

    half_sem = {(name, l): new_sems() for l in range(LAYERS) for name in "duoq"}
    owner_sem = {(name, l): new_sems() for l in range(LAYERS) for name in "duoq"}

    def to_sibling(name, l):
        send(
            getattr(b, "gb_" + name).at[l, pl.ds(4 * (1 - c), 4)], getattr(b, "sb_" + name).at[l], sibling, half_sem[name, l]
        )

    def to_owners(name, l):
        arrived(getattr(b, "sb_" + name).at[l], half_sem[name, l])
        mine = getattr(b, "gb_" + name)[l, pl.ds(4 * c, 4)].astype(F32) + getattr(b, "sb_" + name)[l].astype(F32)
        getattr(b, "gm_" + name)[l] = mine.astype(BF16)
        for k in range(4):
            t = 4 * c + k
            if name != "q":
                send(getattr(b, "gm_" + name).at[l, k], getattr(b, "rg_" + name).at[l, z], (g, t), owner_sem[name, l], True)
                continue
            for cc in range(3):
                u = 32 * cc + 8 * g + t
                j = u // 3
                send(
                    b.gm_q.at[l, k, cc], b.rg_q.at[l, z, u % 3], (j // 8, j % 8), owner_sem["q", l], True
                )

    lane_at = lax.broadcasted_iota(jnp.int32, (PART, 128), 1)

    def norm_grads(grad, scaled, l, k):
        gain_grad = jnp.sum(grad * scaled, axis=1, keepdims=True)
        shift_grad = jnp.sum(grad, axis=1, keepdims=True)
        b.gs_acc[k] += jnp.where(lane_at == 2 * l, gain_grad, 0.0) + jnp.where(
            lane_at == 2 * l + 1, shift_grad, 0.0
        )

    def normalize_back_here(grad, name, l, k, known=None):
        gain, _ = gain_shift(l, k)
        scaled = getattr(b, "xh" + name)[l]
        weighted = grad * gain
        if known is None:
            finish = exchange(
                jnp.sum(weighted, axis=0, keepdims=True), jnp.sum(weighted * scaled, axis=0, keepdims=True)
            )
            norm_grads(grad, scaled, l, k)
            four = finish()
            one, two = (sum(f[i] for f in four) * (1.0 / D) for i in range(2))
        else:
            one, two = known
        return getattr(b, "r" + name)[l, 0:1] * (weighted - one - scaled * two)

    gs_sem = new_sems()

    def send_norm_grads():
        for k in range(2):
            turned = b.gs_acc[k].T[0:8]
            for q in range(4):
                b.gs_out[k, q] = jnp.concatenate([turned[:, 48 * q : 48 * (q + 1)], jnp.zeros((8, 80), F32)], axis=1)
                send(
                    b.gs_out.at[k, q], b.gs_in.at[2 * z + c], (2 * k + g // 2, 4 * (g % 2) + q), gs_sem, True
                )

    bg_sem = [new_sems(3) for _ in range(LAYERS)]
    dx_sem = [new_sems() for _ in range(LAYERS)]

    def backward(l, grad, known=None):
        relay("r", l)
        second_grad = normalize_back_here(grad, "2", l, 1, known)
        b.sgb[l] = second_grad.astype(BF16)
        if l + 1 < LAYERS:
            to_owners("q", l + 1)

        def one_block(i, carry):
            rows = pl.ds(pl.multiple_of(FF_BLOCK * i, FF_BLOCK), FF_BLOCK)
            active_grad = mm(b.wn_d[l, rows, :], b.sgb[l])
            b.eg[l, rows, :] = (active_grad * b.dgl[l, rows, :]).astype(BF16)
            return carry

        lax.fori_loop(0, PART_FF // FF_BLOCK, one_block, 0)
        middle_grad = second_grad + mm(b.wn_u[l], b.eg[l])
        first_grad = normalize_back_here(middle_grad, "1", l, 0)
        b.fg[...] = first_grad
        b.bg_all[l, pl.ds(g_rows, PART), :] = first_grad.astype(BF16)
        piece = b.bg_all.at[l, pl.ds(g_rows, PART), :]
        for d in range(3):
            send(piece, piece, square[d], bg_sem[l] + d)
        if known is not None:
            norm_grads(grad, b.xh2[l], l, 1)
        if l == 0:
            send_norm_grads()
        grads = mm_nt(b.act[l], b.sgb[l])
        b.left[...] = grads[:, :128]
        b.right[:, 0:64] = grads[:, 128:]
        for i, part in enumerate(triples_from_rows(PART_FF // 2, b.left, b.right)):
            b.raw[every(i, PART_FF // 2, 3), :] = part
        b.gb_d[l] = b.raw[...].astype(BF16).reshape(8, FLAT, 128)
        to_sibling("d", l)
        b.gb_u[l] = flat_units(mm_nt(b.mid[l], b.eg[l]))
        to_sibling("u", l)
        relayed("r", l)
        wide_rows(b.wr_in[l], b.wn_r.at[l])
        for d, (fx, fy) in enumerate(((0, 1), (1, 0), (1, 1))):
            px = 1 - x if fx else x
            py = 1 - y if fy else y
            start = pl.multiple_of(PART * (2 * px + py), PART)
            arrived(b.bg_all.at[l, pl.ds(start, PART), :], bg_sem[l] + d)
        att = b.att_all[l, pl.ds(g_rows, PART), :]
        b.gb_o[l] = flat_units(mm_nt(att, b.bg_all[l]))
        to_sibling("o", l)
        b.do_t[...] = mm(b.wn_r[l], b.bg_all[l]).astype(BF16)
        to_owners("d", l)
        to_owners("u", l)
        to_owners("o", l)

        def one_head(h, carry):
            head = pl.multiple_of(HEAD * h, HEAD)
            rows = pl.ds(head, HEAD)
            inverse = b.rinv[l, h, 0:1]
            grad_out = b.do_t[rows, :].astype(F32)
            delta = jnp.sum(grad_out * b.o_t[l, rows, :], axis=0, keepdims=True) * inverse
            grad_scaled = (grad_out * inverse).astype(BF16)
            for kb in range(0, FULL, KEY_BLOCK):
                block = slice(kb, kb + KEY_BLOCK)
                grad_probs = mm(b.v_n[l, h, block, :], grad_scaled)
                b.ds_scr[block] = (b.p_t[l, h, block].astype(F32) * (grad_probs - delta)).astype(BF16)
            b.dq_t[rows, :] = (mm(b.k_t[l, rows, :], b.ds_scr[...]) * 0.125).astype(BF16)
            b.dk_t[rows, :] = mm_nt(b.q_t[l, rows, :], b.ds_scr[...]).astype(BF16)
            b.dv_t[rows, :] = mm_nt(grad_scaled, b.p_t[l, h]).astype(BF16)
            return carry

        lax.fori_loop(0, HEADS_HERE, one_head, 0)
        w_q, w_k, w_v = (b.wn_q[l, cc] for cc in range(3))
        b.dx_out[l] = mm(w_k, b.dk_t[:, pl.ds(other, HALF)]) + mm(w_v, b.dv_t[:, pl.ds(other, HALF)])
        send(b.dx_out.at[l], b.dx_in.at[l], sibling, dx_sem[l])
        x_own = b.x_all[l, :, pl.ds(own, HALF)]
        b.gb_q[l, :, 0] = units_of(mm_nt(x_own, b.dq_t[...]))
        b.gb_q[l, :, 1] = units_of(mm_nt(b.x_all[l], b.dk_t[...]))
        b.gb_q[l, :, 2] = units_of(mm_nt(b.x_all[l], b.dv_t[...]))
        to_sibling("q", l)
        here = mm(w_q, b.dq_t[...])
        here += mm(w_k, b.dk_t[:, pl.ds(own, HALF)]) + mm(w_v, b.dv_t[:, pl.ds(own, HALF)])
        arrived(b.dx_in.at[l], dx_sem[l])
        return b.fg[...] + here + b.dx_in[l]

    grad = backward(1, grad, (one, two))
    grad = backward(0, grad)
    send_back(grad, b.tg_out, b.tg_in, tg_sem)
    to_owners("q", 0)

    arrived(b.mix_in, mix_sem)
    mixed[...] = b.mix_in[...].T
    for l in reversed(range(LAYERS)):
        for name, out in (("d", g_down), ("u", g_up), ("o", g_out)):
            rg = getattr(b, "rg_" + name)
            arrived(rg.at[l], owner_sem[name, l])
            out[every(l, FLAT, 2), :] = sum(rg[l, i].astype(F32) for i in range(4))
        arrived(b.rg_q.at[l], owner_sem["q", l])
        total = sum(b.rg_q[l, i].astype(F32) for i in range(4))
        b.left[0:72] = total[:, :UNIT].reshape(72, 128)
        b.right[0:72] = total[:, UNIT:].reshape(72, 128)
        for i, part in enumerate(triples_from_rows(36, b.left, b.right)):
            g_qkv[every(l + 2 * i, 36, 6), :] = part
    arrived(b.tg_in, tg_sem)
    tokens_grad[...] = b.tg_in[...].T
    arrived(b.gs_in, gs_sem)
    g_norm[...] = sum(b.gs_in[i] for i in range(8))

    for copy, when in pending:
        if when is None:
            copy.wait_send()
        else:
            pl.when(when)(copy.wait_send)
    for l in range(LAYERS):
        for h in range(HEADS_HERE):
            for d in range(3):
                piece = b.att_all.at[l, pl.ds(pl.multiple_of(g_rows + HEAD * h, HEAD), HEAD), :]
                pltpu.make_async_remote_copy(
                    piece, piece, sems.at[att_send[l][d] + h], sems.at[att_sem[l][d] + h],
                    device_id=square[d], device_id_type=MESH,
                ).wait_send()


def fast_device(
    tokens, lengths, qkv_weight, out_weight, up_weight, down_weight, norm_gain, norm_shift, cotangent
):
    def raw(array):
        return array.reshape(LAYERS, -1, 128).transpose(1, 0, 2).reshape(-1, 128)

    def unraw(array):
        return array.reshape(-1, LAYERS, 128).transpose(1, 0, 2).reshape(LAYERS, -1)

    operands = (
        tokens[0],
        cotangent[0],
        lengths,
        norm_gain,
        norm_shift,
        raw(qkv_weight),
        raw(out_weight),
        raw(up_weight),
        raw(down_weight),
    )
    vmem = pl.BlockSpec(memory_space=pltpu.VMEM)
    shapes = (
        ((ROWS, D), BF16),
        ((ROWS, D), BF16),
        ((3 * LAYERS * 36, 128), F32),
        ((LAYERS * FLAT, 128), F32),
        ((LAYERS * FLAT, 128), F32),
        ((LAYERS * FLAT, 128), F32),
        ((8, 128), F32),
    )
    mixed, tokens_grad, g_qkv, g_out, g_up, g_down, g_norm = pl.pallas_call(
        fast_kernel,
        out_shape=tuple(jax.ShapeDtypeStruct(*shape) for shape in shapes),
        in_specs=[vmem] * 2 + [pl.BlockSpec(memory_space=pltpu.SMEM)] + [vmem] * 6,
        out_specs=tuple([vmem] * len(shapes)),
        scratch_shapes=[pltpu.SemaphoreType.DMA((SEMS,))] + [pltpu.VMEM(*entry) for entry in SCRATCH.values()],
        compiler_params=pltpu.CompilerParams(
            collective_id=0, has_side_effects=True, vmem_limit_bytes=60 * 2**20
        ),
        name="encoder",
    )(*operands)
    g_norm = g_norm[:4, :48]
    return (
        mixed[None],
        tokens_grad[None],
        unraw(g_qkv),
        unraw(g_out),
        unraw(g_up),
        unraw(g_down),
        g_norm[0::2],
        g_norm[1::2],
    )


def solution(mesh):
    small = (mesh.shape["dp"], mesh.shape["seq"]) == (4, 8)
    return jax.shard_map(
        fast_device if small else per_device,
        mesh=mesh,
        in_specs=(
            P("dp", "seq", None),
            P("dp"),
            P(None, ("dp", "seq")),
            P(None, ("dp", "seq")),
            P(None, ("dp", "seq")),
            P(None, ("dp", "seq")),
            P(None, ("dp", "seq")),
            P(None, ("dp", "seq")),
            P("dp", "seq", None),
        ),
        out_specs=(
            P("dp", "seq", None),
            P("dp", "seq", None),
            P(None, ("dp", "seq")),
            P(None, ("dp", "seq")),
            P(None, ("dp", "seq")),
            P(None, ("dp", "seq")),
            P(None, ("dp", "seq")),
            P(None, ("dp", "seq")),
        ),
        check_vma=False,
    )
```

```python
import types
from functools import partial

import jax
import jax.numpy as jnp
from jax import lax
from jax.experimental import pallas as pl
from jax.experimental.pallas import tpu as pltpu
from jax.sharding import PartitionSpec as P

D = 768
HEADS = 12
HEAD = 64
FF = 3072
GROUPS = 4


EPSILON = 1e-06


def grouped(inputs, weight):
    count = inputs.shape[0]
    shaped = inputs.reshape(count, weight.shape[0], -1)
    result = jnp.einsum("tgi,gio->tgo", shaped, weight, preferred_element_type=jnp.float32)
    return result.reshape(count, -1)


def normalize(values, gain, shift):
    center = values - jnp.mean(values, axis=-1, keepdims=True)
    factor = lax.rsqrt(jnp.mean(center * center, axis=-1, keepdims=True) + EPSILON)
    scaled = center * factor
    return (scaled * gain + shift, scaled, factor)


def normalize_back(grad_out, scaled, factor, gain):
    weighted = grad_out * gain
    grad_in = factor * (
        weighted
        - jnp.mean(weighted, axis=-1, keepdims=True)
        - scaled * jnp.mean(weighted * scaled, axis=-1, keepdims=True)
    )
    return (grad_in, jnp.sum(grad_out * scaled, axis=0), jnp.sum(grad_out, axis=0))


def unpack(pieces):
    qkv_flat, out_flat, up_flat, down_flat, gain_flat, shift_flat = pieces
    part = D // GROUPS
    part_ff = FF // GROUPS
    return (
        qkv_flat.reshape(3, GROUPS, part, part),
        out_flat.reshape(D, D),
        up_flat.reshape(GROUPS, part, part_ff),
        down_flat.reshape(GROUPS, part_ff, part),
        gain_flat.reshape(2, D).astype(jnp.float32),
        shift_flat.reshape(2, D).astype(jnp.float32),
    )


def project_heads(rows, matrices):
    total_rows = rows.shape[0]
    part = D // GROUPS
    result = jnp.einsum(
        "tgi,cgio->ctgo",
        rows.reshape(total_rows, GROUPS, part),
        matrices,
        preferred_element_type=jnp.float32,
    ).astype(jnp.bfloat16)
    return result.reshape(matrices.shape[0], total_rows, HEADS, HEAD).transpose(0, 2, 1, 3)


def head_forward(key_ok, scaling, pieces):
    query_head, key_head, value_head = pieces
    scores = (
        jnp.einsum("td,sd->ts", query_head, key_head, preferred_element_type=jnp.float32) * scaling
    )
    scores = jnp.where(key_ok[None, :], scores, -1e30)
    largest = jnp.max(scores, axis=-1, keepdims=True)
    powers = jnp.exp(scores - largest)
    total = jnp.sum(powers, axis=-1, keepdims=True)
    probs = (powers / total).astype(jnp.bfloat16)
    result = jnp.dot(probs, value_head, preferred_element_type=jnp.float32)
    return (result, (largest + jnp.log(total))[:, 0])


def head_backward(key_ok, scaling, pieces):
    query_head, key_head, value_head, grad_head, log_total = pieces
    scores = (
        jnp.einsum("td,sd->ts", query_head, key_head, preferred_element_type=jnp.float32) * scaling
    )
    scores = jnp.where(key_ok[None, :], scores, -1e30)
    probs = jnp.exp(scores - log_total[:, None])
    grad_probs = jnp.einsum("td,sd->ts", grad_head, value_head, preferred_element_type=jnp.float32)
    delta_row = jnp.sum(probs * grad_probs, axis=-1, keepdims=True)
    grad_scores = (probs * (grad_probs - delta_row)).astype(jnp.bfloat16)
    grad_query = jnp.dot(grad_scores, key_head, preferred_element_type=jnp.float32) * scaling
    grad_key = (
        jnp.einsum("ts,td->sd", grad_scores, query_head, preferred_element_type=jnp.float32)
        * scaling
    )
    grad_value = jnp.einsum(
        "ts,td->sd", probs.astype(jnp.bfloat16), grad_head, preferred_element_type=jnp.float32
    )
    return (grad_query, grad_key, grad_value)


def per_device(
    tokens,
    lengths,
    qkv_weight,
    out_weight,
    up_weight,
    down_weight,
    norm_gain,
    norm_shift,
    cotangent,
):
    layers = qkv_weight.shape[0]
    count = tokens.shape[1]
    slots = count * lax.axis_size("seq")
    first_slot = lax.axis_index("seq") * count
    length = lengths[0]
    key_ok = jnp.arange(slots, dtype=jnp.int32) < length
    row_ok = first_slot + jnp.arange(count, dtype=jnp.int32) < length
    scaling = HEAD ** (-0.5)
    part = D // GROUPS
    part_ff = FF // GROUPS
    hidden_low = tokens[0]
    saved = []
    for layer_index in range(layers):
        gathered = (
            lax.all_gather(qkv_weight[layer_index], ("dp", "seq"), axis=0, tiled=True),
            lax.all_gather(out_weight[layer_index], ("dp", "seq"), axis=0, tiled=True),
            lax.all_gather(up_weight[layer_index], ("dp", "seq"), axis=0, tiled=True),
            lax.all_gather(down_weight[layer_index], ("dp", "seq"), axis=0, tiled=True),
            lax.all_gather(norm_gain[layer_index], ("dp", "seq"), axis=0, tiled=True),
            lax.all_gather(norm_shift[layer_index], ("dp", "seq"), axis=0, tiled=True),
        )
        project, out_matrix, up_matrix, down_matrix, gains, shifts = unpack(gathered)
        heads = project_heads(hidden_low, project)
        key_all, value_all = (
            lax.all_gather(heads[1], "seq", axis=1, tiled=True),
            lax.all_gather(heads[2], "seq", axis=1, tiled=True),
        )
        attended, log_total = lax.map(
            partial(head_forward, key_ok, scaling), (heads[0], key_all, value_all)
        )
        attended_low = attended.transpose(1, 0, 2).reshape(count, D).astype(jnp.bfloat16)
        branch = jnp.dot(attended_low, out_matrix, preferred_element_type=jnp.float32)
        middle, scaled_one, factor_one = normalize(
            hidden_low.astype(jnp.float32) + branch, gains[0], shifts[0]
        )
        middle_low = middle.astype(jnp.bfloat16)
        expanded = grouped(middle_low, up_matrix)
        activated = jax.nn.gelu(expanded, approximate=False).astype(jnp.bfloat16)
        shrunk = grouped(activated, down_matrix)
        output, scaled_two, factor_two = normalize(
            middle_low.astype(jnp.float32) + shrunk, gains[1], shifts[1]
        )
        kept = None
        saved.append(
            (
                hidden_low,
                heads,
                log_total,
                attended_low,
                middle_low,
                expanded,
                activated,
                scaled_one,
                factor_one,
                scaled_two,
                factor_two,
                kept,
            )
        )
        hidden_low = output.astype(jnp.bfloat16)
    mixed = hidden_low[None]
    grad_hidden = cotangent[0].astype(jnp.float32) * row_ok[:, None].astype(jnp.float32)
    owned_list = []
    for layer_index in reversed(range(layers)):
        (
            inputs_low,
            heads,
            log_total,
            attended_low,
            middle_low,
            expanded,
            activated,
            scaled_one,
            factor_one,
            scaled_two,
            factor_two,
            kept,
        ) = saved[layer_index]
        gathered = (
            lax.all_gather(qkv_weight[layer_index], ("dp", "seq"), axis=0, tiled=True),
            lax.all_gather(out_weight[layer_index], ("dp", "seq"), axis=0, tiled=True),
            lax.all_gather(up_weight[layer_index], ("dp", "seq"), axis=0, tiled=True),
            lax.all_gather(down_weight[layer_index], ("dp", "seq"), axis=0, tiled=True),
            lax.all_gather(norm_gain[layer_index], ("dp", "seq"), axis=0, tiled=True),
            lax.all_gather(norm_shift[layer_index], ("dp", "seq"), axis=0, tiled=True),
        )
        project, out_matrix, up_matrix, down_matrix, gains, shifts = unpack(gathered)
        key_all, value_all = (
            lax.all_gather(heads[1], "seq", axis=1, tiled=True),
            lax.all_gather(heads[2], "seq", axis=1, tiled=True),
        )
        grad_two, gain_two, shift_two = normalize_back(
            grad_hidden, scaled_two, factor_two, gains[1]
        )
        shrunk_grad = grad_two.astype(jnp.bfloat16).reshape(count, GROUPS, part)
        down_terms = jnp.einsum(
            "tgf,tgo->gfo",
            activated.reshape(count, GROUPS, part_ff),
            shrunk_grad,
            preferred_element_type=jnp.float32,
        )
        active_grad = jnp.einsum(
            "tgo,gfo->tgf", shrunk_grad, down_matrix, preferred_element_type=jnp.float32
        ).reshape(count, FF)
        unused_value, gelu_pull = jax.vjp(partial(jax.nn.gelu, approximate=False), expanded)
        expanded_grad = (
            gelu_pull(active_grad)[0].astype(jnp.bfloat16).reshape(count, GROUPS, part_ff)
        )
        up_terms = jnp.einsum(
            "tgi,tgf->gif",
            middle_low.reshape(count, GROUPS, part),
            expanded_grad,
            preferred_element_type=jnp.float32,
        )
        middle_grad = grad_two + jnp.einsum(
            "tgf,gif->tgi", expanded_grad, up_matrix, preferred_element_type=jnp.float32
        ).reshape(count, D)
        grad_one, gain_one, shift_one = normalize_back(
            middle_grad, scaled_one, factor_one, gains[0]
        )
        branch_grad = grad_one.astype(jnp.bfloat16)
        out_terms = jnp.einsum(
            "ti,to->io", attended_low, branch_grad, preferred_element_type=jnp.float32
        )
        attended_grad = jnp.einsum(
            "to,io->ti", branch_grad, out_matrix, preferred_element_type=jnp.float32
        ).astype(jnp.bfloat16)
        grad_heads = attended_grad.reshape(count, HEADS, HEAD).transpose(1, 0, 2)
        grad_query, key_terms, value_terms = lax.map(
            partial(head_backward, key_ok, scaling),
            (heads[0], key_all, value_all, grad_heads, log_total),
        )
        grad_key, grad_value = (
            lax.psum_scatter(
                key_terms.astype(jnp.bfloat16), "seq", scatter_dimension=1, tiled=True
            ).astype(jnp.float32),
            lax.psum_scatter(
                value_terms.astype(jnp.bfloat16), "seq", scatter_dimension=1, tiled=True
            ).astype(jnp.float32),
        )
        grad_projected = jnp.stack((grad_query, grad_key, grad_value)).astype(jnp.bfloat16)
        grad_projected = grad_projected.transpose(0, 2, 1, 3).reshape(3, count, GROUPS, part)
        qkv_terms = jnp.einsum(
            "tgi,ctgo->cgio",
            inputs_low.reshape(count, GROUPS, part),
            grad_projected,
            preferred_element_type=jnp.float32,
        )
        grad_hidden = grad_one + jnp.einsum(
            "ctgo,cgio->tgi", grad_projected, project, preferred_element_type=jnp.float32
        ).reshape(count, D)
        owned = (
            lax.psum_scatter(qkv_terms.reshape(-1), ("dp", "seq"), scatter_dimension=0, tiled=True),
            lax.psum_scatter(out_terms.reshape(-1), ("dp", "seq"), scatter_dimension=0, tiled=True),
            lax.psum_scatter(up_terms.reshape(-1), ("dp", "seq"), scatter_dimension=0, tiled=True),
            lax.psum_scatter(
                down_terms.reshape(-1), ("dp", "seq"), scatter_dimension=0, tiled=True
            ),
            lax.psum_scatter(
                jnp.stack((gain_one, gain_two)).reshape(-1),
                ("dp", "seq"),
                scatter_dimension=0,
                tiled=True,
            ),
            lax.psum_scatter(
                jnp.stack((shift_one, shift_two)).reshape(-1),
                ("dp", "seq"),
                scatter_dimension=0,
                tiled=True,
            ),
        )
        owned_list.insert(0, owned)
    tokens_grad = grad_hidden.astype(jnp.bfloat16)[None]
    stacked = tuple((jnp.stack([entry[member] for entry in owned_list]) for member in range(6)))
    return (
        mixed,
        tokens_grad,
        stacked[0],
        stacked[1],
        stacked[2],
        stacked[3],
        stacked[4],
        stacked[5],
    )


F32 = jnp.float32
BF16 = jnp.bfloat16
PART = D // GROUPS
PART_FF = FF // GROUPS
LAYERS = 2
ROWS = 128
HALF = 4 * ROWS
FULL = 2 * HALF
NDEV = 32
UNIT = PART // 8
FLAT = UNIT * PART_FF // 128
COLS_AT = 2 * FLAT
ROWS_AT = COLS_AT + GROUPS * 2 * UNIT
SHARD = ROWS_AT + FLAT
HEADS_HERE = HEADS // GROUPS
KEY_BLOCK = 256
FF_BLOCK = 128
SEMS = 512
MESH = pl.DeviceIdType.MESH

SCRATCH = dict(
    x_all=((LAYERS, PART, FULL), BF16),
    cot_t=((PART, HALF), BF16),
    tok_t=((D, ROWS), BF16),
    cotown_t=((D, ROWS), BF16),
    ln_in=((8, 128), F32),
    gn_in=((2, PART, 128), BF16),
    misc=((128, 128), BF16),
    ln_out=((8, 128), F32),
    wq_out=((LAYERS, 3, 2 * UNIT, 128), BF16),
    wc_out=((LAYERS, GROUPS, 2 * UNIT, 128), BF16),
    wr_out=((LAYERS, FLAT, 128), BF16),
    wm_out=((LAYERS, 2 * FLAT, 128), BF16),
    wq_in=((LAYERS, 3, 8, 2 * UNIT, 128), BF16),
    w_in=((LAYERS, 2, 4, SHARD, 128), BF16),
    raw=((8 * FLAT, 128), F32),
    left=((PART_FF, 128), F32),
    right=((PART_FF, 128), F32),
    wn_q=((LAYERS, 3, PART, PART), BF16),
    wn_r=((LAYERS, PART, D), BF16),
    wn_u=((LAYERS, PART, PART_FF), BF16),
    wn_d=((LAYERS, PART_FF, PART), BF16),
    wt_u=((PART_FF, PART), BF16),
    bias=((FULL, 128), F32),
    q_t=((LAYERS, PART, HALF), BF16),
    k_t=((LAYERS, PART, FULL), BF16),
    v_t=((LAYERS, PART, FULL), BF16),
    k_n=((LAYERS, HEADS_HERE, FULL, HEAD), BF16),
    v_n=((LAYERS, HEADS_HERE, FULL, HEAD), BF16),
    p_t=((LAYERS, HEADS_HERE, FULL, HALF), BF16),
    rinv=((LAYERS, HEADS_HERE, 8, HALF), F32),
    s_scr=((FULL, HALF), F32),
    ds_scr=((FULL, HALF), BF16),
    o_t=((LAYERS, PART, HALF), F32),
    att_all=((LAYERS, D, HALF), BF16),
    bg_all=((LAYERS, D, HALF), BF16),
    xh1=((LAYERS, PART, HALF), F32),
    xh2=((LAYERS, PART, HALF), F32),
    r1=((LAYERS, 8, HALF), F32),
    r2=((LAYERS, 8, HALF), F32),
    mid=((LAYERS, PART, HALF), BF16),
    act=((LAYERS, PART_FF, HALF), BF16),
    dgl=((LAYERS, PART_FF, HALF), F32),
    eg=((LAYERS, PART_FF, HALF), BF16),
    sgb=((LAYERS, PART, HALF), BF16),
    fg=((PART, HALF), F32),
    do_t=((PART, HALF), BF16),
    dq_t=((PART, HALF), BF16),
    dk_t=((PART, FULL), BF16),
    dv_t=((PART, FULL), BF16),
    dx_out=((LAYERS, PART, HALF), F32),
    dx_in=((LAYERS, PART, HALF), F32),
    stats=((4 * LAYERS, 4, 16, 128), F32),
    mix_out=((PART, HALF), BF16),
    mix_in=((D, ROWS), BF16),
    tg_out=((PART, HALF), BF16),
    tg_in=((D, ROWS), BF16),
    gs_acc=((2, PART, 128), F32),
    gs_out=((2, 4, 8, 128), F32),
    gs_in=((8, 8, 128), F32),
    gb_m=((LAYERS, 2, 4, 2 * FLAT, 128), BF16),
    gb_o=((LAYERS, 2, 4, FLAT, 128), BF16),
    gb_q=((LAYERS, 8, 3, 2 * UNIT, 128), BF16),
    sb_m=((LAYERS, 4, 2 * FLAT, 128), BF16),
    sb_o=((LAYERS, 4, FLAT, 128), BF16),
    sb_q=((LAYERS, 4, 3, 2 * UNIT, 128), BF16),
    gm_m=((LAYERS, 4, 2 * FLAT, 128), BF16),
    gm_o=((LAYERS, 4, FLAT, 128), BF16),
    gm_q=((LAYERS, 4, 3, 2 * UNIT, 128), BF16),
    rz_m=((LAYERS, 4, 2 * FLAT, 128), BF16),
    rz_o=((LAYERS, 4, FLAT, 128), BF16),
    gf_m=((LAYERS, 2 * FLAT, 128), BF16),
    gf_o=((LAYERS, FLAT, 128), BF16),
    rg_m=((LAYERS, 2 * FLAT, 128), BF16),
    rg_o=((LAYERS, FLAT, 128), BF16),
    rg_q=((LAYERS, 4, 3, 2 * UNIT, 128), BF16),
)


def mm(a, b):
    return jnp.dot(a, b, preferred_element_type=F32)


def mm_nt(a, b):
    return lax.dot_general(a, b, (((1,), (1,)), ((), ())), preferred_element_type=F32)


def turn(v):
    return pltpu.roll(v, 64, axis=1)


def low_lanes(a, b):
    return jnp.where(lax.broadcasted_iota(jnp.int32, a.shape, 1) < 64, a, b)


def every(start, count, step):
    return pl.ds(start, count, stride=step)


def rows_from_triples(first, second, third, left, right):
    count = first.shape[0]
    second_turned, third_turned = turn(second), turn(third)
    left[every(0, count, 2), :] = first
    left[every(1, count, 2), :] = low_lanes(second_turned, third_turned)
    right[every(0, count, 2), :] = second
    right[every(1, count, 2), :] = third_turned


def triples_from_rows(count, left, right):
    turned = turn(left[every(1, count, 2), :])
    first = left[every(0, count, 2), :]
    second = low_lanes(right[every(0, count, 2), :], turned)
    third = low_lanes(turned, turn(right[every(1, count, 2), :]))
    return first, second, third


def matrix_of(units):
    count = units.shape[0]
    wide = units.astype(F32)
    left = wide[:, :UNIT].reshape(UNIT * count, 128)
    right = wide[:, UNIT:].reshape(UNIT * count, 128)
    return jnp.concatenate([left, right[:, :64]], axis=1).astype(BF16)


def units_of(matrix):
    count = matrix.shape[0] // UNIT
    left = matrix[:, :128].reshape(count, UNIT, 128)
    right = jnp.concatenate([matrix[:, 128:], matrix[:, :64]], axis=1).reshape(count, UNIT, 128)
    return jnp.concatenate([left, right], axis=1).astype(BF16)


def erf_pair(v):
    cdf = 0.5 * (1.0 + lax.erf(v * (0.5**0.5)))
    slope = cdf + v * (jnp.exp(-0.5 * v * v) * 0.3989422804014327)
    return cdf, slope


def fast_kernel(
    tokens, cotangent, length, gains, shifts, w_qkv, w_out, w_up, w_down,
    mixed, tokens_grad, g_qkv, g_out, g_up, g_down, g_norm,
    sems, *scratch,
):
    b = types.SimpleNamespace(**dict(zip(SCRATCH, scratch)))
    p, s = lax.axis_index("dp"), lax.axis_index("seq")
    x, c, z, y = p // 2, p % 2, s // 2, s % 2
    g = 2 * x + y
    seq_here = jnp.where(z == 3, 3, (z + 2) % 3)
    z_mine = jnp.where(p == 3, 3, (p + 1) % 3)
    own = pl.multiple_of(HALF * c, HALF)
    other = pl.multiple_of(HALF * (1 - c), HALF)
    g_rows = pl.multiple_of(PART * g, PART)
    used = [0]
    pending = []

    def new_sems(count=1):
        first = used[0]
        used[0] += count
        assert used[0] <= SEMS
        return first

    def dev(dx, dc, dz, dy):
        return (2 * dx + dc, 2 * dz + dy)

    sibling = dev(x, 1 - c, z, y)
    square = (dev(x, c, z, 1 - y), dev(1 - x, c, z, y), dev(1 - x, c, z, 1 - y))

    def send(src, dst, to, arrive, maybe_here=False):
        copy = pltpu.make_async_remote_copy(
            src, dst, sems.at[new_sems()], sems.at[arrive], device_id=to, device_id_type=MESH
        )
        if not maybe_here:
            copy.start()
            pending.append((copy, None))
            return
        away = jnp.logical_or(to[0] != p, to[1] != s)

        @pl.when(away)
        def _():
            copy.start()

        @pl.when(jnp.logical_not(away))
        def _():
            pltpu.make_async_copy(src, dst, sems.at[arrive]).start()

        pending.append((copy, away))

    def arrived(ref, arrive):
        pltpu.make_async_copy(ref, ref, sems.at[arrive]).wait()

    me = 8 * p + s
    barrier = pltpu.get_barrier_semaphore()

    def greet(i, carry):
        d = (me + i) % NDEV
        pl.semaphore_signal(barrier, inc=1, device_id=(d // 8, d % 8), device_id_type=MESH)
        return carry

    lax.fori_loop(1, NDEV, greet, 0)
    b.tok_t[...] = tokens[...].T
    b.cotown_t[...] = cotangent[...].T
    b.gs_acc[...] = jnp.zeros((2, PART, 128), F32)
    b.ln_out[...] = jnp.full((8, 128), length[0].astype(F32), F32)
    norm_rows = [ref[...].astype(F32)[l : l + 1] for l in range(LAYERS) for ref in (gains, shifts)]
    norm_rows = jnp.concatenate(norm_rows + [jnp.zeros((4, 48), F32)], axis=0)
    norm_rows = jnp.concatenate([norm_rows, jnp.zeros((8, 80), F32)], axis=1)
    norm_rows = jnp.concatenate([norm_rows, jnp.zeros((120, 128), F32)], axis=0)
    b.misc[...] = norm_rows.T.astype(BF16)
    for k in range(108):
        b.raw[2 * k : 2 * k + 2] = w_qkv[:, 128 * k : 128 * (k + 1)].astype(F32)
    for l in range(LAYERS):
        rows_from_triples(*(b.raw[every(l + 2 * i, 36, 6), :] for i in range(3)), b.left, b.right)
        for k in range(3):
            rows = slice(UNIT * k, UNIT * (k + 1))
            b.wq_out[l, k] = jnp.concatenate([b.left[rows], b.right[rows]], axis=0).astype(BF16)
    pl.semaphore_wait(barrier, NDEV - 1)

    tok_sem, len_sem, cot_sem, gn_sem = (new_sems() for _ in range(4))
    half_of = s // 4
    for gg in range(4):
        to = dev(gg // 2, half_of, z_mine, gg % 2)
        lane = pl.multiple_of(ROWS * s, ROWS)
        send(
            b.tok_t.at[pl.ds(PART * gg, PART), :],
            b.x_all.at[0, :, pl.ds(lane, ROWS)],
            to, tok_sem, True,
        )
    len_copies = []
    first_chunk = s % 4 == 0
    for gg in range(4):
        to = dev(gg // 2, half_of, z_mine, gg % 2)
        away = jnp.logical_or(to[0] != p, to[1] != s)
        copy = pltpu.make_async_remote_copy(
            b.ln_out, b.ln_in, sems.at[new_sems()], sems.at[len_sem], device_id=to, device_id_type=MESH
        )

        @pl.when(jnp.logical_and(first_chunk, away))
        def _():
            copy.start()

        @pl.when(jnp.logical_and(first_chunk, jnp.logical_not(away)))
        def _():
            pltpu.make_async_copy(b.ln_out, b.ln_in, sems.at[len_sem]).start()

        pending.append((copy, jnp.logical_and(first_chunk, away)))

    arrive_q = [new_sems() for _ in range(LAYERS)]
    relay_q = [new_sems() for _ in range(LAYERS)]
    level_w = [new_sems() for _ in range(LAYERS)]
    PARTS = dict(c=(COLS_AT, ROWS_AT - COLS_AT), m=(0, COLS_AT), r=(ROWS_AT, FLAT))
    along_w = {(name, l): new_sems(3) for l in range(LAYERS) for name in PARTS}
    relay_w = {(name, l): new_sems() for l in range(LAYERS) for name in PARTS}

    def send_qkv(l):
        for k in range(3):
            u = 3 * me + k
            cc, gg, t = u // 32, (u % 32) // 8, u % 8
            for zz in range(4):
                send(
                    b.wq_out.at[l, k], b.wq_in.at[l, cc, t],
                    dev(gg // 2, t // 4, zz, gg % 2), arrive_q[l], True,
                )

    def relay_qkv(l):
        mine = b.wq_in.at[l, :, pl.ds(4 * c, 4)]
        arrived(mine, arrive_q[l])
        send(mine, mine, sibling, relay_q[l])

    def send_level(l):
        to = dev(p // 2, y, z, p % 2)
        into = b.w_in.at[l, y, z]
        send(b.wm_out.at[l], into.at[0:COLS_AT], to, level_w[l], True)
        for cg in range(4):
            row = pl.multiple_of(COLS_AT + 2 * UNIT * p, 16)
            send(b.wc_out.at[l, cg], into.at[pl.ds(row, 2 * UNIT)], dev(cg // 2, y, z, cg % 2), level_w[l], True)
        send(b.wr_out.at[l], into.at[ROWS_AT:SHARD], to, level_w[l], True)

    def level_here(l):
        arrived(b.w_in.at[l, c, z], level_w[l])

    def send_along(name, l):
        start, count = PARTS[name]
        piece = b.w_in.at[l, c, z, start : start + count]
        for i in range(3):
            send(piece, piece, dev(x, c, (z + i + 1) % 4, y), along_w[name, l] + i)

    def relay(name, l):
        start, count = PARTS[name]
        for i in range(3):
            arrived(b.w_in.at[l, c, (z + 3 - i) % 4, start : start + count], along_w[name, l] + i)
        mine = b.w_in.at[l, c, :, start : start + count]
        send(mine, mine, sibling, relay_w[name, l])

    def relayed(name, l):
        start, count = PARTS[name]
        arrived(b.w_in.at[l, 1 - c, :, start : start + count], relay_w[name, l])

    send_qkv(0)
    for zz in range(4):
        for cc in range(2):
            gg = 2 * (p % 2) + s // 4
            row = pl.multiple_of(48 * (s % 4), 16)
            send(
                b.misc.at[0:48, :], b.gn_in.at[p // 2, pl.ds(row, 48), :],
                dev(gg // 2, cc, zz, gg % 2), gn_sem, True,
            )
    b.raw[0:288] = w_out[...].astype(F32)
    for l in range(LAYERS):
        b.wr_out[l] = b.raw[every(l, FLAT, 2), :].astype(BF16)
        parts = [b.raw[every(2 * i + l, UNIT, 12), :] for i in range(6)]
        turned = [turn(part) for part in parts]
        pieces = (
            (parts[0], parts[1]),
            (low_lanes(turned[1], turned[2]), turned[2]),
            (parts[3], parts[4]),
            (low_lanes(turned[4], turned[5]), turned[5]),
        )
        for cg in range(4):
            b.wc_out[l, cg] = jnp.concatenate(pieces[cg], axis=0).astype(BF16)
    for i, ref in enumerate((w_up, w_down)):
        b.raw[0:288] = ref[...].astype(F32)
        for l in range(LAYERS):
            b.wm_out[l, FLAT * i : FLAT * (i + 1)] = b.raw[every(l, FLAT, 2), :].astype(BF16)

    send_level(0)
    send_level(1)
    level_here(0)
    x_sem = [new_sems() for _ in range(LAYERS)]
    x_half = b.x_all.at[0, :, pl.ds(own, HALF)]
    arrived(x_half, tok_sem)
    send(x_half, x_half, sibling, x_sem[0])
    send_along("c", 0)
    send_along("m", 0)
    relay_qkv(0)
    arrived(b.ln_in, len_sem)
    valid = b.ln_in[0:1, 0:1]
    key_at = lax.broadcasted_iota(jnp.int32, (FULL, 128), 0).astype(F32)
    b.bias[...] = jnp.where(key_at < valid, 0.0, -1e30)
    arrived(b.gn_in, gn_sem)

    def gain_shift(l, k):
        columns = b.gn_in[k].astype(F32)
        return columns[:, 2 * l : 2 * l + 1], columns[:, 2 * l + 1 : 2 * l + 2]

    stat_used = [0]

    def exchange(*rows):
        i = stat_used[0]
        stat_used[0] += 1
        buffer = b.stats.at[i]
        count = 4 * len(rows)
        buffer[0, 0:count] = jnp.concatenate(
            [row[:, ROWS * j : ROWS * (j + 1)] for row in rows for j in range(4)], axis=0
        )
        base = new_sems(3)
        for d in range(3):
            send(buffer.at[0, 0:count], buffer.at[d + 1, 0:count], square[d], base + d)

        def finish():
            for d in range(3):
                arrived(buffer.at[d + 1, 0:count], base + d)
            whole = [buffer[d, 0:count] for d in range(4)]
            return [
                [
                    jnp.concatenate([four[4 * i + j : 4 * i + j + 1] for j in range(4)], axis=1)
                    for i in range(len(rows))
                ]
                for four in whole
            ]

        return finish

    def normalize_here(v, name, l, gain, shift, weighted=None):
        mean_here = jnp.sum(v, axis=0, keepdims=True) * (1.0 / PART)
        d = v - mean_here
        rows = [mean_here, jnp.sum(d * d, axis=0, keepdims=True)]
        if weighted is not None:
            rows += [jnp.sum(weighted, axis=0, keepdims=True), jnp.sum(weighted * d, axis=0, keepdims=True)]
        exchanged = exchange(*rows)
        return lambda: normalize_there(exchanged(), v, name, l, gain, shift, weighted)

    def normalize_there(four, v, name, l, gain, shift, weighted):
        mean = (four[0][0] + four[1][0] + four[2][0] + four[3][0]) * 0.25
        total = sum(f[1] + PART * (f[0] - mean) * (f[0] - mean) for f in four)
        factor = lax.rsqrt(total * (1.0 / D) + EPSILON)
        scaled = (v - mean) * factor
        getattr(b, "xh" + name)[l] = scaled
        getattr(b, "r" + name)[l, 0:1] = factor
        result = scaled * gain + shift
        if weighted is None:
            return result
        one = sum(f[2] for f in four) * (1.0 / D)
        two = sum(f[3] + (f[0] - mean) * f[2] for f in four) * factor * (1.0 / D)
        return result, one, two

    def gather_raw(l, start):
        for t in range(8):
            b.raw[FLAT * t : FLAT * (t + 1)] = b.w_in[l, t % 2, t // 2, start : start + FLAT].astype(F32)

    def wide_rows(l, start, into):
        gather_raw(l, start)
        for i in range(6):
            into[:, 128 * i : 128 * (i + 1)] = b.raw[every(i, PART, 6), :].astype(BF16)

    def scatter_raw(ref, start):
        for t in range(8):
            ref[t % 2, t // 2, start : start + FLAT] = b.raw[FLAT * t : FLAT * (t + 1)].astype(BF16)

    def flat_units(matrix, ref, start):
        for i in range(6):
            b.raw[every(i, PART, 6), :] = matrix[:, 128 * i : 128 * (i + 1)]
        scatter_raw(ref, start)

    att_sem = [[new_sems(3) for _ in range(3)] for _ in range(LAYERS)]
    att_send = [[new_sems(3) for _ in range(3)] for _ in range(LAYERS)]

    def send_cotangent():
        for gg in range(4):
            lane = pl.multiple_of(ROWS * (s % 4), ROWS)
            send(
                b.cotown_t.at[pl.ds(PART * gg, PART), :], b.cot_t.at[:, pl.ds(lane, ROWS)],
                dev(gg // 2, half_of, z_mine, gg % 2), cot_sem, True,
            )

    def forward(l):
        x_own = b.x_all[l, :, pl.ds(own, HALF)]
        arrived(b.wq_in.at[l, :, pl.ds(4 * (1 - c), 4)], relay_q[l])
        turned = []
        for cc in range(3):
            nat = matrix_of(b.wq_in[l, cc])
            b.wn_q[l, cc] = nat
            turned.append(nat.T)
        b.q_t[l] = mm(turned[0], x_own).astype(BF16) * jnp.asarray(0.125, BF16)

        def keys_values(start, part):
            for matrix, name in ((turned[1], "k"), (turned[2], "v")):
                value = mm(matrix, part).astype(BF16)
                getattr(b, name + "_t")[l, :, pl.ds(start, HALF)] = value
                for h in range(HEADS_HERE):
                    getattr(b, name + "_n")[l, h, pl.ds(start, HALF), :] = value[HEAD * h : HEAD * (h + 1)].T

        keys_values(own, x_own)
        arrived(b.x_all.at[l, :, pl.ds(other, HALF)], x_sem[l])
        keys_values(other, b.x_all[l, :, pl.ds(other, HALF)])

        def one_head(h, carry):
            head = pl.multiple_of(HEAD * h, HEAD)
            q = b.q_t[l, pl.ds(head, HEAD), :]
            largest = jnp.full((1, HALF), -jnp.inf, F32)
            for kb in range(0, FULL, KEY_BLOCK):
                scores = mm(b.k_n[l, h, kb : kb + KEY_BLOCK, :], q) + b.bias[kb : kb + KEY_BLOCK, 0:1]
                b.s_scr[kb : kb + KEY_BLOCK] = scores
                largest = jnp.maximum(largest, jnp.max(scores, axis=0, keepdims=True))
            total = jnp.zeros((1, HALF), F32)
            for kb in range(0, FULL, KEY_BLOCK):
                powers = jnp.exp(b.s_scr[kb : kb + KEY_BLOCK] - largest)
                total += jnp.sum(powers, axis=0, keepdims=True)
                b.p_t[l, h, kb : kb + KEY_BLOCK] = powers.astype(BF16)
            inverse = 1.0 / total
            b.rinv[l, h, 0:1] = inverse
            out = mm(b.v_t[l, pl.ds(head, HEAD), :], b.p_t[l, h]) * inverse
            b.o_t[l, pl.ds(head, HEAD), :] = out
            rows = pl.ds(pl.multiple_of(g_rows + head, HEAD), HEAD)
            b.att_all[l, rows, :] = out.astype(BF16)
            piece = b.att_all.at[l, rows, :]
            for d in range(3):
                pltpu.make_async_remote_copy(
                    piece, piece, sems.at[att_send[l][d] + h], sems.at[att_sem[l][d] + h],
                    device_id=square[d], device_id_type=MESH,
                ).start()
            return carry

        lax.fori_loop(0, HEADS_HERE, one_head, 0)
        relay("c", l)
        relayed("c", l)
        for r in range(4):
            for t in range(8):
                rows = slice(UNIT * (8 * r + t), UNIT * (8 * r + t + 1))
                start = COLS_AT + 2 * UNIT * r
                unit = b.w_in[l, t % 2, t // 2, start : start + 2 * UNIT].astype(F32)
                b.left[rows] = unit[:UNIT]
                b.right[rows] = unit[UNIT:]
        columns_t = jnp.concatenate([b.left[...], b.right[:, 0:64]], axis=1).astype(BF16).T
        flips = ((0, 1), (1, 0), (1, 1))
        for h in range(HEADS_HERE):
            for d, (fx, fy) in enumerate(flips):
                px = 1 - x if fx else x
                py = 1 - y if fy else y
                start = pl.multiple_of(PART * (2 * px + py) + HEAD * h, HEAD)
                arrived(b.att_all.at[l, pl.ds(start, HEAD), :], att_sem[l][d] + h)
        relay("m", l)
        branch = mm(columns_t, b.att_all[l])
        gain, shift = gain_shift(l, 0)
        finish = normalize_here(x_own.astype(F32) + branch, "1", l, gain, shift)
        relayed("m", l)
        wide_rows(l, 0, b.wn_u.at[l])
        b.wt_u[...] = b.wn_u[l].T
        gather_raw(l, FLAT)
        rows_from_triples(*(b.raw[every(i, PART_FF // 2, 3), :] for i in range(3)), b.left, b.right)
        nat = jnp.concatenate([b.left[...], b.right[:, 0:64]], axis=1).astype(BF16)
        b.wn_d[l] = nat
        down_t = nat.T
        middle = finish().astype(BF16)
        if l == 0:
            send_qkv(1)
            level_here(1)
            send_along("c", 1)
            send_along("m", 1)
            send_cotangent()
        b.mid[l] = middle

        def one_block(i, carry):
            rows = pl.ds(pl.multiple_of(FF_BLOCK * i, FF_BLOCK), FF_BLOCK)
            expanded = mm(b.wt_u[rows, :], b.mid[l])
            cdf, slope = erf_pair(expanded)
            b.act[l, rows, :] = (expanded * cdf).astype(BF16)
            b.dgl[l, rows, :] = slope
            return carry

        lax.fori_loop(0, PART_FF // FF_BLOCK, one_block, 0)
        second = middle.astype(F32) + mm(down_t, b.act[l])
        gain, shift = gain_shift(l, 1)
        if l + 1 < LAYERS:
            return normalize_here(second, "2", l, gain, shift)()
        arrived(b.cot_t, cot_sem)
        position = lax.broadcasted_iota(jnp.int32, (PART, HALF), 1) + HALF * c
        grad = jnp.where(position.astype(F32) < valid, b.cot_t[...].astype(F32), 0.0)
        return normalize_here(second, "2", l, gain, shift, grad * gain)(), grad

    hidden = forward(0)
    b.x_all[1, :, pl.ds(own, HALF)] = hidden.astype(BF16)
    x_half = b.x_all.at[1, :, pl.ds(own, HALF)]
    send(x_half, x_half, sibling, x_sem[1])
    relay_qkv(1)
    send_along("r", 1)
    send_along("r", 0)
    (hidden, one, two), grad = forward(1)

    mix_sem, tg_sem = new_sems(), new_sems()

    def send_back(value, out_ref, in_ref, arrive):
        out_ref[...] = value.astype(BF16)
        for k in range(4):
            send(
                out_ref.at[:, ROWS * k : ROWS * (k + 1)], in_ref.at[pl.ds(g_rows, PART), :],
                (seq_here, 4 * c + k), arrive, True,
            )

    send_back(hidden, b.mix_out, b.mix_in, mix_sem)

    half_sem = {(name, l): new_sems() for l in range(LAYERS) for name in "moq"}
    level_sem = {(name, l): new_sems(3) for l in range(LAYERS) for name in "mo"}
    owner_sem = {(name, l): new_sems() for l in range(LAYERS) for name in "moq"}

    def to_sibling(name, l):
        there = pl.ds(4 * (1 - c), 4) if name == "q" else 1 - c
        send(getattr(b, "gb_" + name).at[l, there], getattr(b, "sb_" + name).at[l], sibling, half_sem[name, l])

    def to_level(name, l):
        here, mine = getattr(b, "sb_" + name), getattr(b, "gm_" + name)
        arrived(here.at[l], half_sem[name, l])
        mine[l] = (getattr(b, "gb_" + name)[l, c].astype(F32) + here[l].astype(F32)).astype(BF16)
        for i in range(3):
            there = (z + i + 1) % 4
            send(
                mine.at[l, there], getattr(b, "rz_" + name).at[l, i], dev(x, c, there, y), level_sem[name, l] + i
            )

    def to_owner(name, l):
        four = getattr(b, "rz_" + name)
        for i in range(3):
            arrived(four.at[l, i], level_sem[name, l] + i)
        total = getattr(b, "gm_" + name)[l, z].astype(F32) + sum(four[l, i].astype(F32) for i in range(3))
        final = getattr(b, "gf_" + name)
        final[l] = total.astype(BF16)
        send(final.at[l], getattr(b, "rg_" + name).at[l], dev(g // 2, g % 2, z, c), owner_sem[name, l], True)

    def qkv_to_owners(l):
        arrived(b.sb_q.at[l], half_sem["q", l])
        b.gm_q[l] = (b.gb_q[l, pl.ds(4 * c, 4)].astype(F32) + b.sb_q[l].astype(F32)).astype(BF16)
        for k in range(4):
            for cc in range(3):
                u = 32 * cc + 8 * g + 4 * c + k
                j = u // 3
                send(
                    b.gm_q.at[l, k, cc], b.rg_q.at[l, z, u % 3], (j // 8, j % 8), owner_sem["q", l], True
                )

    lane_at = lax.broadcasted_iota(jnp.int32, (PART, 128), 1)

    def norm_grads(grad, scaled, l, k):
        gain_grad = jnp.sum(grad * scaled, axis=1, keepdims=True)
        shift_grad = jnp.sum(grad, axis=1, keepdims=True)
        b.gs_acc[k] += jnp.where(lane_at == 2 * l, gain_grad, 0.0) + jnp.where(
            lane_at == 2 * l + 1, shift_grad, 0.0
        )

    def normalize_back_here(grad, name, l, k, known=None):
        gain, _ = gain_shift(l, k)
        scaled = getattr(b, "xh" + name)[l]
        weighted = grad * gain
        if known is None:
            finish = exchange(
                jnp.sum(weighted, axis=0, keepdims=True), jnp.sum(weighted * scaled, axis=0, keepdims=True)
            )
            norm_grads(grad, scaled, l, k)
            four = finish()
            one, two = (sum(f[i] for f in four) * (1.0 / D) for i in range(2))
        else:
            one, two = known
        return getattr(b, "r" + name)[l, 0:1] * (weighted - one - scaled * two)

    gs_sem = new_sems()

    def send_norm_grads():
        for k in range(2):
            turned = b.gs_acc[k].T[0:8]
            for q in range(4):
                b.gs_out[k, q] = jnp.concatenate([turned[:, 48 * q : 48 * (q + 1)], jnp.zeros((8, 80), F32)], axis=1)
                send(
                    b.gs_out.at[k, q], b.gs_in.at[2 * z + c], (2 * k + g // 2, 4 * (g % 2) + q), gs_sem, True
                )

    bg_sem = [new_sems(3) for _ in range(LAYERS)]
    dx_sem = [new_sems() for _ in range(LAYERS)]

    def backward(l, grad, known=None):
        relay("r", l)
        second_grad = normalize_back_here(grad, "2", l, 1, known)
        b.sgb[l] = second_grad.astype(BF16)
        if l + 1 < LAYERS:
            qkv_to_owners(l + 1)

        def one_block(i, carry):
            rows = pl.ds(pl.multiple_of(FF_BLOCK * i, FF_BLOCK), FF_BLOCK)
            active_grad = mm(b.wn_d[l, rows, :], b.sgb[l])
            b.eg[l, rows, :] = (active_grad * b.dgl[l, rows, :]).astype(BF16)
            return carry

        lax.fori_loop(0, PART_FF // FF_BLOCK, one_block, 0)
        middle_grad = second_grad + mm(b.wn_u[l], b.eg[l])
        first_grad = normalize_back_here(middle_grad, "1", l, 0)
        b.fg[...] = first_grad
        b.bg_all[l, pl.ds(g_rows, PART), :] = first_grad.astype(BF16)
        piece = b.bg_all.at[l, pl.ds(g_rows, PART), :]
        for d in range(3):
            send(piece, piece, square[d], bg_sem[l] + d)
        if known is not None:
            norm_grads(grad, b.xh2[l], l, 1)
        if l == 0:
            send_norm_grads()
        grads = mm_nt(b.act[l], b.sgb[l])
        b.left[...] = grads[:, :128]
        b.right[:, 0:64] = grads[:, 128:]
        for i, part in enumerate(triples_from_rows(PART_FF // 2, b.left, b.right)):
            b.raw[every(i, PART_FF // 2, 3), :] = part
        scatter_raw(b.gb_m.at[l], 0)
        flat_units(mm_nt(b.mid[l], b.eg[l]), b.gb_m.at[l], FLAT)
        to_sibling("m", l)
        if l + 1 < LAYERS:
            to_owner("m", l + 1)
            to_owner("o", l + 1)
        relayed("r", l)
        wide_rows(l, ROWS_AT, b.wn_r.at[l])
        for d, (fx, fy) in enumerate(((0, 1), (1, 0), (1, 1))):
            px = 1 - x if fx else x
            py = 1 - y if fy else y
            start = pl.multiple_of(PART * (2 * px + py), PART)
            arrived(b.bg_all.at[l, pl.ds(start, PART), :], bg_sem[l] + d)
        att = b.att_all[l, pl.ds(g_rows, PART), :]
        flat_units(mm_nt(att, b.bg_all[l]), b.gb_o.at[l], 0)
        to_sibling("o", l)
        b.do_t[...] = mm(b.wn_r[l], b.bg_all[l]).astype(BF16)
        to_level("m", l)
        to_level("o", l)

        def one_head(h, carry):
            head = pl.multiple_of(HEAD * h, HEAD)
            rows = pl.ds(head, HEAD)
            inverse = b.rinv[l, h, 0:1]
            grad_out = b.do_t[rows, :].astype(F32)
            delta = jnp.sum(grad_out * b.o_t[l, rows, :], axis=0, keepdims=True) * inverse
            grad_scaled = (grad_out * inverse).astype(BF16)
            for kb in range(0, FULL, KEY_BLOCK):
                block = slice(kb, kb + KEY_BLOCK)
                grad_probs = mm(b.v_n[l, h, block, :], grad_scaled)
                b.ds_scr[block] = (b.p_t[l, h, block].astype(F32) * (grad_probs - delta)).astype(BF16)
            b.dq_t[rows, :] = (mm(b.k_t[l, rows, :], b.ds_scr[...]) * 0.125).astype(BF16)
            b.dk_t[rows, :] = mm_nt(b.q_t[l, rows, :], b.ds_scr[...]).astype(BF16)
            b.dv_t[rows, :] = mm_nt(grad_scaled, b.p_t[l, h]).astype(BF16)
            return carry

        lax.fori_loop(0, HEADS_HERE, one_head, 0)
        w_q, w_k, w_v = (b.wn_q[l, cc] for cc in range(3))
        b.dx_out[l] = mm(w_k, b.dk_t[:, pl.ds(other, HALF)]) + mm(w_v, b.dv_t[:, pl.ds(other, HALF)])
        send(b.dx_out.at[l], b.dx_in.at[l], sibling, dx_sem[l])
        x_own = b.x_all[l, :, pl.ds(own, HALF)]
        b.gb_q[l, :, 0] = units_of(mm_nt(x_own, b.dq_t[...]))
        b.gb_q[l, :, 1] = units_of(mm_nt(b.x_all[l], b.dk_t[...]))
        b.gb_q[l, :, 2] = units_of(mm_nt(b.x_all[l], b.dv_t[...]))
        to_sibling("q", l)
        here = mm(w_q, b.dq_t[...])
        here += mm(w_k, b.dk_t[:, pl.ds(own, HALF)]) + mm(w_v, b.dv_t[:, pl.ds(own, HALF)])
        arrived(b.dx_in.at[l], dx_sem[l])
        return b.fg[...] + here + b.dx_in[l]

    grad = backward(1, grad, (one, two))
    grad = backward(0, grad)
    send_back(grad, b.tg_out, b.tg_in, tg_sem)
    qkv_to_owners(0)
    to_owner("m", 0)
    to_owner("o", 0)

    arrived(b.mix_in, mix_sem)
    mixed[...] = b.mix_in[...].T
    for l in reversed(range(LAYERS)):
        arrived(b.rg_m.at[l], owner_sem["m", l])
        g_down[every(l, FLAT, 2), :] = b.rg_m[l, 0:FLAT].astype(F32)
        g_up[every(l, FLAT, 2), :] = b.rg_m[l, FLAT : 2 * FLAT].astype(F32)
        arrived(b.rg_o.at[l], owner_sem["o", l])
        g_out[every(l, FLAT, 2), :] = b.rg_o[l].astype(F32)
        arrived(b.rg_q.at[l], owner_sem["q", l])
        total = sum(b.rg_q[l, i].astype(F32) for i in range(4))
        b.left[0:72] = total[:, :UNIT].reshape(72, 128)
        b.right[0:72] = total[:, UNIT:].reshape(72, 128)
        for i, part in enumerate(triples_from_rows(36, b.left, b.right)):
            b.raw[every(l + 2 * i, 36, 6), :] = part
    arrived(b.tg_in, tg_sem)
    tokens_grad[...] = b.tg_in[...].T
    arrived(b.gs_in, gs_sem)
    g_norm[...] = sum(b.gs_in[i] for i in range(8))

    for k in range(108):
        g_qkv[:, 128 * k : 128 * (k + 1)] = b.raw[2 * k : 2 * k + 2]

    for copy, when in pending:
        if when is None:
            copy.wait_send()
        else:
            pl.when(when)(copy.wait_send)
    for l in range(LAYERS):
        for h in range(HEADS_HERE):
            for d in range(3):
                piece = b.att_all.at[l, pl.ds(pl.multiple_of(g_rows + HEAD * h, HEAD), HEAD), :]
                pltpu.make_async_remote_copy(
                    piece, piece, sems.at[att_send[l][d] + h], sems.at[att_sem[l][d] + h],
                    device_id=square[d], device_id_type=MESH,
                ).wait_send()


def hand_over(*refs):
    plain, norms, outs = refs[:6], refs[6], refs[7:]
    for ref, out in zip(plain, outs):
        out[...] = ref[...]
    for k in range(2):
        for l in range(LAYERS):
            outs[6 + k][l : l + 1, :] = norms[2 * l + k : 2 * l + k + 1, 0 : PART // 4]


def fast_device(
    tokens, lengths, qkv_weight, out_weight, up_weight, down_weight, norm_gain, norm_shift, cotangent
):
    def raw(array):
        return array.reshape(LAYERS, -1, 128).transpose(1, 0, 2).reshape(-1, 128)

    def unraw(array):
        return array.reshape(-1, LAYERS, 128).transpose(1, 0, 2).reshape(LAYERS, -1)

    operands = (
        tokens[0],
        cotangent[0],
        lengths,
        norm_gain,
        norm_shift,
        qkv_weight,
        raw(out_weight),
        raw(up_weight),
        raw(down_weight),
    )
    vmem = pl.BlockSpec(memory_space=pltpu.VMEM)
    shapes = (
        ((ROWS, D), BF16),
        ((ROWS, D), BF16),
        ((LAYERS, 3 * UNIT * PART), F32),
        ((LAYERS * FLAT, 128), F32),
        ((LAYERS * FLAT, 128), F32),
        ((LAYERS * FLAT, 128), F32),
        ((8, 128), F32),
    )
    mixed, tokens_grad, g_qkv, g_out, g_up, g_down, g_norm = pl.pallas_call(
        fast_kernel,
        out_shape=tuple(jax.ShapeDtypeStruct(*shape) for shape in shapes),
        in_specs=[vmem] * 2 + [pl.BlockSpec(memory_space=pltpu.SMEM)] + [vmem] * 6,
        out_specs=tuple([vmem] * len(shapes)),
        scratch_shapes=[pltpu.SemaphoreType.DMA((SEMS,))] + [pltpu.VMEM(*entry) for entry in SCRATCH.values()],
        compiler_params=pltpu.CompilerParams(
            collective_id=0, has_side_effects=True, vmem_limit_bytes=60 * 2**20
        ),
        name="encoder",
    )(*operands)
    results = (mixed, tokens_grad, g_qkv, g_out, g_up, g_down)
    shapes = [jax.ShapeDtypeStruct(array.shape, array.dtype) for array in results]
    shapes += [jax.ShapeDtypeStruct((LAYERS, PART // 4), F32)] * 2
    mixed, tokens_grad, g_qkv, g_out, g_up, g_down, g_gain, g_shift = pl.pallas_call(
        hand_over,
        out_shape=tuple(shapes),
        in_specs=[vmem] * (len(results) + 1),
        out_specs=tuple([vmem] * len(shapes)),
        name="hand_over",
    )(*results, g_norm)
    return (
        mixed[None],
        tokens_grad[None],
        g_qkv,
        unraw(g_out),
        unraw(g_up),
        unraw(g_down),
        g_gain,
        g_shift,
    )


def solution(mesh):
    small = (mesh.shape["dp"], mesh.shape["seq"]) == (4, 8)
    return jax.shard_map(
        fast_device if small else per_device,
        mesh=mesh,
        in_specs=(
            P("dp", "seq", None),
            P("dp"),
            P(None, ("dp", "seq")),
            P(None, ("dp", "seq")),
            P(None, ("dp", "seq")),
            P(None, ("dp", "seq")),
            P(None, ("dp", "seq")),
            P(None, ("dp", "seq")),
            P("dp", "seq", None),
        ),
        out_specs=(
            P("dp", "seq", None),
            P("dp", "seq", None),
            P(None, ("dp", "seq")),
            P(None, ("dp", "seq")),
            P(None, ("dp", "seq")),
            P(None, ("dp", "seq")),
            P(None, ("dp", "seq")),
            P(None, ("dp", "seq")),
        ),
        check_vma=False,
    )
```

```python
import types
from functools import partial

import jax
import jax.numpy as jnp
from jax import lax
from jax.experimental import pallas as pl
from jax.experimental.pallas import tpu as pltpu
from jax.sharding import PartitionSpec as P

D = 768
HEADS = 12
HEAD = 64
FF = 3072
GROUPS = 4


EPSILON = 1e-06


def grouped(inputs, weight):
    count = inputs.shape[0]
    shaped = inputs.reshape(count, weight.shape[0], -1)
    result = jnp.einsum("tgi,gio->tgo", shaped, weight, preferred_element_type=jnp.float32)
    return result.reshape(count, -1)


def normalize(values, gain, shift):
    center = values - jnp.mean(values, axis=-1, keepdims=True)
    factor = lax.rsqrt(jnp.mean(center * center, axis=-1, keepdims=True) + EPSILON)
    scaled = center * factor
    return (scaled * gain + shift, scaled, factor)


def normalize_back(grad_out, scaled, factor, gain):
    weighted = grad_out * gain
    grad_in = factor * (
        weighted
        - jnp.mean(weighted, axis=-1, keepdims=True)
        - scaled * jnp.mean(weighted * scaled, axis=-1, keepdims=True)
    )
    return (grad_in, jnp.sum(grad_out * scaled, axis=0), jnp.sum(grad_out, axis=0))


def unpack(pieces):
    qkv_flat, out_flat, up_flat, down_flat, gain_flat, shift_flat = pieces
    part = D // GROUPS
    part_ff = FF // GROUPS
    return (
        qkv_flat.reshape(3, GROUPS, part, part),
        out_flat.reshape(D, D),
        up_flat.reshape(GROUPS, part, part_ff),
        down_flat.reshape(GROUPS, part_ff, part),
        gain_flat.reshape(2, D).astype(jnp.float32),
        shift_flat.reshape(2, D).astype(jnp.float32),
    )


def project_heads(rows, matrices):
    total_rows = rows.shape[0]
    part = D // GROUPS
    result = jnp.einsum(
        "tgi,cgio->ctgo",
        rows.reshape(total_rows, GROUPS, part),
        matrices,
        preferred_element_type=jnp.float32,
    ).astype(jnp.bfloat16)
    return result.reshape(matrices.shape[0], total_rows, HEADS, HEAD).transpose(0, 2, 1, 3)


def head_forward(key_ok, scaling, pieces):
    query_head, key_head, value_head = pieces
    scores = (
        jnp.einsum("td,sd->ts", query_head, key_head, preferred_element_type=jnp.float32) * scaling
    )
    scores = jnp.where(key_ok[None, :], scores, -1e30)
    largest = jnp.max(scores, axis=-1, keepdims=True)
    powers = jnp.exp(scores - largest)
    total = jnp.sum(powers, axis=-1, keepdims=True)
    probs = (powers / total).astype(jnp.bfloat16)
    result = jnp.dot(probs, value_head, preferred_element_type=jnp.float32)
    return (result, (largest + jnp.log(total))[:, 0])


def head_backward(key_ok, scaling, pieces):
    query_head, key_head, value_head, grad_head, log_total = pieces
    scores = (
        jnp.einsum("td,sd->ts", query_head, key_head, preferred_element_type=jnp.float32) * scaling
    )
    scores = jnp.where(key_ok[None, :], scores, -1e30)
    probs = jnp.exp(scores - log_total[:, None])
    grad_probs = jnp.einsum("td,sd->ts", grad_head, value_head, preferred_element_type=jnp.float32)
    delta_row = jnp.sum(probs * grad_probs, axis=-1, keepdims=True)
    grad_scores = (probs * (grad_probs - delta_row)).astype(jnp.bfloat16)
    grad_query = jnp.dot(grad_scores, key_head, preferred_element_type=jnp.float32) * scaling
    grad_key = (
        jnp.einsum("ts,td->sd", grad_scores, query_head, preferred_element_type=jnp.float32)
        * scaling
    )
    grad_value = jnp.einsum(
        "ts,td->sd", probs.astype(jnp.bfloat16), grad_head, preferred_element_type=jnp.float32
    )
    return (grad_query, grad_key, grad_value)


def per_device(
    tokens,
    lengths,
    qkv_weight,
    out_weight,
    up_weight,
    down_weight,
    norm_gain,
    norm_shift,
    cotangent,
):
    layers = qkv_weight.shape[0]
    count = tokens.shape[1]
    slots = count * lax.axis_size("seq")
    first_slot = lax.axis_index("seq") * count
    length = lengths[0]
    key_ok = jnp.arange(slots, dtype=jnp.int32) < length
    row_ok = first_slot + jnp.arange(count, dtype=jnp.int32) < length
    scaling = HEAD ** (-0.5)
    part = D // GROUPS
    part_ff = FF // GROUPS
    hidden_low = tokens[0]
    saved = []
    for layer_index in range(layers):
        gathered = (
            lax.all_gather(qkv_weight[layer_index], ("dp", "seq"), axis=0, tiled=True),
            lax.all_gather(out_weight[layer_index], ("dp", "seq"), axis=0, tiled=True),
            lax.all_gather(up_weight[layer_index], ("dp", "seq"), axis=0, tiled=True),
            lax.all_gather(down_weight[layer_index], ("dp", "seq"), axis=0, tiled=True),
            lax.all_gather(norm_gain[layer_index], ("dp", "seq"), axis=0, tiled=True),
            lax.all_gather(norm_shift[layer_index], ("dp", "seq"), axis=0, tiled=True),
        )
        project, out_matrix, up_matrix, down_matrix, gains, shifts = unpack(gathered)
        heads = project_heads(hidden_low, project)
        key_all, value_all = (
            lax.all_gather(heads[1], "seq", axis=1, tiled=True),
            lax.all_gather(heads[2], "seq", axis=1, tiled=True),
        )
        attended, log_total = lax.map(
            partial(head_forward, key_ok, scaling), (heads[0], key_all, value_all)
        )
        attended_low = attended.transpose(1, 0, 2).reshape(count, D).astype(jnp.bfloat16)
        branch = jnp.dot(attended_low, out_matrix, preferred_element_type=jnp.float32)
        middle, scaled_one, factor_one = normalize(
            hidden_low.astype(jnp.float32) + branch, gains[0], shifts[0]
        )
        middle_low = middle.astype(jnp.bfloat16)
        expanded = grouped(middle_low, up_matrix)
        activated = jax.nn.gelu(expanded, approximate=False).astype(jnp.bfloat16)
        shrunk = grouped(activated, down_matrix)
        output, scaled_two, factor_two = normalize(
            middle_low.astype(jnp.float32) + shrunk, gains[1], shifts[1]
        )
        kept = None
        saved.append(
            (
                hidden_low,
                heads,
                log_total,
                attended_low,
                middle_low,
                expanded,
                activated,
                scaled_one,
                factor_one,
                scaled_two,
                factor_two,
                kept,
            )
        )
        hidden_low = output.astype(jnp.bfloat16)
    mixed = hidden_low[None]
    grad_hidden = cotangent[0].astype(jnp.float32) * row_ok[:, None].astype(jnp.float32)
    owned_list = []
    for layer_index in reversed(range(layers)):
        (
            inputs_low,
            heads,
            log_total,
            attended_low,
            middle_low,
            expanded,
            activated,
            scaled_one,
            factor_one,
            scaled_two,
            factor_two,
            kept,
        ) = saved[layer_index]
        gathered = (
            lax.all_gather(qkv_weight[layer_index], ("dp", "seq"), axis=0, tiled=True),
            lax.all_gather(out_weight[layer_index], ("dp", "seq"), axis=0, tiled=True),
            lax.all_gather(up_weight[layer_index], ("dp", "seq"), axis=0, tiled=True),
            lax.all_gather(down_weight[layer_index], ("dp", "seq"), axis=0, tiled=True),
            lax.all_gather(norm_gain[layer_index], ("dp", "seq"), axis=0, tiled=True),
            lax.all_gather(norm_shift[layer_index], ("dp", "seq"), axis=0, tiled=True),
        )
        project, out_matrix, up_matrix, down_matrix, gains, shifts = unpack(gathered)
        key_all, value_all = (
            lax.all_gather(heads[1], "seq", axis=1, tiled=True),
            lax.all_gather(heads[2], "seq", axis=1, tiled=True),
        )
        grad_two, gain_two, shift_two = normalize_back(
            grad_hidden, scaled_two, factor_two, gains[1]
        )
        shrunk_grad = grad_two.astype(jnp.bfloat16).reshape(count, GROUPS, part)
        down_terms = jnp.einsum(
            "tgf,tgo->gfo",
            activated.reshape(count, GROUPS, part_ff),
            shrunk_grad,
            preferred_element_type=jnp.float32,
        )
        active_grad = jnp.einsum(
            "tgo,gfo->tgf", shrunk_grad, down_matrix, preferred_element_type=jnp.float32
        ).reshape(count, FF)
        unused_value, gelu_pull = jax.vjp(partial(jax.nn.gelu, approximate=False), expanded)
        expanded_grad = (
            gelu_pull(active_grad)[0].astype(jnp.bfloat16).reshape(count, GROUPS, part_ff)
        )
        up_terms = jnp.einsum(
            "tgi,tgf->gif",
            middle_low.reshape(count, GROUPS, part),
            expanded_grad,
            preferred_element_type=jnp.float32,
        )
        middle_grad = grad_two + jnp.einsum(
            "tgf,gif->tgi", expanded_grad, up_matrix, preferred_element_type=jnp.float32
        ).reshape(count, D)
        grad_one, gain_one, shift_one = normalize_back(
            middle_grad, scaled_one, factor_one, gains[0]
        )
        branch_grad = grad_one.astype(jnp.bfloat16)
        out_terms = jnp.einsum(
            "ti,to->io", attended_low, branch_grad, preferred_element_type=jnp.float32
        )
        attended_grad = jnp.einsum(
            "to,io->ti", branch_grad, out_matrix, preferred_element_type=jnp.float32
        ).astype(jnp.bfloat16)
        grad_heads = attended_grad.reshape(count, HEADS, HEAD).transpose(1, 0, 2)
        grad_query, key_terms, value_terms = lax.map(
            partial(head_backward, key_ok, scaling),
            (heads[0], key_all, value_all, grad_heads, log_total),
        )
        grad_key, grad_value = (
            lax.psum_scatter(
                key_terms.astype(jnp.bfloat16), "seq", scatter_dimension=1, tiled=True
            ).astype(jnp.float32),
            lax.psum_scatter(
                value_terms.astype(jnp.bfloat16), "seq", scatter_dimension=1, tiled=True
            ).astype(jnp.float32),
        )
        grad_projected = jnp.stack((grad_query, grad_key, grad_value)).astype(jnp.bfloat16)
        grad_projected = grad_projected.transpose(0, 2, 1, 3).reshape(3, count, GROUPS, part)
        qkv_terms = jnp.einsum(
            "tgi,ctgo->cgio",
            inputs_low.reshape(count, GROUPS, part),
            grad_projected,
            preferred_element_type=jnp.float32,
        )
        grad_hidden = grad_one + jnp.einsum(
            "ctgo,cgio->tgi", grad_projected, project, preferred_element_type=jnp.float32
        ).reshape(count, D)
        owned = (
            lax.psum_scatter(qkv_terms.reshape(-1), ("dp", "seq"), scatter_dimension=0, tiled=True),
            lax.psum_scatter(out_terms.reshape(-1), ("dp", "seq"), scatter_dimension=0, tiled=True),
            lax.psum_scatter(up_terms.reshape(-1), ("dp", "seq"), scatter_dimension=0, tiled=True),
            lax.psum_scatter(
                down_terms.reshape(-1), ("dp", "seq"), scatter_dimension=0, tiled=True
            ),
            lax.psum_scatter(
                jnp.stack((gain_one, gain_two)).reshape(-1),
                ("dp", "seq"),
                scatter_dimension=0,
                tiled=True,
            ),
            lax.psum_scatter(
                jnp.stack((shift_one, shift_two)).reshape(-1),
                ("dp", "seq"),
                scatter_dimension=0,
                tiled=True,
            ),
        )
        owned_list.insert(0, owned)
    tokens_grad = grad_hidden.astype(jnp.bfloat16)[None]
    stacked = tuple((jnp.stack([entry[member] for entry in owned_list]) for member in range(6)))
    return (
        mixed,
        tokens_grad,
        stacked[0],
        stacked[1],
        stacked[2],
        stacked[3],
        stacked[4],
        stacked[5],
    )


F32 = jnp.float32
BF16 = jnp.bfloat16
PART = D // GROUPS
PART_FF = FF // GROUPS
LAYERS = 2
ROWS = 128
HALF = 4 * ROWS
FULL = 2 * HALF
NDEV = 32
UNIT = PART // 8
FLAT = UNIT * PART_FF // 128
COLS_AT = 2 * FLAT
ROWS_AT = COLS_AT + GROUPS * 2 * UNIT
QKV_AT = ROWS_AT + FLAT
SHARD = QKV_AT + 3 * 2 * UNIT
HEADS_HERE = HEADS // GROUPS
KEY_BLOCK = 256
FF_BLOCK = 128
SEMS = 512
MESH = pl.DeviceIdType.MESH

SCRATCH = dict(
    tokens=((ROWS, D), BF16),
    w_qkv=((LAYERS, 3 * UNIT * PART), BF16),
    gains=((LAYERS, PART // 4), BF16),
    shifts=((LAYERS, PART // 4), BF16),
    w_out=((LAYERS * FLAT, 128), BF16),
    w_up=((LAYERS * FLAT, 128), BF16),
    w_down=((LAYERS * FLAT, 128), BF16),
    cotangent=((ROWS, D), BF16),
    x_all=((LAYERS, PART, FULL), BF16),
    cot_t=((PART, HALF), BF16),
    tok_t=((D, ROWS), BF16),
    cotown_t=((D, ROWS), BF16),
    ln_in=((8, 128), F32),
    gn_in=((2, PART, 128), BF16),
    misc=((128, 128), BF16),
    ln_out=((8, 128), F32),
    wq_out=((LAYERS, 3, 2 * UNIT, 128), BF16),
    wc_out=((LAYERS, GROUPS, 2 * UNIT, 128), BF16),
    wr_out=((LAYERS, FLAT, 128), BF16),
    wm_out=((LAYERS, 2 * FLAT, 128), BF16),
    w_in=((LAYERS, 2, 4, SHARD, 128), BF16),
    raw=((8 * FLAT, 128), F32),
    left=((PART_FF, 128), F32),
    right=((PART_FF, 128), F32),
    wn_q=((LAYERS, 3, PART, PART), BF16),
    wn_r=((LAYERS, PART, D), BF16),
    wn_u=((LAYERS, PART, PART_FF), BF16),
    wn_d=((LAYERS, PART_FF, PART), BF16),
    wt_u=((PART_FF, PART), BF16),
    bias=((FULL, 128), F32),
    q_t=((LAYERS, PART, HALF), BF16),
    k_t=((LAYERS, PART, FULL), BF16),
    v_t=((LAYERS, PART, FULL), BF16),
    k_n=((LAYERS, HEADS_HERE, FULL, HEAD), BF16),
    v_n=((LAYERS, HEADS_HERE, FULL, HEAD), BF16),
    p_t=((LAYERS, HEADS_HERE, FULL, HALF), BF16),
    rinv=((LAYERS, HEADS_HERE, 8, HALF), F32),
    s_scr=((FULL, HALF), F32),
    ds_scr=((FULL, HALF), BF16),
    o_t=((LAYERS, PART, HALF), F32),
    att_all=((LAYERS, D, HALF), BF16),
    bg_all=((LAYERS, D, HALF), BF16),
    xh1=((LAYERS, PART, HALF), F32),
    xh2=((LAYERS, PART, HALF), F32),
    r1=((LAYERS, 8, HALF), F32),
    r2=((LAYERS, 8, HALF), F32),
    mid=((LAYERS, PART, HALF), BF16),
    act=((LAYERS, PART_FF, HALF), BF16),
    dgl=((LAYERS, PART_FF, HALF), F32),
    eg=((LAYERS, PART_FF, HALF), BF16),
    sgb=((LAYERS, PART, HALF), BF16),
    fg=((PART, HALF), F32),
    do_t=((PART, HALF), BF16),
    dq_t=((PART, HALF), BF16),
    dk_t=((PART, FULL), BF16),
    dv_t=((PART, FULL), BF16),
    dx_out=((LAYERS, PART, HALF), F32),
    dx_in=((LAYERS, PART, HALF), F32),
    stats=((4 * LAYERS, 4, 16, 128), F32),
    mix_out=((PART, HALF), BF16),
    mix_in=((D, ROWS), BF16),
    tg_out=((PART, HALF), BF16),
    tg_in=((D, ROWS), BF16),
    gs_acc=((2, PART, 128), F32),
    gs_out=((2, 4, 8, 128), F32),
    gs_in=((8, 8, 128), F32),
    gb_m=((LAYERS, 2, 4, 2 * FLAT, 128), BF16),
    gb_o=((LAYERS, 2, 4, FLAT, 128), BF16),
    gb_q=((LAYERS, 8, 3, 2 * UNIT, 128), BF16),
    sb_m=((LAYERS, 4, 2 * FLAT, 128), BF16),
    sb_o=((LAYERS, 4, FLAT, 128), BF16),
    sb_q=((LAYERS, 4, 3, 2 * UNIT, 128), BF16),
    gm_m=((LAYERS, 4, 2 * FLAT, 128), BF16),
    gm_o=((LAYERS, 4, FLAT, 128), BF16),
    gm_q=((LAYERS, 4, 3, 2 * UNIT, 128), BF16),
    rz_m=((LAYERS, 4, 2 * FLAT, 128), BF16),
    rz_o=((LAYERS, 4, FLAT, 128), BF16),
    gf_m=((LAYERS, 2 * FLAT, 128), BF16),
    gf_o=((LAYERS, FLAT, 128), BF16),
    rg_m=((LAYERS, 2 * FLAT, 128), BF16),
    rg_o=((LAYERS, FLAT, 128), BF16),
    rg_q=((LAYERS, 4, 3, 2 * UNIT, 128), BF16),
)


def mm(a, b):
    return jnp.dot(a, b, preferred_element_type=F32)


def mm_nt(a, b):
    return lax.dot_general(a, b, (((1,), (1,)), ((), ())), preferred_element_type=F32)


def turn(v):
    return pltpu.roll(v, 64, axis=1)


def low_lanes(a, b):
    return jnp.where(lax.broadcasted_iota(jnp.int32, a.shape, 1) < 64, a, b)


def every(start, count, step):
    return pl.ds(start, count, stride=step)


def rows_from_triples(first, second, third, left, right):
    count = first.shape[0]
    second_turned, third_turned = turn(second), turn(third)
    left[every(0, count, 2), :] = first
    left[every(1, count, 2), :] = low_lanes(second_turned, third_turned)
    right[every(0, count, 2), :] = second
    right[every(1, count, 2), :] = third_turned


def triples_from_rows(count, left, right):
    turned = turn(left[every(1, count, 2), :])
    first = left[every(0, count, 2), :]
    second = low_lanes(right[every(0, count, 2), :], turned)
    third = low_lanes(turned, turn(right[every(1, count, 2), :]))
    return first, second, third


def matrix_of(units):
    count = units.shape[0]
    wide = units.astype(F32)
    left = wide[:, :UNIT].reshape(UNIT * count, 128)
    right = wide[:, UNIT:].reshape(UNIT * count, 128)
    return jnp.concatenate([left, right[:, :64]], axis=1).astype(BF16)


def units_of(matrix):
    count = matrix.shape[0] // UNIT
    left = matrix[:, :128].reshape(count, UNIT, 128)
    right = jnp.concatenate([matrix[:, 128:], matrix[:, :64]], axis=1).reshape(count, UNIT, 128)
    return jnp.concatenate([left, right], axis=1).astype(BF16)


def erf_pair(v):
    cdf = 0.5 * (1.0 + lax.erf(v * (0.5**0.5)))
    slope = cdf + v * (jnp.exp(-0.5 * v * v) * 0.3989422804014327)
    return cdf, slope


def fast_kernel(
    tokens_at, cotangent_at, length, gains_at, shifts_at, w_qkv_at, w_out_at, w_up_at, w_down_at,
    mixed, tokens_grad, g_qkv, g_out, g_up, g_down, g_norm,
    sems, *scratch,
):
    b = types.SimpleNamespace(**dict(zip(SCRATCH, scratch)))
    p, s = lax.axis_index("dp"), lax.axis_index("seq")
    x, c, z, y = p // 2, p % 2, s // 2, s % 2
    g = 2 * x + y
    seq_here = jnp.where(z == 3, 3, (z + 2) % 3)
    z_mine = jnp.where(p == 3, 3, (p + 1) % 3)
    own = pl.multiple_of(HALF * c, HALF)
    other = pl.multiple_of(HALF * (1 - c), HALF)
    g_rows = pl.multiple_of(PART * g, PART)
    used = [0]
    pending = []

    def new_sems(count=1):
        first = used[0]
        used[0] += count
        assert used[0] <= SEMS
        return first

    def dev(dx, dc, dz, dy):
        return (2 * dx + dc, 2 * dz + dy)

    sibling = dev(x, 1 - c, z, y)
    square = (dev(x, c, z, 1 - y), dev(1 - x, c, z, y), dev(1 - x, c, z, 1 - y))

    def send(src, dst, to, arrive, maybe_here=False):
        copy = pltpu.make_async_remote_copy(
            src, dst, sems.at[new_sems()], sems.at[arrive], device_id=to, device_id_type=MESH
        )
        if not maybe_here:
            copy.start()
            pending.append((copy, None))
            return
        away = jnp.logical_or(to[0] != p, to[1] != s)

        @pl.when(away)
        def _():
            copy.start()

        @pl.when(jnp.logical_not(away))
        def _():
            pltpu.make_async_copy(src, dst, sems.at[arrive]).start()

        pending.append((copy, away))

    def arrived(ref, arrive):
        pltpu.make_async_copy(ref, ref, sems.at[arrive]).wait()

    reads = {}
    for ref, into in (
        (tokens_at, b.tokens), (w_qkv_at, b.w_qkv), (gains_at, b.gains), (shifts_at, b.shifts), (w_out_at, b.w_out),
        (w_up_at, b.w_up), (w_down_at, b.w_down), (cotangent_at, b.cotangent),
    ):
        reads[id(into)] = pltpu.make_async_copy(ref, into, sems.at[new_sems()])
        reads[id(into)].start()

    def read(ref):
        reads[id(ref)].wait()
        return ref

    me = 8 * p + s
    barrier = pltpu.get_barrier_semaphore()

    def greet(i, carry):
        d = (me + i) % NDEV
        pl.semaphore_signal(barrier, inc=1, device_id=(d // 8, d % 8), device_id_type=MESH)
        return carry

    lax.fori_loop(1, NDEV, greet, 0)
    b.ln_out[...] = jnp.full((8, 128), length[0].astype(F32), F32)
    b.tok_t[...] = read(b.tokens)[...].T
    w_qkv = read(b.w_qkv)
    for k in range(108):
        b.raw[2 * k : 2 * k + 2] = w_qkv[:, 128 * k : 128 * (k + 1)].astype(F32)
    for l in range(LAYERS):
        rows_from_triples(*(b.raw[every(l + 2 * i, 36, 6), :] for i in range(3)), b.left, b.right)
        for k in range(3):
            rows = slice(UNIT * k, UNIT * (k + 1))
            b.wq_out[l, k] = jnp.concatenate([b.left[rows], b.right[rows]], axis=0).astype(BF16)
    pl.semaphore_wait(barrier, NDEV - 1)

    level_w = [new_sems() for _ in range(LAYERS)]
    level_q = [new_sems() for _ in range(LAYERS)]
    PARTS = dict(c=(COLS_AT, ROWS_AT - COLS_AT), m=(0, COLS_AT), r=(ROWS_AT, FLAT), q=(QKV_AT, SHARD - QKV_AT))
    along_w = {(name, l): new_sems(3) for l in range(LAYERS) for name in PARTS}
    relay_w = {(name, l): new_sems() for l in range(LAYERS) for name in PARTS}

    def send_level(l):
        to = dev(p // 2, y, z, p % 2)
        into = b.w_in.at[l, y, z]
        send(b.wm_out.at[l], into.at[0:COLS_AT], to, level_w[l], True)
        for cg in range(4):
            row = pl.multiple_of(COLS_AT + 2 * UNIT * p, 16)
            send(b.wc_out.at[l, cg], into.at[pl.ds(row, 2 * UNIT)], dev(cg // 2, y, z, cg % 2), level_w[l], True)
        send(b.wr_out.at[l], into.at[ROWS_AT:QKV_AT], to, level_w[l], True)

    def send_level_qkv(l):
        into = b.w_in.at[l, y, z]
        for k in range(3):
            gg = (3 * me + k) % 32 // 8
            start = QKV_AT + 2 * UNIT * k
            send(b.wq_out.at[l, k], into.at[start : start + 2 * UNIT], dev(gg // 2, y, z, gg % 2), level_q[l], True)

    def level_here(l):
        arrived(b.w_in.at[l, c, z, 0:QKV_AT], level_w[l])

    def level_qkv_here(l):
        arrived(b.w_in.at[l, c, z, QKV_AT:SHARD], level_q[l])

    def send_along(name, l):
        start, count = PARTS[name]
        piece = b.w_in.at[l, c, z, start : start + count]
        for i in range(3):
            send(piece, piece, dev(x, c, (z + i + 1) % 4, y), along_w[name, l] + i)

    def relay(name, l):
        start, count = PARTS[name]
        for i in range(3):
            arrived(b.w_in.at[l, c, (z + 3 - i) % 4, start : start + count], along_w[name, l] + i)
        mine = b.w_in.at[l, c, :, start : start + count]
        send(mine, mine, sibling, relay_w[name, l])

    def relayed(name, l):
        start, count = PARTS[name]
        arrived(b.w_in.at[l, 1 - c, :, start : start + count], relay_w[name, l])

    def send_first():
        send_level_qkv(0)

    tok_sem, len_sem, cot_sem, gn_sem = (new_sems() for _ in range(4))
    half_of = s // 4
    send_first()
    for gg in range(4):
        to = dev(gg // 2, half_of, z_mine, gg % 2)
        lane = pl.multiple_of(ROWS * s, ROWS)
        send(
            b.tok_t.at[pl.ds(PART * gg, PART), :],
            b.x_all.at[0, :, pl.ds(lane, ROWS)],
            to, tok_sem, True,
        )
    len_copies = []
    first_chunk = s % 4 == 0
    for gg in range(4):
        to = dev(gg // 2, half_of, z_mine, gg % 2)
        away = jnp.logical_or(to[0] != p, to[1] != s)
        copy = pltpu.make_async_remote_copy(
            b.ln_out, b.ln_in, sems.at[new_sems()], sems.at[len_sem], device_id=to, device_id_type=MESH
        )

        @pl.when(jnp.logical_and(first_chunk, away))
        def _():
            copy.start()

        @pl.when(jnp.logical_and(first_chunk, jnp.logical_not(away)))
        def _():
            pltpu.make_async_copy(b.ln_out, b.ln_in, sems.at[len_sem]).start()

        pending.append((copy, jnp.logical_and(first_chunk, away)))

    gains, shifts = read(b.gains), read(b.shifts)
    b.gs_acc[...] = jnp.zeros((2, PART, 128), F32)
    norm_rows = [ref[...].astype(F32)[l : l + 1] for l in range(LAYERS) for ref in (gains, shifts)]
    norm_rows = jnp.concatenate(norm_rows + [jnp.zeros((4, 48), F32)], axis=0)
    norm_rows = jnp.concatenate([norm_rows, jnp.zeros((8, 80), F32)], axis=1)
    norm_rows = jnp.concatenate([norm_rows, jnp.zeros((120, 128), F32)], axis=0)
    b.misc[...] = norm_rows.T.astype(BF16)

    b.raw[0:288] = read(b.w_out)[...].astype(F32)
    for l in range(LAYERS):
        b.wr_out[l] = b.raw[every(l, FLAT, 2), :].astype(BF16)
        parts = [b.raw[every(2 * i + l, UNIT, 12), :] for i in range(6)]
        turned = [turn(part) for part in parts]
        pieces = (
            (parts[0], parts[1]),
            (low_lanes(turned[1], turned[2]), turned[2]),
            (parts[3], parts[4]),
            (low_lanes(turned[4], turned[5]), turned[5]),
        )
        for cg in range(4):
            b.wc_out[l, cg] = jnp.concatenate(pieces[cg], axis=0).astype(BF16)
    for i, ref in enumerate((b.w_up, b.w_down)):
        b.raw[0:288] = read(ref)[...].astype(F32)
        for l in range(LAYERS):
            b.wm_out[l, FLAT * i : FLAT * (i + 1)] = b.raw[every(l, FLAT, 2), :].astype(BF16)

    for zz in range(4):
        for cc in range(2):
            gg = 2 * (p % 2) + s // 4
            row = pl.multiple_of(48 * (s % 4), 16)
            send(
                b.misc.at[0:48, :], b.gn_in.at[p // 2, pl.ds(row, 48), :],
                dev(gg // 2, cc, zz, gg % 2), gn_sem, True,
            )
    send_level(0)
    send_level_qkv(1)
    send_level(1)
    level_qkv_here(0)
    send_along("q", 0)
    b.cotown_t[...] = read(b.cotangent)[...].T
    x_sem = [new_sems() for _ in range(LAYERS)]
    x_half = b.x_all.at[0, :, pl.ds(own, HALF)]
    arrived(x_half, tok_sem)
    send(x_half, x_half, sibling, x_sem[0])
    relay("q", 0)
    level_here(0)
    send_along("c", 0)
    send_along("m", 0)
    arrived(b.ln_in, len_sem)
    valid = b.ln_in[0:1, 0:1]
    key_at = lax.broadcasted_iota(jnp.int32, (FULL, 128), 0).astype(F32)
    b.bias[...] = jnp.where(key_at < valid, 0.0, -1e30)

    def gain_shift(l, k):
        columns = b.gn_in[k].astype(F32)
        return columns[:, 2 * l : 2 * l + 1], columns[:, 2 * l + 1 : 2 * l + 2]

    stat_used = [0]

    def exchange(*rows):
        i = stat_used[0]
        stat_used[0] += 1
        buffer = b.stats.at[i]
        count = 4 * len(rows)
        buffer[0, 0:count] = jnp.concatenate(
            [row[:, ROWS * j : ROWS * (j + 1)] for row in rows for j in range(4)], axis=0
        )
        base = new_sems(3)
        for d in range(3):
            send(buffer.at[0, 0:count], buffer.at[d + 1, 0:count], square[d], base + d)

        def finish():
            for d in range(3):
                arrived(buffer.at[d + 1, 0:count], base + d)
            whole = [buffer[d, 0:count] for d in range(4)]
            return [
                [
                    jnp.concatenate([four[4 * i + j : 4 * i + j + 1] for j in range(4)], axis=1)
                    for i in range(len(rows))
                ]
                for four in whole
            ]

        return finish

    def normalize_here(v, name, l, gain, shift, weighted=None):
        mean_here = jnp.sum(v, axis=0, keepdims=True) * (1.0 / PART)
        d = v - mean_here
        rows = [mean_here, jnp.sum(d * d, axis=0, keepdims=True)]
        if weighted is not None:
            rows += [jnp.sum(weighted, axis=0, keepdims=True), jnp.sum(weighted * d, axis=0, keepdims=True)]
        exchanged = exchange(*rows)
        return lambda: normalize_there(exchanged(), v, name, l, gain, shift, weighted)

    def normalize_there(four, v, name, l, gain, shift, weighted):
        mean = (four[0][0] + four[1][0] + four[2][0] + four[3][0]) * 0.25
        total = sum(f[1] + PART * (f[0] - mean) * (f[0] - mean) for f in four)
        factor = lax.rsqrt(total * (1.0 / D) + EPSILON)
        scaled = (v - mean) * factor
        getattr(b, "xh" + name)[l] = scaled
        getattr(b, "r" + name)[l, 0:1] = factor
        result = scaled * gain + shift
        if weighted is None:
            return result
        one = sum(f[2] for f in four) * (1.0 / D)
        two = sum(f[3] + (f[0] - mean) * f[2] for f in four) * factor * (1.0 / D)
        return result, one, two

    def gather_raw(l, start):
        for t in range(8):
            b.raw[FLAT * t : FLAT * (t + 1)] = b.w_in[l, t % 2, t // 2, start : start + FLAT].astype(F32)

    def wide_rows(l, start, into):
        gather_raw(l, start)
        for i in range(6):
            into[:, 128 * i : 128 * (i + 1)] = b.raw[every(i, PART, 6), :].astype(BF16)

    def scatter_raw(ref, start):
        for t in range(8):
            ref[t % 2, t // 2, start : start + FLAT] = b.raw[FLAT * t : FLAT * (t + 1)].astype(BF16)

    def flat_units(matrix, ref, start):
        for i in range(6):
            b.raw[every(i, PART, 6), :] = matrix[:, 128 * i : 128 * (i + 1)]
        scatter_raw(ref, start)

    att_sem = [[new_sems(3) for _ in range(3)] for _ in range(LAYERS)]
    att_send = [[new_sems(3) for _ in range(3)] for _ in range(LAYERS)]

    def send_cotangent():
        for gg in range(4):
            lane = pl.multiple_of(ROWS * (s % 4), ROWS)
            send(
                b.cotown_t.at[pl.ds(PART * gg, PART), :], b.cot_t.at[:, pl.ds(lane, ROWS)],
                dev(gg // 2, half_of, z_mine, gg % 2), cot_sem, True,
            )

    def forward(l):
        x_own = b.x_all[l, :, pl.ds(own, HALF)]
        relayed("q", l)
        for n in range(24):
            rows = slice(UNIT * n, UNIT * (n + 1))
            start = QKV_AT + 2 * UNIT * (n % 3)
            unit = b.w_in[l, n // 3 % 2, n // 6, start : start + 2 * UNIT].astype(F32)
            b.left[rows] = unit[:UNIT]
            b.right[rows] = unit[UNIT:]
        turned = []
        for cc in range(3):
            rows = pl.ds(pl.multiple_of(PART * ((cc + g) % 3), UNIT), PART)
            nat = jnp.concatenate([b.left[rows, :], b.right[rows, :][:, 0:64]], axis=1).astype(BF16)
            b.wn_q[l, cc] = nat
            turned.append(nat.T)
        b.q_t[l] = mm(turned[0], x_own).astype(BF16) * jnp.asarray(0.125, BF16)

        def keys_values(start, part):
            for matrix, name in ((turned[1], "k"), (turned[2], "v")):
                value = mm(matrix, part).astype(BF16)
                getattr(b, name + "_t")[l, :, pl.ds(start, HALF)] = value
                for h in range(HEADS_HERE):
                    getattr(b, name + "_n")[l, h, pl.ds(start, HALF), :] = value[HEAD * h : HEAD * (h + 1)].T

        keys_values(own, x_own)
        arrived(b.x_all.at[l, :, pl.ds(other, HALF)], x_sem[l])
        keys_values(other, b.x_all[l, :, pl.ds(other, HALF)])

        if l == 1:
            send_cotangent()

        def one_head(h, carry):
            head = pl.multiple_of(HEAD * h, HEAD)
            q = b.q_t[l, pl.ds(head, HEAD), :]
            largest = jnp.full((1, HALF), -jnp.inf, F32)
            for kb in range(0, FULL, KEY_BLOCK):
                scores = mm(b.k_n[l, h, kb : kb + KEY_BLOCK, :], q) + b.bias[kb : kb + KEY_BLOCK, 0:1]
                b.s_scr[kb : kb + KEY_BLOCK] = scores
                largest = jnp.maximum(largest, jnp.max(scores, axis=0, keepdims=True))
            total = jnp.zeros((1, HALF), F32)
            for kb in range(0, FULL, KEY_BLOCK):
                powers = jnp.exp(b.s_scr[kb : kb + KEY_BLOCK] - largest)
                total += jnp.sum(powers, axis=0, keepdims=True)
                b.p_t[l, h, kb : kb + KEY_BLOCK] = powers.astype(BF16)
            inverse = 1.0 / total
            b.rinv[l, h, 0:1] = inverse
            out = mm(b.v_t[l, pl.ds(head, HEAD), :], b.p_t[l, h]) * inverse
            b.o_t[l, pl.ds(head, HEAD), :] = out
            rows = pl.ds(pl.multiple_of(g_rows + head, HEAD), HEAD)
            b.att_all[l, rows, :] = out.astype(BF16)
            piece = b.att_all.at[l, rows, :]
            for d in range(3):
                pltpu.make_async_remote_copy(
                    piece, piece, sems.at[att_send[l][d] + h], sems.at[att_sem[l][d] + h],
                    device_id=square[d], device_id_type=MESH,
                ).start()
            return carry

        lax.fori_loop(0, HEADS_HERE, one_head, 0)
        relay("c", l)
        relayed("c", l)
        for r in range(4):
            for t in range(8):
                rows = slice(UNIT * (8 * r + t), UNIT * (8 * r + t + 1))
                start = COLS_AT + 2 * UNIT * r
                unit = b.w_in[l, t % 2, t // 2, start : start + 2 * UNIT].astype(F32)
                b.left[rows] = unit[:UNIT]
                b.right[rows] = unit[UNIT:]
        columns_t = jnp.concatenate([b.left[...], b.right[:, 0:64]], axis=1).astype(BF16).T
        flips = ((0, 1), (1, 0), (1, 1))
        for h in range(HEADS_HERE):
            for d, (fx, fy) in enumerate(flips):
                px = 1 - x if fx else x
                py = 1 - y if fy else y
                start = pl.multiple_of(PART * (2 * px + py) + HEAD * h, HEAD)
                arrived(b.att_all.at[l, pl.ds(start, HEAD), :], att_sem[l][d] + h)
        relay("m", l)
        if l == 0:
            arrived(b.gn_in, gn_sem)
        branch = mm(columns_t, b.att_all[l])
        gain, shift = gain_shift(l, 0)
        finish = normalize_here(x_own.astype(F32) + branch, "1", l, gain, shift)
        relayed("m", l)
        wide_rows(l, 0, b.wn_u.at[l])
        b.wt_u[...] = b.wn_u[l].T
        gather_raw(l, FLAT)
        rows_from_triples(*(b.raw[every(i, PART_FF // 2, 3), :] for i in range(3)), b.left, b.right)
        nat = jnp.concatenate([b.left[...], b.right[:, 0:64]], axis=1).astype(BF16)
        b.wn_d[l] = nat
        down_t = nat.T
        middle = finish().astype(BF16)
        if l == 0:
            level_here(1)
            level_qkv_here(1)
            send_along("q", 1)
            send_along("c", 1)
            send_along("m", 1)
        b.mid[l] = middle

        def one_block(i, carry):
            rows = pl.ds(pl.multiple_of(FF_BLOCK * i, FF_BLOCK), FF_BLOCK)
            expanded = mm(b.wt_u[rows, :], b.mid[l])
            cdf, slope = erf_pair(expanded)
            b.act[l, rows, :] = (expanded * cdf).astype(BF16)
            b.dgl[l, rows, :] = slope
            return carry

        lax.fori_loop(0, PART_FF // FF_BLOCK, one_block, 0)
        second = middle.astype(F32) + mm(down_t, b.act[l])
        gain, shift = gain_shift(l, 1)
        if l + 1 < LAYERS:
            return normalize_here(second, "2", l, gain, shift)()
        arrived(b.cot_t, cot_sem)
        position = lax.broadcasted_iota(jnp.int32, (PART, HALF), 1) + HALF * c
        grad = jnp.where(position.astype(F32) < valid, b.cot_t[...].astype(F32), 0.0)
        return normalize_here(second, "2", l, gain, shift, grad * gain)(), grad

    hidden = forward(0)
    b.x_all[1, :, pl.ds(own, HALF)] = hidden.astype(BF16)
    x_half = b.x_all.at[1, :, pl.ds(own, HALF)]
    send(x_half, x_half, sibling, x_sem[1])
    relay("q", 1)
    send_along("r", 1)
    send_along("r", 0)
    (hidden, one, two), grad = forward(1)

    mix_sem, tg_sem = new_sems(), new_sems()

    def send_back(out_ref, in_ref, arrive):
        for k in range(4):
            send(
                out_ref.at[:, ROWS * k : ROWS * (k + 1)], in_ref.at[pl.ds(g_rows, PART), :],
                (seq_here, 4 * c + k), arrive, True,
            )

    b.mix_out[...] = hidden.astype(BF16)

    half_sem = {(name, l): new_sems() for l in range(LAYERS) for name in "moq"}
    level_sem = {(name, l): new_sems(3) for l in range(LAYERS) for name in "mo"}
    owner_sem = {(name, l): new_sems() for l in range(LAYERS) for name in "moq"}

    def to_sibling(name, l):
        there = pl.ds(4 * (1 - c), 4) if name == "q" else 1 - c
        send(getattr(b, "gb_" + name).at[l, there], getattr(b, "sb_" + name).at[l], sibling, half_sem[name, l])

    def to_level(name, l):
        here, mine = getattr(b, "sb_" + name), getattr(b, "gm_" + name)
        arrived(here.at[l], half_sem[name, l])
        mine[l] = (getattr(b, "gb_" + name)[l, c].astype(F32) + here[l].astype(F32)).astype(BF16)
        for i in range(3):
            there = (z + i + 1) % 4
            send(
                mine.at[l, there], getattr(b, "rz_" + name).at[l, i], dev(x, c, there, y), level_sem[name, l] + i
            )

    def to_owner(name, l):
        four = getattr(b, "rz_" + name)
        for i in range(3):
            arrived(four.at[l, i], level_sem[name, l] + i)
        total = getattr(b, "gm_" + name)[l, z].astype(F32) + sum(four[l, i].astype(F32) for i in range(3))
        final = getattr(b, "gf_" + name)
        final[l] = total.astype(BF16)
        return lambda: send(final.at[l], getattr(b, "rg_" + name).at[l], dev(g // 2, g % 2, z, c), owner_sem[name, l], True)

    def qkv_to_owners(l):
        arrived(b.sb_q.at[l], half_sem["q", l])
        b.gm_q[l] = (b.gb_q[l, pl.ds(4 * c, 4)].astype(F32) + b.sb_q[l].astype(F32)).astype(BF16)
        return lambda: qkv_sends(l)

    def qkv_sends(l):
        for k in range(4):
            for cc in range(3):
                u = 32 * cc + 8 * g + 4 * c + k
                j = u // 3
                send(
                    b.gm_q.at[l, k, cc], b.rg_q.at[l, z, u % 3], (j // 8, j % 8), owner_sem["q", l], True
                )

    lane_at = lax.broadcasted_iota(jnp.int32, (PART, 128), 1)

    def norm_grads(grad, scaled, l, k):
        gain_grad = jnp.sum(grad * scaled, axis=1, keepdims=True)
        shift_grad = jnp.sum(grad, axis=1, keepdims=True)
        b.gs_acc[k] += jnp.where(lane_at == 2 * l, gain_grad, 0.0) + jnp.where(
            lane_at == 2 * l + 1, shift_grad, 0.0
        )

    def normalize_back_here(grad, name, l, k, known=None):
        gain, _ = gain_shift(l, k)
        scaled = getattr(b, "xh" + name)[l]
        weighted = grad * gain
        if known is None:
            finish = exchange(
                jnp.sum(weighted, axis=0, keepdims=True), jnp.sum(weighted * scaled, axis=0, keepdims=True)
            )
            norm_grads(grad, scaled, l, k)
            four = finish()
            one, two = (sum(f[i] for f in four) * (1.0 / D) for i in range(2))
        else:
            one, two = known
        return getattr(b, "r" + name)[l, 0:1] * (weighted - one - scaled * two)

    gs_sem = new_sems()

    def send_norm_grads():
        for k in range(2):
            turned = b.gs_acc[k].T[0:8]
            for q in range(4):
                b.gs_out[k, q] = jnp.concatenate([turned[:, 48 * q : 48 * (q + 1)], jnp.zeros((8, 80), F32)], axis=1)
                send(
                    b.gs_out.at[k, q], b.gs_in.at[2 * z + c], (2 * k + g // 2, 4 * (g % 2) + q), gs_sem, True
                )

    bg_sem = [new_sems(3) for _ in range(LAYERS)]
    dx_sem = [new_sems() for _ in range(LAYERS)]

    def backward(l, grad, known=None):
        relay("r", l)
        second_grad = normalize_back_here(grad, "2", l, 1, known)
        b.sgb[l] = second_grad.astype(BF16)

        def one_block(i, carry):
            rows = pl.ds(pl.multiple_of(FF_BLOCK * i, FF_BLOCK), FF_BLOCK)
            active_grad = mm(b.wn_d[l, rows, :], b.sgb[l])
            b.eg[l, rows, :] = (active_grad * b.dgl[l, rows, :]).astype(BF16)
            return carry

        lax.fori_loop(0, PART_FF // FF_BLOCK, one_block, 0)
        middle_grad = second_grad + mm(b.wn_u[l], b.eg[l])
        first_grad = normalize_back_here(middle_grad, "1", l, 0)
        b.fg[...] = first_grad
        b.bg_all[l, pl.ds(g_rows, PART), :] = first_grad.astype(BF16)
        piece = b.bg_all.at[l, pl.ds(g_rows, PART), :]
        for d in range(3):
            send(piece, piece, square[d], bg_sem[l] + d)
        if known is not None:
            norm_grads(grad, b.xh2[l], l, 1)
        if l == 0:
            send_norm_grads()
        grads = mm_nt(b.act[l], b.sgb[l])
        b.left[...] = grads[:, :128]
        b.right[:, 0:64] = grads[:, 128:]
        for i, part in enumerate(triples_from_rows(PART_FF // 2, b.left, b.right)):
            b.raw[every(i, PART_FF // 2, 3), :] = part
        scatter_raw(b.gb_m.at[l], 0)
        flat_units(mm_nt(b.mid[l], b.eg[l]), b.gb_m.at[l], FLAT)
        to_sibling("m", l)
        if l + 1 < LAYERS:
            later = [qkv_to_owners(l + 1), to_owner("m", l + 1), to_owner("o", l + 1)]
        else:
            later = [lambda: send_back(b.mix_out, b.mix_in, mix_sem)]
        to_level("m", l)
        relayed("r", l)
        wide_rows(l, ROWS_AT, b.wn_r.at[l])
        for d, (fx, fy) in enumerate(((0, 1), (1, 0), (1, 1))):
            px = 1 - x if fx else x
            py = 1 - y if fy else y
            start = pl.multiple_of(PART * (2 * px + py), PART)
            arrived(b.bg_all.at[l, pl.ds(start, PART), :], bg_sem[l] + d)
        att = b.att_all[l, pl.ds(g_rows, PART), :]
        flat_units(mm_nt(att, b.bg_all[l]), b.gb_o.at[l], 0)
        to_sibling("o", l)
        b.do_t[...] = mm(b.wn_r[l], b.bg_all[l]).astype(BF16)
        to_level("o", l)
        for sends in later:
            sends()

        def one_head(h, carry):
            head = pl.multiple_of(HEAD * h, HEAD)
            rows = pl.ds(head, HEAD)
            inverse = b.rinv[l, h, 0:1]
            grad_out = b.do_t[rows, :].astype(F32)
            delta = jnp.sum(grad_out * b.o_t[l, rows, :], axis=0, keepdims=True) * inverse
            grad_scaled = (grad_out * inverse).astype(BF16)
            for kb in range(0, FULL, KEY_BLOCK):
                block = slice(kb, kb + KEY_BLOCK)
                grad_probs = mm(b.v_n[l, h, block, :], grad_scaled)
                b.ds_scr[block] = (b.p_t[l, h, block].astype(F32) * (grad_probs - delta)).astype(BF16)
            b.dq_t[rows, :] = (mm(b.k_t[l, rows, :], b.ds_scr[...]) * 0.125).astype(BF16)
            b.dk_t[rows, :] = mm_nt(b.q_t[l, rows, :], b.ds_scr[...]).astype(BF16)
            b.dv_t[rows, :] = mm_nt(grad_scaled, b.p_t[l, h]).astype(BF16)
            return carry

        lax.fori_loop(0, HEADS_HERE, one_head, 0)
        w_q, w_k, w_v = (b.wn_q[l, cc] for cc in range(3))
        b.dx_out[l] = mm(w_k, b.dk_t[:, pl.ds(other, HALF)]) + mm(w_v, b.dv_t[:, pl.ds(other, HALF)])
        send(b.dx_out.at[l], b.dx_in.at[l], sibling, dx_sem[l])
        x_own = b.x_all[l, :, pl.ds(own, HALF)]
        b.gb_q[l, :, 0] = units_of(mm_nt(x_own, b.dq_t[...]))
        b.gb_q[l, :, 1] = units_of(mm_nt(b.x_all[l], b.dk_t[...]))
        b.gb_q[l, :, 2] = units_of(mm_nt(b.x_all[l], b.dv_t[...]))
        to_sibling("q", l)
        here = mm(w_q, b.dq_t[...])
        here += mm(w_k, b.dk_t[:, pl.ds(own, HALF)]) + mm(w_v, b.dv_t[:, pl.ds(own, HALF)])
        arrived(b.dx_in.at[l], dx_sem[l])
        return b.fg[...] + here + b.dx_in[l]

    grad = backward(1, grad, (one, two))
    grad = backward(0, grad)
    b.tg_out[...] = grad.astype(BF16)
    send_back(b.tg_out, b.tg_in, tg_sem)
    qkv_to_owners(0)()
    to_owner("m", 0)()
    to_owner("o", 0)()

    arrived(b.mix_in, mix_sem)
    mixed[...] = b.mix_in[...].T
    for l in reversed(range(LAYERS)):
        arrived(b.rg_m.at[l], owner_sem["m", l])
        g_down[every(l, FLAT, 2), :] = b.rg_m[l, 0:FLAT].astype(F32)
        g_up[every(l, FLAT, 2), :] = b.rg_m[l, FLAT : 2 * FLAT].astype(F32)
        arrived(b.rg_o.at[l], owner_sem["o", l])
        g_out[every(l, FLAT, 2), :] = b.rg_o[l].astype(F32)
        arrived(b.rg_q.at[l], owner_sem["q", l])
        total = sum(b.rg_q[l, i].astype(F32) for i in range(4))
        b.left[0:72] = total[:, :UNIT].reshape(72, 128)
        b.right[0:72] = total[:, UNIT:].reshape(72, 128)
        for i, part in enumerate(triples_from_rows(36, b.left, b.right)):
            b.raw[every(l + 2 * i, 36, 6), :] = part
    arrived(b.tg_in, tg_sem)
    tokens_grad[...] = b.tg_in[...].T
    arrived(b.gs_in, gs_sem)
    g_norm[...] = sum(b.gs_in[i] for i in range(8))

    for k in range(108):
        g_qkv[:, 128 * k : 128 * (k + 1)] = b.raw[2 * k : 2 * k + 2]

    for copy, when in pending:
        if when is None:
            copy.wait_send()
        else:
            pl.when(when)(copy.wait_send)
    for l in range(LAYERS):
        for h in range(HEADS_HERE):
            for d in range(3):
                piece = b.att_all.at[l, pl.ds(pl.multiple_of(g_rows + HEAD * h, HEAD), HEAD), :]
                pltpu.make_async_remote_copy(
                    piece, piece, sems.at[att_send[l][d] + h], sems.at[att_sem[l][d] + h],
                    device_id=square[d], device_id_type=MESH,
                ).wait_send()


def hand_over(*refs):
    plain, norms, outs = refs[:6], refs[6], refs[7:]
    for ref, out in zip(plain, outs):
        out[...] = ref[...]
    for k in range(2):
        for l in range(LAYERS):
            outs[6 + k][l : l + 1, :] = norms[2 * l + k : 2 * l + k + 1, 0 : PART // 4]


def fast_device(
    tokens, lengths, qkv_weight, out_weight, up_weight, down_weight, norm_gain, norm_shift, cotangent
):
    def raw(array):
        return array.reshape(LAYERS, -1, 128).transpose(1, 0, 2).reshape(-1, 128)

    def unraw(array):
        return array.reshape(-1, LAYERS, 128).transpose(1, 0, 2).reshape(LAYERS, -1)

    operands = (
        tokens[0],
        cotangent[0],
        lengths,
        norm_gain,
        norm_shift,
        qkv_weight,
        raw(out_weight),
        raw(up_weight),
        raw(down_weight),
    )
    vmem = pl.BlockSpec(memory_space=pltpu.VMEM)
    anywhere = pl.BlockSpec(memory_space=pl.ANY)
    shapes = (
        ((ROWS, D), BF16),
        ((ROWS, D), BF16),
        ((LAYERS, 3 * UNIT * PART), F32),
        ((LAYERS * FLAT, 128), F32),
        ((LAYERS * FLAT, 128), F32),
        ((LAYERS * FLAT, 128), F32),
        ((8, 128), F32),
    )
    mixed, tokens_grad, g_qkv, g_out, g_up, g_down, g_norm = pl.pallas_call(
        fast_kernel,
        out_shape=tuple(jax.ShapeDtypeStruct(*shape) for shape in shapes),
        in_specs=[anywhere] * 2 + [pl.BlockSpec(memory_space=pltpu.SMEM)] + [anywhere] * 6,
        out_specs=tuple([vmem] * len(shapes)),
        scratch_shapes=[pltpu.SemaphoreType.DMA((SEMS,))] + [pltpu.VMEM(*entry) for entry in SCRATCH.values()],
        compiler_params=pltpu.CompilerParams(
            collective_id=0, has_side_effects=True, vmem_limit_bytes=60 * 2**20
        ),
        name="encoder",
    )(*operands)
    results = (mixed, tokens_grad, g_qkv, g_out, g_up, g_down)
    shapes = [jax.ShapeDtypeStruct(array.shape, array.dtype) for array in results]
    shapes += [jax.ShapeDtypeStruct((LAYERS, PART // 4), F32)] * 2
    mixed, tokens_grad, g_qkv, g_out, g_up, g_down, g_gain, g_shift = pl.pallas_call(
        hand_over,
        out_shape=tuple(shapes),
        in_specs=[vmem] * (len(results) + 1),
        out_specs=tuple([vmem] * len(shapes)),
        name="hand_over",
    )(*results, g_norm)
    return (
        mixed[None],
        tokens_grad[None],
        g_qkv,
        unraw(g_out),
        unraw(g_up),
        unraw(g_down),
        g_gain,
        g_shift,
    )


def solution(mesh):
    small = (mesh.shape["dp"], mesh.shape["seq"]) == (4, 8)
    return jax.shard_map(
        fast_device if small else per_device,
        mesh=mesh,
        in_specs=(
            P("dp", "seq", None),
            P("dp"),
            P(None, ("dp", "seq")),
            P(None, ("dp", "seq")),
            P(None, ("dp", "seq")),
            P(None, ("dp", "seq")),
            P(None, ("dp", "seq")),
            P(None, ("dp", "seq")),
            P("dp", "seq", None),
        ),
        out_specs=(
            P("dp", "seq", None),
            P("dp", "seq", None),
            P(None, ("dp", "seq")),
            P(None, ("dp", "seq")),
            P(None, ("dp", "seq")),
            P(None, ("dp", "seq")),
            P(None, ("dp", "seq")),
            P(None, ("dp", "seq")),
        ),
        check_vma=False,
    )
```

```python
import types
from functools import partial

import jax
import jax.numpy as jnp
from jax import lax
from jax.experimental import pallas as pl
from jax.experimental.pallas import tpu as pltpu
from jax.sharding import PartitionSpec as P

D = 768
HEADS = 12
HEAD = 64
FF = 3072
GROUPS = 4


EPSILON = 1e-06


def grouped(inputs, weight):
    count = inputs.shape[0]
    shaped = inputs.reshape(count, weight.shape[0], -1)
    result = jnp.einsum("tgi,gio->tgo", shaped, weight, preferred_element_type=jnp.float32)
    return result.reshape(count, -1)


def normalize(values, gain, shift):
    center = values - jnp.mean(values, axis=-1, keepdims=True)
    factor = lax.rsqrt(jnp.mean(center * center, axis=-1, keepdims=True) + EPSILON)
    scaled = center * factor
    return (scaled * gain + shift, scaled, factor)


def normalize_back(grad_out, scaled, factor, gain):
    weighted = grad_out * gain
    grad_in = factor * (
        weighted
        - jnp.mean(weighted, axis=-1, keepdims=True)
        - scaled * jnp.mean(weighted * scaled, axis=-1, keepdims=True)
    )
    return (grad_in, jnp.sum(grad_out * scaled, axis=0), jnp.sum(grad_out, axis=0))


def unpack(pieces):
    qkv_flat, out_flat, up_flat, down_flat, gain_flat, shift_flat = pieces
    part = D // GROUPS
    part_ff = FF // GROUPS
    return (
        qkv_flat.reshape(3, GROUPS, part, part),
        out_flat.reshape(D, D),
        up_flat.reshape(GROUPS, part, part_ff),
        down_flat.reshape(GROUPS, part_ff, part),
        gain_flat.reshape(2, D).astype(jnp.float32),
        shift_flat.reshape(2, D).astype(jnp.float32),
    )


def project_heads(rows, matrices):
    total_rows = rows.shape[0]
    part = D // GROUPS
    result = jnp.einsum(
        "tgi,cgio->ctgo",
        rows.reshape(total_rows, GROUPS, part),
        matrices,
        preferred_element_type=jnp.float32,
    ).astype(jnp.bfloat16)
    return result.reshape(matrices.shape[0], total_rows, HEADS, HEAD).transpose(0, 2, 1, 3)


def head_forward(key_ok, scaling, pieces):
    query_head, key_head, value_head = pieces
    scores = (
        jnp.einsum("td,sd->ts", query_head, key_head, preferred_element_type=jnp.float32) * scaling
    )
    scores = jnp.where(key_ok[None, :], scores, -1e30)
    largest = jnp.max(scores, axis=-1, keepdims=True)
    powers = jnp.exp(scores - largest)
    total = jnp.sum(powers, axis=-1, keepdims=True)
    probs = (powers / total).astype(jnp.bfloat16)
    result = jnp.dot(probs, value_head, preferred_element_type=jnp.float32)
    return (result, (largest + jnp.log(total))[:, 0])


def head_backward(key_ok, scaling, pieces):
    query_head, key_head, value_head, grad_head, log_total = pieces
    scores = (
        jnp.einsum("td,sd->ts", query_head, key_head, preferred_element_type=jnp.float32) * scaling
    )
    scores = jnp.where(key_ok[None, :], scores, -1e30)
    probs = jnp.exp(scores - log_total[:, None])
    grad_probs = jnp.einsum("td,sd->ts", grad_head, value_head, preferred_element_type=jnp.float32)
    delta_row = jnp.sum(probs * grad_probs, axis=-1, keepdims=True)
    grad_scores = (probs * (grad_probs - delta_row)).astype(jnp.bfloat16)
    grad_query = jnp.dot(grad_scores, key_head, preferred_element_type=jnp.float32) * scaling
    grad_key = (
        jnp.einsum("ts,td->sd", grad_scores, query_head, preferred_element_type=jnp.float32)
        * scaling
    )
    grad_value = jnp.einsum(
        "ts,td->sd", probs.astype(jnp.bfloat16), grad_head, preferred_element_type=jnp.float32
    )
    return (grad_query, grad_key, grad_value)


def per_device(
    tokens,
    lengths,
    qkv_weight,
    out_weight,
    up_weight,
    down_weight,
    norm_gain,
    norm_shift,
    cotangent,
):
    layers = qkv_weight.shape[0]
    count = tokens.shape[1]
    slots = count * lax.axis_size("seq")
    first_slot = lax.axis_index("seq") * count
    length = lengths[0]
    key_ok = jnp.arange(slots, dtype=jnp.int32) < length
    row_ok = first_slot + jnp.arange(count, dtype=jnp.int32) < length
    scaling = HEAD ** (-0.5)
    part = D // GROUPS
    part_ff = FF // GROUPS
    hidden_low = tokens[0]
    saved = []
    for layer_index in range(layers):
        gathered = (
            lax.all_gather(qkv_weight[layer_index], ("dp", "seq"), axis=0, tiled=True),
            lax.all_gather(out_weight[layer_index], ("dp", "seq"), axis=0, tiled=True),
            lax.all_gather(up_weight[layer_index], ("dp", "seq"), axis=0, tiled=True),
            lax.all_gather(down_weight[layer_index], ("dp", "seq"), axis=0, tiled=True),
            lax.all_gather(norm_gain[layer_index], ("dp", "seq"), axis=0, tiled=True),
            lax.all_gather(norm_shift[layer_index], ("dp", "seq"), axis=0, tiled=True),
        )
        project, out_matrix, up_matrix, down_matrix, gains, shifts = unpack(gathered)
        heads = project_heads(hidden_low, project)
        key_all, value_all = (
            lax.all_gather(heads[1], "seq", axis=1, tiled=True),
            lax.all_gather(heads[2], "seq", axis=1, tiled=True),
        )
        attended, log_total = lax.map(
            partial(head_forward, key_ok, scaling), (heads[0], key_all, value_all)
        )
        attended_low = attended.transpose(1, 0, 2).reshape(count, D).astype(jnp.bfloat16)
        branch = jnp.dot(attended_low, out_matrix, preferred_element_type=jnp.float32)
        middle, scaled_one, factor_one = normalize(
            hidden_low.astype(jnp.float32) + branch, gains[0], shifts[0]
        )
        middle_low = middle.astype(jnp.bfloat16)
        expanded = grouped(middle_low, up_matrix)
        activated = jax.nn.gelu(expanded, approximate=False).astype(jnp.bfloat16)
        shrunk = grouped(activated, down_matrix)
        output, scaled_two, factor_two = normalize(
            middle_low.astype(jnp.float32) + shrunk, gains[1], shifts[1]
        )
        kept = None
        saved.append(
            (
                hidden_low,
                heads,
                log_total,
                attended_low,
                middle_low,
                expanded,
                activated,
                scaled_one,
                factor_one,
                scaled_two,
                factor_two,
                kept,
            )
        )
        hidden_low = output.astype(jnp.bfloat16)
    mixed = hidden_low[None]
    grad_hidden = cotangent[0].astype(jnp.float32) * row_ok[:, None].astype(jnp.float32)
    owned_list = []
    for layer_index in reversed(range(layers)):
        (
            inputs_low,
            heads,
            log_total,
            attended_low,
            middle_low,
            expanded,
            activated,
            scaled_one,
            factor_one,
            scaled_two,
            factor_two,
            kept,
        ) = saved[layer_index]
        gathered = (
            lax.all_gather(qkv_weight[layer_index], ("dp", "seq"), axis=0, tiled=True),
            lax.all_gather(out_weight[layer_index], ("dp", "seq"), axis=0, tiled=True),
            lax.all_gather(up_weight[layer_index], ("dp", "seq"), axis=0, tiled=True),
            lax.all_gather(down_weight[layer_index], ("dp", "seq"), axis=0, tiled=True),
            lax.all_gather(norm_gain[layer_index], ("dp", "seq"), axis=0, tiled=True),
            lax.all_gather(norm_shift[layer_index], ("dp", "seq"), axis=0, tiled=True),
        )
        project, out_matrix, up_matrix, down_matrix, gains, shifts = unpack(gathered)
        key_all, value_all = (
            lax.all_gather(heads[1], "seq", axis=1, tiled=True),
            lax.all_gather(heads[2], "seq", axis=1, tiled=True),
        )
        grad_two, gain_two, shift_two = normalize_back(
            grad_hidden, scaled_two, factor_two, gains[1]
        )
        shrunk_grad = grad_two.astype(jnp.bfloat16).reshape(count, GROUPS, part)
        down_terms = jnp.einsum(
            "tgf,tgo->gfo",
            activated.reshape(count, GROUPS, part_ff),
            shrunk_grad,
            preferred_element_type=jnp.float32,
        )
        active_grad = jnp.einsum(
            "tgo,gfo->tgf", shrunk_grad, down_matrix, preferred_element_type=jnp.float32
        ).reshape(count, FF)
        unused_value, gelu_pull = jax.vjp(partial(jax.nn.gelu, approximate=False), expanded)
        expanded_grad = (
            gelu_pull(active_grad)[0].astype(jnp.bfloat16).reshape(count, GROUPS, part_ff)
        )
        up_terms = jnp.einsum(
            "tgi,tgf->gif",
            middle_low.reshape(count, GROUPS, part),
            expanded_grad,
            preferred_element_type=jnp.float32,
        )
        middle_grad = grad_two + jnp.einsum(
            "tgf,gif->tgi", expanded_grad, up_matrix, preferred_element_type=jnp.float32
        ).reshape(count, D)
        grad_one, gain_one, shift_one = normalize_back(
            middle_grad, scaled_one, factor_one, gains[0]
        )
        branch_grad = grad_one.astype(jnp.bfloat16)
        out_terms = jnp.einsum(
            "ti,to->io", attended_low, branch_grad, preferred_element_type=jnp.float32
        )
        attended_grad = jnp.einsum(
            "to,io->ti", branch_grad, out_matrix, preferred_element_type=jnp.float32
        ).astype(jnp.bfloat16)
        grad_heads = attended_grad.reshape(count, HEADS, HEAD).transpose(1, 0, 2)
        grad_query, key_terms, value_terms = lax.map(
            partial(head_backward, key_ok, scaling),
            (heads[0], key_all, value_all, grad_heads, log_total),
        )
        grad_key, grad_value = (
            lax.psum_scatter(
                key_terms.astype(jnp.bfloat16), "seq", scatter_dimension=1, tiled=True
            ).astype(jnp.float32),
            lax.psum_scatter(
                value_terms.astype(jnp.bfloat16), "seq", scatter_dimension=1, tiled=True
            ).astype(jnp.float32),
        )
        grad_projected = jnp.stack((grad_query, grad_key, grad_value)).astype(jnp.bfloat16)
        grad_projected = grad_projected.transpose(0, 2, 1, 3).reshape(3, count, GROUPS, part)
        qkv_terms = jnp.einsum(
            "tgi,ctgo->cgio",
            inputs_low.reshape(count, GROUPS, part),
            grad_projected,
            preferred_element_type=jnp.float32,
        )
        grad_hidden = grad_one + jnp.einsum(
            "ctgo,cgio->tgi", grad_projected, project, preferred_element_type=jnp.float32
        ).reshape(count, D)
        owned = (
            lax.psum_scatter(qkv_terms.reshape(-1), ("dp", "seq"), scatter_dimension=0, tiled=True),
            lax.psum_scatter(out_terms.reshape(-1), ("dp", "seq"), scatter_dimension=0, tiled=True),
            lax.psum_scatter(up_terms.reshape(-1), ("dp", "seq"), scatter_dimension=0, tiled=True),
            lax.psum_scatter(
                down_terms.reshape(-1), ("dp", "seq"), scatter_dimension=0, tiled=True
            ),
            lax.psum_scatter(
                jnp.stack((gain_one, gain_two)).reshape(-1),
                ("dp", "seq"),
                scatter_dimension=0,
                tiled=True,
            ),
            lax.psum_scatter(
                jnp.stack((shift_one, shift_two)).reshape(-1),
                ("dp", "seq"),
                scatter_dimension=0,
                tiled=True,
            ),
        )
        owned_list.insert(0, owned)
    tokens_grad = grad_hidden.astype(jnp.bfloat16)[None]
    stacked = tuple((jnp.stack([entry[member] for entry in owned_list]) for member in range(6)))
    return (
        mixed,
        tokens_grad,
        stacked[0],
        stacked[1],
        stacked[2],
        stacked[3],
        stacked[4],
        stacked[5],
    )


F32 = jnp.float32
BF16 = jnp.bfloat16
PART = D // GROUPS
PART_FF = FF // GROUPS
LAYERS = 2
ROWS = 128
HALF = 4 * ROWS
FULL = 2 * HALF
NDEV = 32
UNIT = PART // 8
FLAT = UNIT * PART_FF // 128
COLS_AT = 2 * FLAT
ROWS_AT = COLS_AT + GROUPS * 2 * UNIT
QKV_AT = ROWS_AT + FLAT
SHARD = QKV_AT + 3 * 2 * UNIT
HEADS_HERE = HEADS // GROUPS
KEY_BLOCK = 256
FF_BLOCK = 256
SEMS = 512
MESH = pl.DeviceIdType.MESH

SCRATCH = dict(
    tokens=((ROWS, D), BF16),
    w_qkv=((LAYERS, 3 * UNIT * PART), BF16),
    gains=((LAYERS, PART // 4), BF16),
    shifts=((LAYERS, PART // 4), BF16),
    w_out=((LAYERS * FLAT, 128), BF16),
    w_up=((LAYERS * FLAT, 128), BF16),
    w_down=((LAYERS * FLAT, 128), BF16),
    cotangent=((ROWS, D), BF16),
    x_all=((LAYERS, PART, FULL), BF16),
    cot_t=((PART, HALF), BF16),
    tok_t=((D, ROWS), BF16),
    cotown_t=((D, ROWS), BF16),
    ln_in=((8, 128), F32),
    gn_in=((2, PART, 128), BF16),
    misc=((128, 128), BF16),
    ln_out=((8, 128), F32),
    wq_out=((LAYERS, 3, 2 * UNIT, 128), BF16),
    wc_out=((LAYERS, GROUPS, 2 * UNIT, 128), BF16),
    wr_out=((LAYERS, FLAT, 128), BF16),
    wm_out=((LAYERS, 2 * FLAT, 128), BF16),
    w_in=((LAYERS, 2, 4, SHARD, 128), BF16),
    raw=((8 * FLAT, 128), F32),
    left=((PART_FF, 128), F32),
    right=((PART_FF, 128), F32),
    wn_q=((LAYERS, 3, PART, PART), BF16),
    wn_r=((LAYERS, PART, D), BF16),
    wn_u=((LAYERS, PART, PART_FF), BF16),
    wn_d=((LAYERS, PART_FF, PART), BF16),
    wt_u=((PART_FF, PART), BF16),
    bias=((FULL, 128), F32),
    q_t=((LAYERS, PART, HALF), BF16),
    k_t=((LAYERS, PART, FULL), BF16),
    v_t=((LAYERS, PART, FULL), BF16),
    k_n=((LAYERS, HEADS_HERE, FULL, HEAD), BF16),
    v_n=((LAYERS, HEADS_HERE, FULL, HEAD), BF16),
    p_t=((LAYERS, HEADS_HERE, FULL, HALF), BF16),
    rinv=((LAYERS, HEADS_HERE, 8, HALF), F32),
    s_scr=((FULL, HALF), F32),
    ds_scr=((FULL, HALF), BF16),
    o_t=((LAYERS, PART, HALF), F32),
    att_all=((LAYERS, D, HALF), BF16),
    bg_all=((LAYERS, D, HALF), BF16),
    xh1=((LAYERS, PART, HALF), F32),
    xh2=((LAYERS, PART, HALF), F32),
    r1=((LAYERS, 8, HALF), F32),
    r2=((LAYERS, 8, HALF), F32),
    mid=((LAYERS, PART, HALF), BF16),
    act=((LAYERS, PART_FF, HALF), BF16),
    dgl=((LAYERS, PART_FF, HALF), F32),
    eg=((LAYERS, PART_FF, HALF), BF16),
    sgb=((LAYERS, PART, HALF), BF16),
    fg=((PART, HALF), F32),
    do_t=((PART, HALF), BF16),
    dq_t=((PART, HALF), BF16),
    dk_t=((PART, FULL), BF16),
    dv_t=((PART, FULL), BF16),
    dx_out=((LAYERS, PART, HALF), F32),
    dx_in=((LAYERS, PART, HALF), F32),
    stats=((4 * LAYERS, 4, 16, 128), F32),
    mix_out=((PART, HALF), BF16),
    mix_in=((D, ROWS), BF16),
    tg_out=((PART, HALF), BF16),
    tg_in=((D, ROWS), BF16),
    gs_acc=((2, PART, 128), F32),
    gs_out=((2, 4, 8, 128), F32),
    gs_in=((8, 8, 128), F32),
    gb_m=((LAYERS, 2, 4, 2 * FLAT, 128), BF16),
    gb_o=((LAYERS, 2, 4, FLAT, 128), BF16),
    gb_q=((LAYERS, 8, 3, 2 * UNIT, 128), BF16),
    sb_m=((LAYERS, 4, 2 * FLAT, 128), BF16),
    sb_o=((LAYERS, 4, FLAT, 128), BF16),
    sb_q=((LAYERS, 4, 3, 2 * UNIT, 128), BF16),
    gm_m=((LAYERS, 4, 2 * FLAT, 128), BF16),
    gm_o=((LAYERS, 4, FLAT, 128), BF16),
    gm_q=((LAYERS, 4, 3, 2 * UNIT, 128), BF16),
    rz_m=((LAYERS, 4, 2 * FLAT, 128), BF16),
    rz_o=((LAYERS, 4, FLAT, 128), BF16),
    gf_m=((LAYERS, 2 * FLAT, 128), BF16),
    gf_o=((LAYERS, FLAT, 128), BF16),
    rg_m=((LAYERS, 2 * FLAT, 128), BF16),
    rg_o=((LAYERS, FLAT, 128), BF16),
    rg_q=((LAYERS, 4, 3, 2 * UNIT, 128), BF16),
)


def mm(a, b):
    return jnp.dot(a, b, preferred_element_type=F32)


def mm_nt(a, b):
    return lax.dot_general(a, b, (((1,), (1,)), ((), ())), preferred_element_type=F32)


def turn(v):
    return pltpu.roll(v, 64, axis=1)


def low_lanes(a, b):
    return jnp.where(lax.broadcasted_iota(jnp.int32, a.shape, 1) < 64, a, b)


def every(start, count, step):
    return pl.ds(start, count, stride=step)


def rows_from_triples(first, second, third, left, right):
    count = first.shape[0]
    second_turned, third_turned = turn(second), turn(third)
    left[every(0, count, 2), :] = first
    left[every(1, count, 2), :] = low_lanes(second_turned, third_turned)
    right[every(0, count, 2), :] = second
    right[every(1, count, 2), :] = third_turned


def triples_from_rows(count, left, right):
    turned = turn(left[every(1, count, 2), :])
    first = left[every(0, count, 2), :]
    second = low_lanes(right[every(0, count, 2), :], turned)
    third = low_lanes(turned, turn(right[every(1, count, 2), :]))
    return first, second, third


def matrix_of(units):
    count = units.shape[0]
    wide = units.astype(F32)
    left = wide[:, :UNIT].reshape(UNIT * count, 128)
    right = wide[:, UNIT:].reshape(UNIT * count, 128)
    return jnp.concatenate([left, right[:, :64]], axis=1).astype(BF16)


def units_of(matrix):
    count = matrix.shape[0] // UNIT
    left = matrix[:, :128].reshape(count, UNIT, 128)
    right = jnp.concatenate([matrix[:, 128:], matrix[:, :64]], axis=1).reshape(count, UNIT, 128)
    return jnp.concatenate([left, right], axis=1).astype(BF16)


def erf_pair(v):
    cdf = 0.5 * (1.0 + lax.erf(v * (0.5**0.5)))
    slope = cdf + v * (jnp.exp(-0.5 * v * v) * 0.3989422804014327)
    return cdf, slope


def fast_kernel(
    tokens_at, cotangent_at, length, gains_at, shifts_at, w_qkv_at, w_out_at, w_up_at, w_down_at,
    mixed, tokens_grad, g_qkv, g_out, g_up, g_down, g_gain, g_shift,
    sems, *scratch,
):
    b = types.SimpleNamespace(**dict(zip(SCRATCH, scratch)))
    p, s = lax.axis_index("dp"), lax.axis_index("seq")
    x, c, z, y = p // 2, p % 2, s // 2, s % 2
    g = 2 * x + y
    seq_here = jnp.where(z == 3, 3, (z + 2) % 3)
    z_mine = jnp.where(p == 3, 3, (p + 1) % 3)
    own = pl.multiple_of(HALF * c, HALF)
    other = pl.multiple_of(HALF * (1 - c), HALF)
    g_rows = pl.multiple_of(PART * g, PART)
    used = [0]
    pending = []

    def new_sems(count=1):
        first = used[0]
        used[0] += count
        assert used[0] <= SEMS
        return first

    def dev(dx, dc, dz, dy):
        return (2 * dx + dc, 2 * dz + dy)

    sibling = dev(x, 1 - c, z, y)
    square = (dev(x, c, z, 1 - y), dev(1 - x, c, z, y), dev(1 - x, c, z, 1 - y))

    def send(src, dst, to, arrive, maybe_here=False):
        copy = pltpu.make_async_remote_copy(
            src, dst, sems.at[new_sems()], sems.at[arrive], device_id=to, device_id_type=MESH
        )
        if not maybe_here:
            copy.start()
            pending.append((copy, None))
            return
        away = jnp.logical_or(to[0] != p, to[1] != s)

        @pl.when(away)
        def _():
            copy.start()

        @pl.when(jnp.logical_not(away))
        def _():
            pltpu.make_async_copy(src, dst, sems.at[arrive]).start()

        pending.append((copy, away))

    def arrived(ref, arrive):
        pltpu.make_async_copy(ref, ref, sems.at[arrive]).wait()

    reads = {}
    for ref, into in (
        (tokens_at, b.tokens), (w_qkv_at, b.w_qkv), (gains_at, b.gains), (shifts_at, b.shifts), (w_out_at, b.w_out),
        (w_up_at, b.w_up), (w_down_at, b.w_down), (cotangent_at, b.cotangent),
    ):
        reads[id(into)] = pltpu.make_async_copy(ref, into, sems.at[new_sems()])
        reads[id(into)].start()

    def read(ref):
        reads[id(ref)].wait()
        return ref

    me = 8 * p + s
    barrier = pltpu.get_barrier_semaphore()

    def greet(i, carry):
        d = (me + i) % NDEV
        pl.semaphore_signal(barrier, inc=1, device_id=(d // 8, d % 8), device_id_type=MESH)
        return carry

    lax.fori_loop(1, NDEV, greet, 0)
    b.ln_out[...] = jnp.full((8, 128), length[0].astype(F32), F32)
    b.tok_t[...] = read(b.tokens)[...].T
    w_qkv = read(b.w_qkv)
    for k in range(108):
        b.raw[2 * k : 2 * k + 2] = w_qkv[:, 128 * k : 128 * (k + 1)].astype(F32)
    for l in range(LAYERS):
        rows_from_triples(*(b.raw[every(l + 2 * i, 36, 6), :] for i in range(3)), b.left, b.right)
        for k in range(3):
            rows = slice(UNIT * k, UNIT * (k + 1))
            b.wq_out[l, k] = jnp.concatenate([b.left[rows], b.right[rows]], axis=0).astype(BF16)
    pl.semaphore_wait(barrier, NDEV - 1)

    level_w = [new_sems() for _ in range(LAYERS)]
    level_q = [new_sems() for _ in range(LAYERS)]
    PARTS = dict(c=(COLS_AT, ROWS_AT - COLS_AT), m=(0, COLS_AT), r=(ROWS_AT, FLAT), q=(QKV_AT, SHARD - QKV_AT))
    along_w = {(name, l): new_sems(3) for l in range(LAYERS) for name in PARTS}
    relay_w = {(name, l): new_sems() for l in range(LAYERS) for name in PARTS}

    def send_level(l):
        to = dev(p // 2, y, z, p % 2)
        into = b.w_in.at[l, y, z]
        send(b.wm_out.at[l], into.at[0:COLS_AT], to, level_w[l], True)
        for cg in range(4):
            row = pl.multiple_of(COLS_AT + 2 * UNIT * p, 16)
            send(b.wc_out.at[l, cg], into.at[pl.ds(row, 2 * UNIT)], dev(cg // 2, y, z, cg % 2), level_w[l], True)
        send(b.wr_out.at[l], into.at[ROWS_AT:QKV_AT], to, level_w[l], True)

    def send_level_qkv(l):
        into = b.w_in.at[l, y, z]
        for k in range(3):
            gg = (3 * me + k) % 32 // 8
            start = QKV_AT + 2 * UNIT * k
            send(b.wq_out.at[l, k], into.at[start : start + 2 * UNIT], dev(gg // 2, y, z, gg % 2), level_q[l], True)

    def level_here(l):
        arrived(b.w_in.at[l, c, z, 0:QKV_AT], level_w[l])

    def level_qkv_here(l):
        arrived(b.w_in.at[l, c, z, QKV_AT:SHARD], level_q[l])

    def send_along(name, l):
        start, count = PARTS[name]
        piece = b.w_in.at[l, c, z, start : start + count]
        for i in range(3):
            send(piece, piece, dev(x, c, (z + i + 1) % 4, y), along_w[name, l] + i)

    def relay(name, l):
        start, count = PARTS[name]
        for i in range(3):
            arrived(b.w_in.at[l, c, (z + 3 - i) % 4, start : start + count], along_w[name, l] + i)
        mine = b.w_in.at[l, c, :, start : start + count]
        send(mine, mine, sibling, relay_w[name, l])

    def relayed(name, l):
        start, count = PARTS[name]
        arrived(b.w_in.at[l, 1 - c, :, start : start + count], relay_w[name, l])

    def send_first():
        send_level_qkv(0)

    tok_sem, len_sem, cot_sem, gn_sem = (new_sems() for _ in range(4))
    half_of = s // 4
    send_first()
    for gg in range(4):
        to = dev(gg // 2, half_of, z_mine, gg % 2)
        lane = pl.multiple_of(ROWS * s, ROWS)
        send(
            b.tok_t.at[pl.ds(PART * gg, PART), :],
            b.x_all.at[0, :, pl.ds(lane, ROWS)],
            to, tok_sem, True,
        )
    len_copies = []
    first_chunk = s % 4 == 0
    for gg in range(4):
        to = dev(gg // 2, half_of, z_mine, gg % 2)
        away = jnp.logical_or(to[0] != p, to[1] != s)
        copy = pltpu.make_async_remote_copy(
            b.ln_out, b.ln_in, sems.at[new_sems()], sems.at[len_sem], device_id=to, device_id_type=MESH
        )

        @pl.when(jnp.logical_and(first_chunk, away))
        def _():
            copy.start()

        @pl.when(jnp.logical_and(first_chunk, jnp.logical_not(away)))
        def _():
            pltpu.make_async_copy(b.ln_out, b.ln_in, sems.at[len_sem]).start()

        pending.append((copy, jnp.logical_and(first_chunk, away)))

    gains, shifts = read(b.gains), read(b.shifts)
    b.gs_acc[...] = jnp.zeros((2, PART, 128), F32)
    norm_rows = [ref[...].astype(F32)[l : l + 1] for l in range(LAYERS) for ref in (gains, shifts)]
    norm_rows = jnp.concatenate(norm_rows + [jnp.zeros((4, 48), F32)], axis=0)
    norm_rows = jnp.concatenate([norm_rows, jnp.zeros((8, 80), F32)], axis=1)
    norm_rows = jnp.concatenate([norm_rows, jnp.zeros((120, 128), F32)], axis=0)
    b.misc[...] = norm_rows.T.astype(BF16)

    b.raw[0:288] = read(b.w_out)[...].astype(F32)
    for l in range(LAYERS):
        b.wr_out[l] = b.raw[every(l, FLAT, 2), :].astype(BF16)
        parts = [b.raw[every(2 * i + l, UNIT, 12), :] for i in range(6)]
        turned = [turn(part) for part in parts]
        pieces = (
            (parts[0], parts[1]),
            (low_lanes(turned[1], turned[2]), turned[2]),
            (parts[3], parts[4]),
            (low_lanes(turned[4], turned[5]), turned[5]),
        )
        for cg in range(4):
            b.wc_out[l, cg] = jnp.concatenate(pieces[cg], axis=0).astype(BF16)
    for i, ref in enumerate((b.w_up, b.w_down)):
        b.raw[0:288] = read(ref)[...].astype(F32)
        for l in range(LAYERS):
            b.wm_out[l, FLAT * i : FLAT * (i + 1)] = b.raw[every(l, FLAT, 2), :].astype(BF16)

    for zz in range(4):
        for cc in range(2):
            gg = 2 * (p % 2) + s // 4
            row = pl.multiple_of(48 * (s % 4), 16)
            send(
                b.misc.at[0:48, :], b.gn_in.at[p // 2, pl.ds(row, 48), :],
                dev(gg // 2, cc, zz, gg % 2), gn_sem, True,
            )
    send_level(0)
    send_level_qkv(1)
    send_level(1)
    level_qkv_here(0)
    send_along("q", 0)
    b.cotown_t[...] = read(b.cotangent)[...].T
    x_sem = [new_sems() for _ in range(LAYERS)]
    x_half = b.x_all.at[0, :, pl.ds(own, HALF)]
    arrived(x_half, tok_sem)
    send(x_half, x_half, sibling, x_sem[0])
    relay("q", 0)
    level_here(0)
    send_along("c", 0)
    send_along("m", 0)
    arrived(b.ln_in, len_sem)
    valid = b.ln_in[0:1, 0:1]
    key_at = lax.broadcasted_iota(jnp.int32, (FULL, 128), 0).astype(F32)
    b.bias[...] = jnp.where(key_at < valid, 0.0, -1e30)

    def gain_shift(l, k):
        columns = b.gn_in[k].astype(F32)
        return columns[:, 2 * l : 2 * l + 1], columns[:, 2 * l + 1 : 2 * l + 2]

    stat_used = [0]

    def exchange(*rows):
        i = stat_used[0]
        stat_used[0] += 1
        buffer = b.stats.at[i]
        count = 4 * len(rows)
        buffer[0, 0:count] = jnp.concatenate(
            [row[:, ROWS * j : ROWS * (j + 1)] for row in rows for j in range(4)], axis=0
        )
        base = new_sems(3)
        for d in range(3):
            send(buffer.at[0, 0:count], buffer.at[d + 1, 0:count], square[d], base + d)

        def finish():
            for d in range(3):
                arrived(buffer.at[d + 1, 0:count], base + d)
            whole = [buffer[d, 0:count] for d in range(4)]
            return [
                [
                    jnp.concatenate([four[4 * i + j : 4 * i + j + 1] for j in range(4)], axis=1)
                    for i in range(len(rows))
                ]
                for four in whole
            ]

        return finish

    def normalize_here(v, name, l, gain, shift, weighted=None):
        mean_here = jnp.sum(v, axis=0, keepdims=True) * (1.0 / PART)
        d = v - mean_here
        rows = [mean_here, jnp.sum(d * d, axis=0, keepdims=True)]
        if weighted is not None:
            rows += [jnp.sum(weighted, axis=0, keepdims=True), jnp.sum(weighted * d, axis=0, keepdims=True)]
        exchanged = exchange(*rows)
        return lambda: normalize_there(exchanged(), v, name, l, gain, shift, weighted)

    def normalize_there(four, v, name, l, gain, shift, weighted):
        mean = (four[0][0] + four[1][0] + four[2][0] + four[3][0]) * 0.25
        total = sum(f[1] + PART * (f[0] - mean) * (f[0] - mean) for f in four)
        factor = lax.rsqrt(total * (1.0 / D) + EPSILON)
        scaled = (v - mean) * factor
        getattr(b, "xh" + name)[l] = scaled
        getattr(b, "r" + name)[l, 0:1] = factor
        result = scaled * gain + shift
        if weighted is None:
            return result
        one = sum(f[2] for f in four) * (1.0 / D)
        two = sum(f[3] + (f[0] - mean) * f[2] for f in four) * factor * (1.0 / D)
        return result, one, two

    def gather_raw(l, start):
        for t in range(8):
            b.raw[FLAT * t : FLAT * (t + 1)] = b.w_in[l, t % 2, t // 2, start : start + FLAT].astype(F32)

    def wide_rows(l, start, into):
        gather_raw(l, start)
        for i in range(6):
            into[:, 128 * i : 128 * (i + 1)] = b.raw[every(i, PART, 6), :].astype(BF16)

    def scatter_raw(ref, start):
        for t in range(8):
            ref[t % 2, t // 2, start : start + FLAT] = b.raw[FLAT * t : FLAT * (t + 1)].astype(BF16)

    def flat_units(matrix, ref, start):
        for i in range(6):
            b.raw[every(i, PART, 6), :] = matrix[:, 128 * i : 128 * (i + 1)]
        scatter_raw(ref, start)

    att_sem = [[new_sems(3) for _ in range(3)] for _ in range(LAYERS)]
    att_send = [[new_sems(3) for _ in range(3)] for _ in range(LAYERS)]

    def send_cotangent():
        for gg in range(4):
            lane = pl.multiple_of(ROWS * (s % 4), ROWS)
            send(
                b.cotown_t.at[pl.ds(PART * gg, PART), :], b.cot_t.at[:, pl.ds(lane, ROWS)],
                dev(gg // 2, half_of, z_mine, gg % 2), cot_sem, True,
            )

    def forward(l):
        x_own = b.x_all[l, :, pl.ds(own, HALF)]
        relayed("q", l)
        for n in range(24):
            rows = slice(UNIT * n, UNIT * (n + 1))
            start = QKV_AT + 2 * UNIT * (n % 3)
            unit = b.w_in[l, n // 3 % 2, n // 6, start : start + 2 * UNIT].astype(F32)
            b.left[rows] = unit[:UNIT]
            b.right[rows] = unit[UNIT:]
        turned = []
        for cc in range(3):
            rows = pl.ds(pl.multiple_of(PART * ((cc + g) % 3), UNIT), PART)
            nat = jnp.concatenate([b.left[rows, :], b.right[rows, :][:, 0:64]], axis=1).astype(BF16)
            b.wn_q[l, cc] = nat
            turned.append(nat.T)
        b.q_t[l] = mm(turned[0], x_own).astype(BF16) * jnp.asarray(0.125, BF16)

        def keys_values(start, part):
            for matrix, name in ((turned[1], "k"), (turned[2], "v")):
                value = mm(matrix, part).astype(BF16)
                getattr(b, name + "_t")[l, :, pl.ds(start, HALF)] = value
                for h in range(HEADS_HERE):
                    getattr(b, name + "_n")[l, h, pl.ds(start, HALF), :] = value[HEAD * h : HEAD * (h + 1)].T

        keys_values(own, x_own)
        arrived(b.x_all.at[l, :, pl.ds(other, HALF)], x_sem[l])
        keys_values(other, b.x_all[l, :, pl.ds(other, HALF)])

        if l == 1:
            send_cotangent()

        def one_head(h, carry):
            head = pl.multiple_of(HEAD * h, HEAD)
            q = b.q_t[l, pl.ds(head, HEAD), :]
            largest = jnp.full((1, HALF), -jnp.inf, F32)
            for kb in range(0, FULL, KEY_BLOCK):
                scores = mm(b.k_n[l, h, kb : kb + KEY_BLOCK, :], q) + b.bias[kb : kb + KEY_BLOCK, 0:1]
                b.s_scr[kb : kb + KEY_BLOCK] = scores
                largest = jnp.maximum(largest, jnp.max(scores, axis=0, keepdims=True))
            total = jnp.zeros((1, HALF), F32)
            for kb in range(0, FULL, KEY_BLOCK):
                powers = jnp.exp(b.s_scr[kb : kb + KEY_BLOCK] - largest)
                total += jnp.sum(powers, axis=0, keepdims=True)
                b.p_t[l, h, kb : kb + KEY_BLOCK] = powers.astype(BF16)
            inverse = 1.0 / total
            b.rinv[l, h, 0:1] = inverse
            out = mm(b.v_t[l, pl.ds(head, HEAD), :], b.p_t[l, h]) * inverse
            b.o_t[l, pl.ds(head, HEAD), :] = out
            rows = pl.ds(pl.multiple_of(g_rows + head, HEAD), HEAD)
            b.att_all[l, rows, :] = out.astype(BF16)
            piece = b.att_all.at[l, rows, :]
            for d in range(3):
                pltpu.make_async_remote_copy(
                    piece, piece, sems.at[att_send[l][d] + h], sems.at[att_sem[l][d] + h],
                    device_id=square[d], device_id_type=MESH,
                ).start()
            return carry

        lax.fori_loop(0, HEADS_HERE, one_head, 0)
        relay("c", l)
        relayed("c", l)
        for r in range(4):
            for t in range(8):
                rows = slice(UNIT * (8 * r + t), UNIT * (8 * r + t + 1))
                start = COLS_AT + 2 * UNIT * r
                unit = b.w_in[l, t % 2, t // 2, start : start + 2 * UNIT].astype(F32)
                b.left[rows] = unit[:UNIT]
                b.right[rows] = unit[UNIT:]
        columns_t = jnp.concatenate([b.left[...], b.right[:, 0:64]], axis=1).astype(BF16).T
        flips = ((0, 1), (1, 0), (1, 1))
        for h in range(HEADS_HERE):
            for d, (fx, fy) in enumerate(flips):
                px = 1 - x if fx else x
                py = 1 - y if fy else y
                start = pl.multiple_of(PART * (2 * px + py) + HEAD * h, HEAD)
                arrived(b.att_all.at[l, pl.ds(start, HEAD), :], att_sem[l][d] + h)
        relay("m", l)
        if l == 0:
            arrived(b.gn_in, gn_sem)
        branch = mm(columns_t, b.att_all[l])
        gain, shift = gain_shift(l, 0)
        finish = normalize_here(x_own.astype(F32) + branch, "1", l, gain, shift)
        relayed("m", l)
        wide_rows(l, 0, b.wn_u.at[l])
        b.wt_u[...] = b.wn_u[l].T
        gather_raw(l, FLAT)
        rows_from_triples(*(b.raw[every(i, PART_FF // 2, 3), :] for i in range(3)), b.left, b.right)
        nat = jnp.concatenate([b.left[...], b.right[:, 0:64]], axis=1).astype(BF16)
        b.wn_d[l] = nat
        down_t = nat.T
        middle = finish().astype(BF16)
        if l == 0:
            level_here(1)
            level_qkv_here(1)
            send_along("q", 1)
            send_along("c", 1)
            send_along("m", 1)
        b.mid[l] = middle

        def one_block(i, carry):
            rows = pl.ds(pl.multiple_of(FF_BLOCK * i, FF_BLOCK), FF_BLOCK)
            expanded = mm(b.wt_u[rows, :], b.mid[l])
            cdf, slope = erf_pair(expanded)
            b.act[l, rows, :] = (expanded * cdf).astype(BF16)
            b.dgl[l, rows, :] = slope
            return carry

        lax.fori_loop(0, PART_FF // FF_BLOCK, one_block, 0)
        second = middle.astype(F32) + mm(down_t, b.act[l])
        gain, shift = gain_shift(l, 1)
        if l + 1 < LAYERS:
            return normalize_here(second, "2", l, gain, shift)()
        arrived(b.cot_t, cot_sem)
        position = lax.broadcasted_iota(jnp.int32, (PART, HALF), 1) + HALF * c
        grad = jnp.where(position.astype(F32) < valid, b.cot_t[...].astype(F32), 0.0)
        return normalize_here(second, "2", l, gain, shift, grad * gain)(), grad

    hidden = forward(0)
    b.x_all[1, :, pl.ds(own, HALF)] = hidden.astype(BF16)
    x_half = b.x_all.at[1, :, pl.ds(own, HALF)]
    send(x_half, x_half, sibling, x_sem[1])
    relay("q", 1)
    send_along("r", 1)
    send_along("r", 0)
    (hidden, one, two), grad = forward(1)

    mix_sem, tg_sem = new_sems(), new_sems()

    def send_back(out_ref, in_ref, arrive):
        for k in range(4):
            send(
                out_ref.at[:, ROWS * k : ROWS * (k + 1)], in_ref.at[pl.ds(g_rows, PART), :],
                (seq_here, 4 * c + k), arrive, True,
            )

    b.mix_out[...] = hidden.astype(BF16)

    half_sem = {(name, l): new_sems() for l in range(LAYERS) for name in "moq"}
    level_sem = {(name, l): new_sems(3) for l in range(LAYERS) for name in "mo"}
    owner_sem = {(name, l): new_sems() for l in range(LAYERS) for name in "moq"}

    def to_sibling(name, l):
        there = pl.ds(4 * (1 - c), 4) if name == "q" else 1 - c
        send(getattr(b, "gb_" + name).at[l, there], getattr(b, "sb_" + name).at[l], sibling, half_sem[name, l])

    def to_level(name, l):
        here, mine = getattr(b, "sb_" + name), getattr(b, "gm_" + name)
        arrived(here.at[l], half_sem[name, l])
        mine[l] = (getattr(b, "gb_" + name)[l, c].astype(F32) + here[l].astype(F32)).astype(BF16)
        for i in range(3):
            there = (z + i + 1) % 4
            send(
                mine.at[l, there], getattr(b, "rz_" + name).at[l, i], dev(x, c, there, y), level_sem[name, l] + i
            )

    def to_owner(name, l):
        four = getattr(b, "rz_" + name)
        for i in range(3):
            arrived(four.at[l, i], level_sem[name, l] + i)
        total = getattr(b, "gm_" + name)[l, z].astype(F32) + sum(four[l, i].astype(F32) for i in range(3))
        final = getattr(b, "gf_" + name)
        final[l] = total.astype(BF16)
        return lambda: send(final.at[l], getattr(b, "rg_" + name).at[l], dev(g // 2, g % 2, z, c), owner_sem[name, l], True)

    def qkv_to_owners(l):
        arrived(b.sb_q.at[l], half_sem["q", l])
        b.gm_q[l] = (b.gb_q[l, pl.ds(4 * c, 4)].astype(F32) + b.sb_q[l].astype(F32)).astype(BF16)
        return lambda: qkv_sends(l)

    def qkv_sends(l):
        for k in range(4):
            for cc in range(3):
                u = 32 * cc + 8 * g + 4 * c + k
                j = u // 3
                send(
                    b.gm_q.at[l, k, cc], b.rg_q.at[l, z, u % 3], (j // 8, j % 8), owner_sem["q", l], True
                )

    lane_at = lax.broadcasted_iota(jnp.int32, (PART, 128), 1)

    def norm_grads(grad, scaled, l, k):
        gain_grad = jnp.sum(grad * scaled, axis=1, keepdims=True)
        shift_grad = jnp.sum(grad, axis=1, keepdims=True)
        b.gs_acc[k] += jnp.where(lane_at == 2 * l, gain_grad, 0.0) + jnp.where(
            lane_at == 2 * l + 1, shift_grad, 0.0
        )

    def normalize_back_here(grad, name, l, k, known=None, meanwhile=None):
        gain, _ = gain_shift(l, k)
        scaled = getattr(b, "xh" + name)[l]
        weighted = grad * gain
        if known is None:
            finish = exchange(
                jnp.sum(weighted, axis=0, keepdims=True), jnp.sum(weighted * scaled, axis=0, keepdims=True)
            )
            norm_grads(grad, scaled, l, k)
            if meanwhile is not None:
                meanwhile()
            four = finish()
            one, two = (sum(f[i] for f in four) * (1.0 / D) for i in range(2))
        else:
            one, two = known
        return getattr(b, "r" + name)[l, 0:1] * (weighted - one - scaled * two)

    gs_sem = new_sems()

    def send_norm_grads():
        for k in range(2):
            turned = b.gs_acc[k].T[0:8]
            for q in range(4):
                b.gs_out[k, q] = jnp.concatenate([turned[:, 48 * q : 48 * (q + 1)], jnp.zeros((8, 80), F32)], axis=1)
                send(
                    b.gs_out.at[k, q], b.gs_in.at[2 * z + c], (2 * k + g // 2, 4 * (g % 2) + q), gs_sem, True
                )

    bg_sem = [new_sems(3) for _ in range(LAYERS)]
    dx_sem = [new_sems() for _ in range(LAYERS)]

    def backward(l, grad, known=None):
        relay("r", l)
        second_grad = normalize_back_here(grad, "2", l, 1, known)
        b.sgb[l] = second_grad.astype(BF16)

        def one_block(i, carry):
            rows = pl.ds(pl.multiple_of(FF_BLOCK * i, FF_BLOCK), FF_BLOCK)
            active_grad = mm(b.wn_d[l, rows, :], b.sgb[l])
            b.eg[l, rows, :] = (active_grad * b.dgl[l, rows, :]).astype(BF16)
            return carry

        lax.fori_loop(0, PART_FF // FF_BLOCK, one_block, 0)
        middle_grad = second_grad + mm(b.wn_u[l], b.eg[l])

        def weight_grads():
            grads = mm_nt(b.act[l], b.sgb[l])
            b.left[...] = grads[:, :128]
            b.right[:, 0:64] = grads[:, 128:]
            for i, part in enumerate(triples_from_rows(PART_FF // 2, b.left, b.right)):
                b.raw[every(i, PART_FF // 2, 3), :] = part
            scatter_raw(b.gb_m.at[l], 0)
            flat_units(mm_nt(b.mid[l], b.eg[l]), b.gb_m.at[l], FLAT)
            to_sibling("m", l)

        first_grad = normalize_back_here(middle_grad, "1", l, 0, None, weight_grads)
        b.fg[...] = first_grad
        b.bg_all[l, pl.ds(g_rows, PART), :] = first_grad.astype(BF16)
        piece = b.bg_all.at[l, pl.ds(g_rows, PART), :]
        for d in range(3):
            send(piece, piece, square[d], bg_sem[l] + d)
        if known is not None:
            norm_grads(grad, b.xh2[l], l, 1)
        if l == 0:
            send_norm_grads()
        if l + 1 < LAYERS:
            later = [qkv_to_owners(l + 1), to_owner("m", l + 1), to_owner("o", l + 1)]
        else:
            later = [lambda: send_back(b.mix_out, b.mix_in, mix_sem)]
        to_level("m", l)
        relayed("r", l)
        wide_rows(l, ROWS_AT, b.wn_r.at[l])
        for d, (fx, fy) in enumerate(((0, 1), (1, 0), (1, 1))):
            px = 1 - x if fx else x
            py = 1 - y if fy else y
            start = pl.multiple_of(PART * (2 * px + py), PART)
            arrived(b.bg_all.at[l, pl.ds(start, PART), :], bg_sem[l] + d)
        att = b.att_all[l, pl.ds(g_rows, PART), :]
        flat_units(mm_nt(att, b.bg_all[l]), b.gb_o.at[l], 0)
        to_sibling("o", l)
        b.do_t[...] = mm(b.wn_r[l], b.bg_all[l]).astype(BF16)
        to_level("o", l)
        for sends in later:
            sends()

        def one_head(h, carry):
            head = pl.multiple_of(HEAD * h, HEAD)
            rows = pl.ds(head, HEAD)
            inverse = b.rinv[l, h, 0:1]
            grad_out = b.do_t[rows, :].astype(F32)
            delta = jnp.sum(grad_out * b.o_t[l, rows, :], axis=0, keepdims=True) * inverse
            grad_scaled = (grad_out * inverse).astype(BF16)
            for kb in range(0, FULL, KEY_BLOCK):
                block = slice(kb, kb + KEY_BLOCK)
                grad_probs = mm(b.v_n[l, h, block, :], grad_scaled)
                b.ds_scr[block] = (b.p_t[l, h, block].astype(F32) * (grad_probs - delta)).astype(BF16)
            b.dq_t[rows, :] = (mm(b.k_t[l, rows, :], b.ds_scr[...]) * 0.125).astype(BF16)
            b.dk_t[rows, :] = mm_nt(b.q_t[l, rows, :], b.ds_scr[...]).astype(BF16)
            b.dv_t[rows, :] = mm_nt(grad_scaled, b.p_t[l, h]).astype(BF16)
            return carry

        lax.fori_loop(0, HEADS_HERE, one_head, 0)
        w_q, w_k, w_v = (b.wn_q[l, cc] for cc in range(3))
        b.dx_out[l] = mm(w_k, b.dk_t[:, pl.ds(other, HALF)]) + mm(w_v, b.dv_t[:, pl.ds(other, HALF)])
        send(b.dx_out.at[l], b.dx_in.at[l], sibling, dx_sem[l])
        x_own = b.x_all[l, :, pl.ds(own, HALF)]
        b.gb_q[l, :, 0] = units_of(mm_nt(x_own, b.dq_t[...]))
        b.gb_q[l, :, 1] = units_of(mm_nt(b.x_all[l], b.dk_t[...]))
        b.gb_q[l, :, 2] = units_of(mm_nt(b.x_all[l], b.dv_t[...]))
        to_sibling("q", l)
        here = mm(w_q, b.dq_t[...])
        here += mm(w_k, b.dk_t[:, pl.ds(own, HALF)]) + mm(w_v, b.dv_t[:, pl.ds(own, HALF)])
        if l == 0:
            qkv_to_owners(0)()
        arrived(b.dx_in.at[l], dx_sem[l])
        return b.fg[...] + here + b.dx_in[l]

    grad = backward(1, grad, (one, two))
    grad = backward(0, grad)
    b.tg_out[...] = grad.astype(BF16)
    send_back(b.tg_out, b.tg_in, tg_sem)
    to_owner("m", 0)()
    to_owner("o", 0)()

    arrived(b.mix_in, mix_sem)
    mixed[...] = b.mix_in[...].T
    for l in reversed(range(LAYERS)):
        arrived(b.rg_m.at[l], owner_sem["m", l])
        g_down[every(l, FLAT, 2), :] = b.rg_m[l, 0:FLAT].astype(F32)
        g_up[every(l, FLAT, 2), :] = b.rg_m[l, FLAT : 2 * FLAT].astype(F32)
        arrived(b.rg_o.at[l], owner_sem["o", l])
        g_out[every(l, FLAT, 2), :] = b.rg_o[l].astype(F32)
        arrived(b.rg_q.at[l], owner_sem["q", l])
        total = sum(b.rg_q[l, i].astype(F32) for i in range(4))
        b.left[0:72] = total[:, :UNIT].reshape(72, 128)
        b.right[0:72] = total[:, UNIT:].reshape(72, 128)
        for i, part in enumerate(triples_from_rows(36, b.left, b.right)):
            b.raw[every(l + 2 * i, 36, 6), :] = part
    arrived(b.tg_in, tg_sem)
    tokens_grad[...] = b.tg_in[...].T
    arrived(b.gs_in, gs_sem)
    norms = sum(b.gs_in[i] for i in range(8))
    for k, out in enumerate((g_gain, g_shift)):
        for l in range(LAYERS):
            out[l : l + 1, :] = norms[2 * l + k : 2 * l + k + 1, 0 : PART // 4]

    for k in range(108):
        g_qkv[:, 128 * k : 128 * (k + 1)] = b.raw[2 * k : 2 * k + 2]

    for copy, when in pending:
        if when is None:
            copy.wait_send()
        else:
            pl.when(when)(copy.wait_send)
    for l in range(LAYERS):
        for h in range(HEADS_HERE):
            for d in range(3):
                piece = b.att_all.at[l, pl.ds(pl.multiple_of(g_rows + HEAD * h, HEAD), HEAD), :]
                pltpu.make_async_remote_copy(
                    piece, piece, sems.at[att_send[l][d] + h], sems.at[att_sem[l][d] + h],
                    device_id=square[d], device_id_type=MESH,
                ).wait_send()


def hand_over(*refs):
    for ref, out in zip(refs[:8], refs[8:]):
        out[...] = ref[...]


def fast_device(
    tokens, lengths, qkv_weight, out_weight, up_weight, down_weight, norm_gain, norm_shift, cotangent
):
    def raw(array):
        return array.reshape(LAYERS, -1, 128).transpose(1, 0, 2).reshape(-1, 128)

    def unraw(array):
        return array.reshape(-1, LAYERS, 128).transpose(1, 0, 2).reshape(LAYERS, -1)

    operands = (
        tokens[0],
        cotangent[0],
        lengths,
        norm_gain,
        norm_shift,
        qkv_weight,
        raw(out_weight),
        raw(up_weight),
        raw(down_weight),
    )
    vmem = pl.BlockSpec(memory_space=pltpu.VMEM)
    anywhere = pl.BlockSpec(memory_space=pl.ANY)
    shapes = (
        ((ROWS, D), BF16),
        ((ROWS, D), BF16),
        ((LAYERS, 3 * UNIT * PART), F32),
        ((LAYERS * FLAT, 128), F32),
        ((LAYERS * FLAT, 128), F32),
        ((LAYERS * FLAT, 128), F32),
        ((LAYERS, PART // 4), F32),
        ((LAYERS, PART // 4), F32),
    )
    results = pl.pallas_call(
        fast_kernel,
        out_shape=tuple(jax.ShapeDtypeStruct(*shape) for shape in shapes),
        in_specs=[anywhere] * 2 + [pl.BlockSpec(memory_space=pltpu.SMEM)] + [anywhere] * 6,
        out_specs=tuple([vmem] * len(shapes)),
        scratch_shapes=[pltpu.SemaphoreType.DMA((SEMS,))] + [pltpu.VMEM(*entry) for entry in SCRATCH.values()],
        compiler_params=pltpu.CompilerParams(
            collective_id=0, has_side_effects=True, vmem_limit_bytes=60 * 2**20
        ),
        name="encoder",
    )(*operands)
    mixed, tokens_grad, g_qkv, g_out, g_up, g_down, g_gain, g_shift = pl.pallas_call(
        hand_over,
        out_shape=tuple(jax.ShapeDtypeStruct(*shape) for shape in shapes),
        in_specs=[vmem] * len(shapes),
        out_specs=tuple([vmem] * len(shapes)),
        name="hand_over",
    )(*results)
    return (
        mixed[None],
        tokens_grad[None],
        g_qkv,
        unraw(g_out),
        unraw(g_up),
        unraw(g_down),
        g_gain,
        g_shift,
    )


def solution(mesh):
    small = (mesh.shape["dp"], mesh.shape["seq"]) == (4, 8)
    return jax.shard_map(
        fast_device if small else per_device,
        mesh=mesh,
        in_specs=(
            P("dp", "seq", None),
            P("dp"),
            P(None, ("dp", "seq")),
            P(None, ("dp", "seq")),
            P(None, ("dp", "seq")),
            P(None, ("dp", "seq")),
            P(None, ("dp", "seq")),
            P(None, ("dp", "seq")),
            P("dp", "seq", None),
        ),
        out_specs=(
            P("dp", "seq", None),
            P("dp", "seq", None),
            P(None, ("dp", "seq")),
            P(None, ("dp", "seq")),
            P(None, ("dp", "seq")),
            P(None, ("dp", "seq")),
            P(None, ("dp", "seq")),
            P(None, ("dp", "seq")),
        ),
        check_vma=False,
    )
```
